256 devices in a mesh: seq: 16 (over z, core), head: 16 (over y, x).
Axes of the slice: x: 4, y: 4, z: 8, core: 2. Of those that a mesh axis runs over, the one named last changes fastest.
Arguments:
- projections: bfloat16 [49152, 8, 384], P(('seq', 'head')), may hold values from -8 to 8
- routed_heads: int32 [49152, 8], P(('seq', 'head')), may hold values from 0 to 63, as said below
- slot_index: int32 [49152, 8], P(('seq', 'head')), may hold values from 0 to 47, as said below
- gate_logits: float32 [49152, 8], P(('seq', 'head')), may hold values from -8 to 8
- doc_lengths: int32 [32], replicated, may hold values from 1 to 3072, 49152 in all
- cotangent: bfloat16 [49152, 8, 128], P(('seq', 'head')), may hold values from -6 to 6
Outputs:
- head_outputs: bfloat16 [49152, 8, 128], P(('seq', 'head'))
- projection_grads: bfloat16 [49152, 8, 384], P(('seq', 'head'))
- gate_grads: float32 [49152, 8], P(('seq', 'head'))
The draws below stay inside these ranges and needn't reach their ends.
Inputs may be any that keep to these rules, and one draw needn't show every extreme that they name: `routed_heads`: each token names 8 different heads. Among the 192 tokens of one aligned block at most 48 name the same head, and in every aligned run of 3072 tokens one head is named by exactly 48 tokens of each of its aligned blocks of 192. slot_index[t, k] is the number of tokens before t in t's aligned block of 192 tokens that name head routed_heads[t, k]. `doc_lengths`: the documents lie in order and together fill the 49152 positions.
All inputs are finite; a program needn't handle non-finite values.
Results may differ from the reference program's by a relative error of at most 0.011.
Values may be sent and summed in bfloat16 or wider, within the bound.
A program may use at most 64 MiB of HBM per device.

```python
import math
from functools import partial
import jax
import jax.numpy as jnp
import numpy as np
from jax import lax

H = 64
HS = 128
TOP = 8
TOK_DEV = 192
CAP = 48
SEQ_TOK = 3072
TOKENS = 49152
NDOC = 32
N_SEQ = 16
N_HEAD = 16


def lane_counts(count_key, total_rows, lane_size):
    base_rows = total_rows // lane_size
    extra_rows = total_rows % lane_size
    counts = base_rows + (jnp.arange(lane_size, dtype=jnp.int32) < extra_rows).astype(jnp.int32)
    pair_count = lane_size // 2
    shifts = jax.random.randint(count_key, (pair_count,), 0, max(base_rows, 1), dtype=jnp.int32)
    counts = counts.at[0:2 * pair_count:2].add(shifts)
    counts = counts.at[1:2 * pair_count:2].add(-shifts)
    return counts.astype(jnp.int32)


def routing(key):
    base_key = jax.random.fold_in(key, 7001)
    hot_key, offset_key, count_key, order_key, column_key = jax.random.split(base_key, 5)
    blocks = TOKENS // TOK_DEV
    groups = TOKENS // SEQ_TOK
    lane_size = H // TOP
    hot_heads = jax.random.randint(hot_key, (groups,), 0, H, dtype=jnp.int32)
    block_hot = jnp.repeat(hot_heads, SEQ_TOK // TOK_DEV)

    def block_heads(one_key):
        others = jax.random.permutation(one_key, H - 1).astype(jnp.int32) + 1
        return jnp.concatenate([jnp.zeros((1,), jnp.int32), others])
    offsets = jax.vmap(block_heads)(jax.random.split(offset_key, blocks))
    head_table = ((block_hot[:, None] + offsets) % H).reshape(blocks, TOP, lane_size)

    def block_counts(one_key):
        first_key, rest_key = jax.random.split(one_key)
        hot_lane = jnp.concatenate([jnp.full((1,), CAP, jnp.int32), lane_counts(first_key, TOK_DEV - CAP, lane_size - 1)])
        other_lanes = jax.vmap(partial(lane_counts, total_rows=TOK_DEV, lane_size=lane_size))(jax.random.split(rest_key, TOP - 1))
        return jnp.concatenate([hot_lane[None, :], other_lanes], 0)
    counts = jax.vmap(block_counts)(jax.random.split(count_key, blocks))
    order_keys = jax.random.split(order_key, blocks * TOP)
    rank_table = jax.vmap(lambda one_key: jax.random.permutation(one_key, TOK_DEV).astype(jnp.int32))(order_keys)
    rank_table = rank_table.reshape(blocks, TOP, TOK_DEV)
    bounds = jnp.cumsum(counts, axis=2)[:, :, :-1]
    lane_place = jnp.sum((rank_table[:, :, :, None] >= bounds[:, :, None, :]).astype(jnp.int32), axis=3)
    chosen = jnp.take_along_axis(head_table, lane_place, axis=2)
    same_head = lane_place[:, :, :, None] == lane_place[:, :, None, :]
    earlier = jnp.arange(TOK_DEV)[None, :] < jnp.arange(TOK_DEV)[:, None]
    slot_table = jnp.sum((same_head & earlier[None, None, :, :]).astype(jnp.int32), axis=3)
    order_scores = jax.random.randint(column_key, (blocks, TOK_DEV, TOP), 0, 1 << 16, dtype=jnp.int32) * TOP + jnp.arange(TOP, dtype=jnp.int32)
    column_order = jnp.argsort(order_scores, axis=2)
    heads_out = jnp.take_along_axis(jnp.transpose(chosen, (0, 2, 1)), column_order, axis=2)
    slots_out = jnp.take_along_axis(jnp.transpose(slot_table, (0, 2, 1)), column_order, axis=2)
    return (heads_out.reshape(TOKENS, TOP).astype(jnp.int32), slots_out.reshape(TOKENS, TOP).astype(jnp.int32))


def draw_routed_heads(key, part):
    return routing(key)[0]


def draw_slot_index(key, part):
    return routing(key)[1]


def draw_projections(key, part):
    draw_key = jax.random.fold_in(key, 9001)
    base_key = jax.random.fold_in(draw_key, 0)
    full_shape = (TOKENS, TOP, 3 * HS)
    entries = jnp.clip(jax.random.normal(base_key, full_shape, jnp.float32), -6.0, 6.0)
    return entries.astype(jnp.bfloat16)


def block_levels(rng, extent, cuts, low, high):
    def one(dim, parts):
        heights = jax.random.uniform(jax.random.fold_in(jax.random.fold_in(rng, 6), dim), (parts,), jnp.float32, low / len(cuts), high / len(cuts))
        return jnp.repeat(jnp.exp(heights), extent[dim] // parts).reshape((-1,) + (1,) * (len(extent) - dim - 1))

    loudness = one(*cuts[0])
    for cut in cuts[1:]:
        loudness = loudness * one(*cut)
    return loudness


def length_profile(count, total, limit, slope):
    portions = [(1 << 20) // math.isqrt(rank ** slope) + 1 for rank in range(2, count + 1)]
    surplus, holding = total - limit - (count - 1), [1] * (count - 1)
    while surplus > 0:
        candidates = [i for i in range(count - 1) if holding[i] < limit]
        mass, remaining = sum([portions[i] for i in candidates]), surplus
        for i in candidates:
            extra = min(limit - holding[i], max(1, remaining * portions[i] // mass), surplus)
            holding[i] = holding[i] + extra
            surplus = surplus - extra
    return np.array([limit] + holding)


def ragged(key, amount, total, bound, skew):
    if amount == 2:
        one = jax.random.randint(key, (), max(1, total - bound), min(bound, total - 1) + 1)
        return jnp.stack([one, total - one])
    sizes = jnp.asarray(length_profile(amount, total, bound, skew), jnp.int32)
    twos = (amount - 1) // 2
    donor, sink = sizes[1:1 + 2 * twos:2], sizes[2:2 + 2 * twos:2]
    slack = jnp.minimum(donor - 1, bound - sink)
    moved = jax.random.randint(jax.random.fold_in(key, 1), (twos,), 0, 1 << 20) % (slack + 1)
    sizes = sizes.at[1:1 + 2 * twos:2].set(donor - moved).at[2:2 + 2 * twos:2].set(sink + moved)
    return sizes[jax.random.permutation(jax.random.fold_in(key, 2), amount)]


def scatter_about(own_key, shape, width, limit, cuts=(), held_as=jnp.bfloat16):
    array = width * jax.random.normal(own_key, shape, jnp.float32)
    if cuts:
        array = array * block_levels(own_key, shape, cuts, -0.22, 0.18)
    return jnp.clip(array, -limit, limit).astype(held_as)


def setup_inputs(seed: int = 0) -> dict:
    streams_of = jax.random.split(jax.random.key(seed), 7)
    return {
        "projections": draw_projections(jax.random.fold_in(streams_of[6], 71), 0),
        "routed_heads": draw_routed_heads(jax.random.fold_in(streams_of[6], 71), 0),
        "slot_index": draw_slot_index(jax.random.fold_in(streams_of[6], 71), 0),
        "gate_logits": scatter_about(streams_of[3], (TOKENS, TOP), 2.0, 8.0, ((0, 256),), jnp.float32),
        "doc_lengths": ragged(streams_of[4], NDOC, TOKENS, SEQ_TOK, 1).astype(jnp.int32),
        "cotangent": scatter_about(streams_of[5], (TOKENS, TOP, HS), 1.0, 6.0, ((0, 256),)),
    }


MASKED = -1e30


def block_pass(rows_here, docs_here, rows_before, docs_before, grads_out, carried):
    head_size = grads_out.shape[1]
    slot_span = docs_here.shape[0]
    scaling = head_size ** -0.5
    queries = rows_here[:, :head_size]
    key_rows = jnp.concatenate([rows_before[:, :head_size], rows_here[:, head_size:2 * head_size]], 0)
    value_rows = jnp.concatenate([rows_before[:, head_size:], rows_here[:, 2 * head_size:]], 0)
    key_docs = jnp.concatenate([docs_before, docs_here], 0)
    row_index = jnp.arange(slot_span, dtype=jnp.int32)[:, None]
    col_index = jnp.arange(2 * slot_span, dtype=jnp.int32)[None, :]
    visible = (key_docs[None, :] == docs_here[:, None]) & (key_docs[None, :] > 0) & (col_index - slot_span <= row_index)
    scores = jnp.dot(queries, key_rows.T, preferred_element_type=jnp.float32) * scaling
    scores = jnp.where(visible, scores, MASKED)
    row_max = jnp.max(scores, axis=1, keepdims=True)
    powers = jnp.exp(scores - row_max)
    row_sum = jnp.sum(powers, axis=1, keepdims=True)
    weights = powers / row_sum
    weights_low = weights.astype(jnp.bfloat16)
    attended = jnp.dot(weights_low, value_rows, preferred_element_type=jnp.float32).astype(jnp.bfloat16)
    attended = lax.optimization_barrier(attended)
    deltas = jnp.sum(grads_out.astype(jnp.float32) * attended.astype(jnp.float32), axis=1, keepdims=True)
    weight_grads = jnp.dot(grads_out, value_rows.T, preferred_element_type=jnp.float32)
    score_grads = (weights * (weight_grads - deltas)).astype(jnp.bfloat16)
    query_grads = jnp.dot(score_grads, key_rows, preferred_element_type=jnp.float32) * scaling
    key_grads = jnp.dot(score_grads.T, queries, preferred_element_type=jnp.float32) * scaling
    value_grads = jnp.dot(weights_low.T, grads_out, preferred_element_type=jnp.float32)
    own_keys = key_grads[slot_span:] + carried[0]
    own_values = value_grads[slot_span:] + carried[1]
    gradients = jnp.concatenate([query_grads, own_keys, own_values], 1).astype(jnp.bfloat16)
    return (key_grads[:slot_span], value_grads[:slot_span]), attended, gradients


def reference(projections, routed_heads, slot_index, gate_logits, doc_lengths, cotangent):
    token_total = projections.shape[0]
    full_width = projections.shape[2]
    head_size = full_width // 3
    slot_span = N_HEAD * CAP
    positions = jnp.arange(token_total, dtype=jnp.int32)
    doc_ends = jnp.cumsum(doc_lengths).astype(jnp.int32)
    documents = jnp.sum((positions[:, None] >= doc_ends[None, :]).astype(jnp.int32), axis=1) + 1
    zero_pairs = jnp.zeros_like(routed_heads)
    seq_block = ((positions // SEQ_TOK)[:, None] + zero_pairs).astype(jnp.int32)
    placed = (((positions // TOK_DEV) % N_HEAD)[:, None] * CAP + slot_index).astype(jnp.int32)
    pair_docs = (documents[:, None] + zero_pairs).astype(jnp.int32)
    gate_values = jax.nn.sigmoid(gate_logits)
    grads_out = (cotangent.astype(jnp.float32) * gate_values[:, :, None]).astype(jnp.bfloat16)
    proj_slots = jnp.zeros((H, N_SEQ, slot_span, full_width), projections.dtype).at[routed_heads, seq_block, placed].set(projections)
    doc_slots = jnp.zeros((H, N_SEQ, slot_span), jnp.int32).at[routed_heads, seq_block, placed].set(pair_docs)
    out_slots = jnp.zeros((H, N_SEQ, slot_span, head_size), grads_out.dtype).at[routed_heads, seq_block, placed].set(grads_out)

    def one_head(operands):
        rows_all, docs_all, outs_all = operands
        rows_before = jnp.concatenate([jnp.zeros_like(rows_all[:1, :, head_size:]), rows_all[:-1, :, head_size:]], 0)
        docs_before = jnp.concatenate([jnp.zeros_like(docs_all[:1]), docs_all[:-1]], 0)

        def advance(carried, inputs):
            rows_here, docs_here, rows_prior, docs_prior, outs_here = inputs
            passed, attended, gradients = block_pass(rows_here, docs_here, rows_prior, docs_prior, outs_here, carried)
            return passed, (attended, gradients)

        start_carry = (jnp.zeros((slot_span, head_size), jnp.float32), jnp.zeros((slot_span, head_size), jnp.float32))
        _, results = lax.scan(advance, start_carry, (rows_all, docs_all, rows_before, docs_before, outs_all), reverse=True)
        return results

    attended_slots, grad_slots = lax.map(one_head, (proj_slots, doc_slots, out_slots))
    attended = attended_slots[routed_heads, seq_block, placed].astype(jnp.float32)
    head_outputs = (attended * gate_values[:, :, None]).astype(jnp.bfloat16)
    projection_grads = grad_slots[routed_heads, seq_block, placed]
    gate_grads = jnp.sum(cotangent.astype(jnp.float32) * attended, axis=2) * gate_values * (1.0 - gate_values)
    return head_outputs, projection_grads, gate_grads
```

```python
import math

import jax
import jax.numpy as jnp
from jax import lax
from jax.experimental import pallas as pl
from jax.experimental.pallas import tpu as pltpu
from jax.sharding import PartitionSpec as P

H = 64
CAP = 48
OWN = 4
PEERS = 16
SPAN = PEERS * CAP
HS = 128
WIDE = 4 * HS
QT = 256
WIN = 1152
KC = 384
MASKED = -1e30
F32 = jnp.float32
BF16 = jnp.bfloat16
MESH = pl.DeviceIdType.MESH


def dot_nt(a, b):
    return lax.dot_general(a, b, (((1,), (1,)), ((), ())), preferred_element_type=F32)


def dot(a, b):
    return jnp.dot(a, b, preferred_element_type=F32)


def one_hot(mask):
    return jnp.where(mask, 1.0, 0.0).astype(BF16)


def div48(v):
    return (v * 1366) >> 16


def kernel(
    x_ref,
    rows_ref,
    dest_ref,
    out_ref,
    fsend,
    frecv,
    doc_send,
    doc_recv,
    doc_prev,
    kv_prev,
    dsend,
    drecv,
    rsend,
    rrecv,
    k_all,
    v_all,
    k_t,
    v_t,
    key_docs,
    query_docs,
    s_buf,
    p_buf,
    ds_buf,
    dk_acc,
    dv_acc,
    f_ssem,
    f_rsem,
    doc_ssem,
    doc_rsem,
    dp_sem,
    kv_ssem,
    kv_rsem,
    d_ssem,
    d_rsem,
    r_ssem,
    r_rsem,
):
    me = lax.axis_index("head")
    here = lax.axis_index("seq")
    after = lax.rem(here + 1, PEERS)
    before = lax.rem(here + PEERS - 1, PEERS)
    routes = x_ref.shape[0]
    scaling = HS ** (-0.5)

    barrier = pltpu.get_barrier_semaphore()

    def peer_of(d):
        px = lax.rem(lax.rem(me, 4) + lax.rem(d, 4), 4)
        py = lax.rem(me // 4 + d // 4, 4)
        return py * 4 + px

    @pl.loop(1, PEERS)
    def _(d):
        pl.semaphore_signal(barrier, inc=1, device_id={"head": peer_of(d)}, device_id_type=MESH)

    pl.semaphore_signal(barrier, inc=1, device_id={"seq": after}, device_id_type=MESH)
    pl.semaphore_signal(barrier, inc=1, device_id={"seq": before}, device_id_type=MESH)

    def block(i):
        return pl.ds(pl.multiple_of(i * CAP, CAP), CAP)

    def fwd_copy(a, d):
        peer = peer_of(d)
        return pltpu.make_async_remote_copy(
            src_ref=fsend.at[a, block(peer)],
            dst_ref=frecv.at[a, block(me)],
            send_sem=f_ssem.at[a, d],
            recv_sem=f_rsem.at[a, d],
            device_id={"head": peer},
            device_id_type=MESH,
        )

    def ret_copy(a, d):
        peer = peer_of(d)
        return pltpu.make_async_remote_copy(
            src_ref=rsend.at[a, block(peer)],
            dst_ref=rrecv.at[a, block(me)],
            send_sem=r_ssem.at[a, d],
            recv_sem=r_rsem.at[a, d],
            device_id={"head": peer},
            device_id_type=MESH,
        )

    def doc_rows(i):
        return pl.ds(pl.multiple_of(i * 16, 16), 16)

    def doc_copy(d):
        peer = peer_of(d)
        return pltpu.make_async_remote_copy(
            src_ref=doc_send.at[doc_rows(peer)],
            dst_ref=doc_recv.at[doc_rows(me)],
            send_sem=doc_ssem.at[d],
            recv_sem=doc_rsem.at[d],
            device_id={"head": peer},
            device_id_type=MESH,
        )

    doc_shift = pltpu.make_async_remote_copy(
        src_ref=doc_recv,
        dst_ref=doc_prev,
        send_sem=dp_sem.at[0],
        recv_sem=dp_sem.at[1],
        device_id={"seq": after},
        device_id_type=MESH,
    )

    def kv_copy(a):
        return pltpu.make_async_remote_copy(
            src_ref=frecv.at[a, :, pl.ds(HS, 2 * HS)],
            dst_ref=kv_prev.at[a],
            send_sem=kv_ssem.at[a],
            recv_sem=kv_rsem.at[a],
            device_id={"seq": after},
            device_id_type=MESH,
        )

    def d_copy(a):
        return pltpu.make_async_remote_copy(
            src_ref=dsend.at[a],
            dst_ref=drecv.at[a],
            send_sem=d_ssem.at[a],
            recv_sem=d_rsem.at[a],
            device_id={"seq": before},
            device_id_type=MESH,
        )

    row = lax.broadcasted_iota(jnp.int32, (256, 128), 0)
    row_head = 4 * (row >> 4) + (row & 3)
    tiles = routes // 128
    at_head = jnp.concatenate([row_head] * tiles, axis=1) == rows_ref[1:2, :]
    docs_wide = jnp.where(at_head, rows_ref[3:4, :].astype(F32), 0.0).astype(BF16)
    lane_slot = lax.broadcasted_iota(jnp.int32, (128, 128), 0)
    at_slot = one_hot(jnp.concatenate([lane_slot] * tiles, axis=1) == rows_ref[2:3, :])
    doc_send[...] = dot_nt(docs_wide, at_slot).astype(BF16)

    def dispatch(a):
        @pl.loop(0, SPAN // 256)
        def _(c):
            first = pl.multiple_of(c * 256, 256)
            r = lax.broadcasted_iota(jnp.int32, (256, 128), 0) + first
            source = div48(r)
            ids = source * (OWN * CAP) + (r - source * CAP) + a * CAP
            hot = one_hot(jnp.concatenate([ids] * tiles, axis=1) == rows_ref[0:1, :])
            fsend[a, pl.ds(first, 256), :] = dot(hot, x_ref[...]).astype(BF16)

        frecv[a, block(me), :] = fsend[a, block(me), :]

    dispatch(0)
    doc_recv[doc_rows(me), :] = doc_send[doc_rows(me), :]
    pl.semaphore_wait(barrier, PEERS + 1)

    @pl.loop(1, PEERS)
    def _(d):
        doc_copy(d).start()

    @pl.loop(0, OWN)
    def _(a):
        @pl.when(a > 0)
        def _():
            dispatch(a)

        @pl.loop(1, PEERS)
        def _(d):
            fwd_copy(a, d).start()

    @pl.loop(1, PEERS)
    def _(d):
        doc_copy(d).wait_recv()

    doc_shift.start()

    def take_head(a):
        @pl.loop(1, PEERS)
        def _(d):
            fwd_copy(a, d).wait_recv()

        kv_copy(a).start()

    def head_docs(a, docs_ref):
        r = lax.broadcasted_iota(jnp.int32, (SPAN, 128), 0)
        lane = lax.broadcasted_iota(jnp.int32, (SPAN, 128), 1)
        source = div48(r)
        wanted = source * 16 + a
        pick = one_hot(jnp.concatenate([lane, lane + 128], axis=1) == jnp.concatenate([wanted] * 2, axis=1))
        spread = dot(pick, docs_ref[...])
        return jnp.where(lane == r - source * CAP, spread, 0.0).astype(BF16)

    def attention(a):
        k_all[:SPAN, :] = kv_prev[a, :, :HS]
        v_all[:SPAN, :] = kv_prev[a, :, HS:]
        k_all[SPAN:, :] = frecv[a, :, HS : 2 * HS]
        v_all[SPAN:, :] = frecv[a, :, 2 * HS : 3 * HS]
        k_t[...] = k_all[...].T
        v_t[...] = v_all[...].T
        ones = jnp.ones((HS, HS), BF16)
        mine = head_docs(a, doc_recv)
        key_docs[:SPAN, :] = dot(head_docs(a, doc_prev), ones)
        key_docs[SPAN:, :] = dot(mine, ones)
        query_docs[...] = dot_nt(ones[:8], mine)
        dk_acc[a] = jnp.zeros((2 * SPAN, HS), F32)
        dv_acc[a] = jnp.zeros((2 * SPAN, HS), F32)

        @pl.loop(0, SPAN // QT)
        def _(i):
            first = pl.multiple_of(i * QT, QT)
            start = pl.multiple_of(((i * (i + 1)) >> 1) * 128, 128)
            q = frecv[a, pl.ds(first, QT), :HS]
            out_grad = frecv[a, pl.ds(first, QT), 3 * HS :]
            q_docs = query_docs[0:1, pl.ds(first, QT)]
            top = jnp.full((1, QT), MASKED, F32)
            for c in range(WIN // KC):
                keys = pl.ds(pl.multiple_of(start + c * KC, 128), KC)
                s = dot_nt(k_all[keys, :], q) * (scaling * math.log2(math.e))
                docs = key_docs[keys, :]
                seen = jnp.concatenate([docs, docs], axis=1) == q_docs
                if (c + 1) * KC > SPAN:
                    k_at = lax.broadcasted_iota(jnp.int32, (KC, QT), 0) + (start + c * KC - SPAN)
                    q_at = lax.broadcasted_iota(jnp.int32, (KC, QT), 1) + first
                    seen = seen & (k_at <= q_at)
                s = jnp.where(seen, s, MASKED)
                s_buf[c * KC : (c + 1) * KC, :] = s
                top = jnp.maximum(top, jnp.max(s, axis=0, keepdims=True))
            total = jnp.zeros((1, QT), F32)
            for c in range(WIN // KC):
                part = slice(c * KC, (c + 1) * KC)
                p = jnp.exp2(s_buf[part, :] - top)
                total = total + jnp.sum(p, axis=0, keepdims=True)
                s_buf[part, :] = p
                p_buf[part, :] = p.astype(BF16)
            inverse = 1.0 / total
            window = pl.ds(start, WIN)
            attended = (dot(v_t[:, window], p_buf[...]) * inverse).astype(BF16)
            out_grad_t = (out_grad.astype(F32).T * inverse).astype(BF16)
            delta = jnp.sum(out_grad_t.astype(F32) * attended.astype(F32), axis=0, keepdims=True)
            for c in range(WIN // KC):
                part = slice(c * KC, (c + 1) * KC)
                keys = pl.ds(pl.multiple_of(start + c * KC, 128), KC)
                dp = dot(v_all[keys, :], out_grad_t)
                ds = (s_buf[part, :] * (dp - delta)).astype(BF16)
                ds_buf[part, :] = ds
                dv_acc[a, keys, :] += dot_nt(p_buf[part, :], out_grad_t)
                dk_acc[a, keys, :] += dot(ds, q)
            dq = dot(k_t[:, window], ds_buf[...]) * scaling
            rsend[a, pl.ds(first, QT), :HS] = attended.astype(F32).T.astype(BF16)
            rsend[a, pl.ds(first, QT), HS : 2 * HS] = dq.T.astype(BF16)

        dsend[a, :, :HS] = (dk_acc[a, :SPAN, :] * scaling).astype(BF16)
        dsend[a, :, HS:] = dv_acc[a, :SPAN, :].astype(BF16)
        d_copy(a).start()

    def finish(a):
        d_copy(a).wait_recv()
        dk = dk_acc[a, SPAN:, :] * scaling + drecv[a, :, :HS].astype(F32)
        dv = dv_acc[a, SPAN:, :] + drecv[a, :, HS:].astype(F32)
        rsend[a, :, 2 * HS : 3 * HS] = dk.astype(BF16)
        rsend[a, :, 3 * HS :] = dv.astype(BF16)

        @pl.loop(1, PEERS)
        def _(d):
            ret_copy(a, d).start()

        rrecv[a, block(me), :] = rsend[a, block(me), :]

    take_head(0)
    doc_shift.wait_recv()

    @pl.loop(0, OWN)
    def _(a):
        @pl.when(a < OWN - 1)
        def _():
            take_head(a + 1)

        kv_copy(a).wait_recv()
        attention(a)

        @pl.when(a > 0)
        def _():
            finish(a - 1)

    finish(OWN - 1)

    out_ref[...] = jnp.zeros(out_ref.shape, BF16)

    @pl.loop(0, OWN)
    def _(a):
        @pl.loop(1, PEERS)
        def _(d):
            ret_copy(a, d).wait_recv()

        @pl.loop(0, routes // 256)
        def _(c):
            rows = pl.ds(pl.multiple_of(c * 256, 256), 256)
            lane = lax.broadcasted_iota(jnp.int32, (8, SPAN), 1)
            source = div48(lane)
            ids = source * (OWN * CAP) + (lane - source * CAP) + a * CAP
            dest = dest_ref[rows, :]
            hot = one_hot(jnp.concatenate([dest] * (SPAN // 128), axis=1) == ids[0:1, :])
            out_ref[rows, :] = (out_ref[rows, :].astype(F32) + dot(hot, rrecv[a])).astype(BF16)

    @pl.loop(1, PEERS)
    def _(d):
        doc_copy(d).wait_send()

    doc_shift.wait_send()

    @pl.loop(0, OWN)
    def _(a):
        @pl.loop(1, PEERS)
        def _(d):
            fwd_copy(a, d).wait_send()
            ret_copy(a, d).wait_send()

        kv_copy(a).wait_send()
        d_copy(a).wait_send()


def per_device(projections, routed_heads, slot_index, gate_logits, doc_lengths, cotangent):
    tokens, top, width = projections.shape
    routes = tokens * top
    offset = (lax.axis_index("seq") * PEERS + lax.axis_index("head")) * tokens
    positions = offset + jnp.arange(tokens, dtype=jnp.int32)
    doc_ends = jnp.cumsum(doc_lengths)
    documents = jnp.sum((positions[:, None] >= doc_ends[None, :]).astype(jnp.int32), axis=1) + 1
    gate = jax.nn.sigmoid(gate_logits)
    grads_out = (cotangent.astype(F32) * gate[:, :, None]).astype(BF16)
    x = jnp.concatenate([projections, grads_out], axis=2).reshape(routes, WIDE)
    dest = routed_heads * CAP + slot_index
    doc_routes = jnp.broadcast_to(documents[:, None], (tokens, top))
    zero = jnp.zeros_like(dest)
    rows = jnp.stack([dest, routed_heads, slot_index, doc_routes, zero, zero, zero, zero], 0)
    rows = rows.reshape(8, routes)
    dest_wide = jnp.broadcast_to(dest.reshape(routes, 1), (routes, 128))
    dma = pltpu.SemaphoreType.DMA
    vmem = pltpu.VMEM
    out = pl.pallas_call(
        kernel,
        out_shape=jax.ShapeDtypeStruct((routes, WIDE), BF16),
        in_specs=[pl.BlockSpec(memory_space=pltpu.VMEM)] * 3,
        out_specs=pl.BlockSpec(memory_space=pltpu.VMEM),
        scratch_shapes=[
            vmem((OWN, SPAN, WIDE), BF16),
            vmem((OWN, SPAN, WIDE), BF16),
            vmem((PEERS * 16, 128), BF16),
            vmem((PEERS * 16, 128), BF16),
            vmem((PEERS * 16, 128), BF16),
            vmem((OWN, SPAN, 2 * HS), BF16),
            vmem((OWN, SPAN, 2 * HS), BF16),
            vmem((OWN, SPAN, 2 * HS), BF16),
            vmem((OWN, SPAN, WIDE), BF16),
            vmem((OWN, SPAN, WIDE), BF16),
            vmem((2 * SPAN, HS), BF16),
            vmem((2 * SPAN, HS), BF16),
            vmem((HS, 2 * SPAN), BF16),
            vmem((HS, 2 * SPAN), BF16),
            vmem((2 * SPAN, HS), F32),
            vmem((8, SPAN), F32),
            vmem((WIN, QT), F32),
            vmem((WIN, QT), BF16),
            vmem((WIN, QT), BF16),
            vmem((OWN, 2 * SPAN, HS), F32),
            vmem((OWN, 2 * SPAN, HS), F32),
            dma((OWN, PEERS)),
            dma((OWN, PEERS)),
            dma((PEERS,)),
            dma((PEERS,)),
            dma((2,)),
            dma((OWN,)),
            dma((OWN,)),
            dma((OWN,)),
            dma((OWN,)),
            dma((OWN, PEERS)),
            dma((OWN, PEERS)),
        ],
        compiler_params=pltpu.CompilerParams(
            collective_id=0, has_side_effects=True, vmem_limit_bytes=60000 * 1024
        ),
    )(x, rows, dest_wide)
    out = out.reshape(tokens, top, WIDE)
    attended = out[:, :, :HS].astype(F32)
    projection_grads = out[:, :, HS:]
    head_outputs = (attended * gate[:, :, None]).astype(BF16)
    gate_grads = jnp.sum(cotangent.astype(F32) * attended, axis=2) * gate * (1.0 - gate)
    return head_outputs, projection_grads, gate_grads


def solution(mesh):
    tokens = P(("seq", "head"), None, None)
    routes = P(("seq", "head"), None)
    return jax.shard_map(
        per_device,
        mesh=mesh,
        in_specs=(tokens, routes, routes, routes, P(), tokens),
        out_specs=(tokens, tokens, routes),
        check_vma=False,
    )
```

```python
import math

import jax
import jax.numpy as jnp
from jax import lax
from jax.experimental import pallas as pl
from jax.experimental.pallas import tpu as pltpu
from jax.sharding import PartitionSpec as P

H = 64
CAP = 48
OWN = 4
PEERS = 16
SPAN = PEERS * CAP
HS = 128
WIDE = 4 * HS
QT = 256
WIN = 1152
KC = 384
MASKED = -1e30
F32 = jnp.float32
BF16 = jnp.bfloat16
MESH = pl.DeviceIdType.MESH


def dot_nt(a, b):
    return lax.dot_general(a, b, (((1,), (1,)), ((), ())), preferred_element_type=F32)


def dot(a, b):
    return jnp.dot(a, b, preferred_element_type=F32)


def one_hot(mask):
    return jnp.where(mask, 1.0, 0.0).astype(BF16)


def thirds(v):
    high = v.astype(BF16).astype(F32)
    middle = (v - high).astype(BF16).astype(F32)
    return [high, middle, v - high - middle]


def dest_weight(f):
    return jnp.where(f < 8, float(CAP), jnp.where(f < 16, 1.0, 0.0)).astype(BF16)


def div48(v):
    return (v * 1366) >> 16


def kernel(
    proj_hbm,
    cot_hbm,
    heads_ref,
    slots_ref,
    logits_ref,
    lengths_ref,
    head_out_hbm,
    proj_out_hbm,
    gate_out,
    x_proj,
    x_cot,
    x_grad,
    token_hot,
    dest_ref,
    gate_ref,
    rows_ref,
    out_acc,
    out_head,
    out_proj,
    dots,
    fsend,
    frecv,
    doc_send,
    doc_recv,
    doc_prev,
    kv_prev,
    dsend,
    drecv,
    rsend,
    rrecv,
    k_all,
    v_all,
    k_t,
    v_t,
    key_docs,
    query_docs,
    s_buf,
    p_buf,
    ds_buf,
    dk_acc,
    dv_acc,
    f_ssem,
    f_rsem,
    doc_ssem,
    doc_rsem,
    dp_sem,
    kv_ssem,
    kv_rsem,
    d_ssem,
    d_rsem,
    r_ssem,
    r_rsem,
    in_sem,
    out_sem,
):
    me = lax.axis_index("head")
    here = lax.axis_index("seq")
    after = lax.rem(here + 1, PEERS)
    before = lax.rem(here + PEERS - 1, PEERS)
    routes = proj_hbm.shape[0]
    tokens = heads_ref.shape[1]
    tiles = routes // 128
    scaling = HS ** (-0.5)
    proj_in = pltpu.make_async_copy(proj_hbm, x_proj, in_sem.at[0])
    cot_in = pltpu.make_async_copy(cot_hbm, x_cot, in_sem.at[1])
    cot_in.start()
    proj_in.start()

    barrier = pltpu.get_barrier_semaphore()

    def peer_of(d):
        px = lax.rem(lax.rem(me, 4) + lax.rem(d, 4), 4)
        py = lax.rem(me // 4 + d // 4, 4)
        return py * 4 + px

    @pl.loop(1, PEERS)
    def _(d):
        pl.semaphore_signal(barrier, inc=1, device_id={"head": peer_of(d)}, device_id_type=MESH)

    pl.semaphore_signal(barrier, inc=1, device_id={"seq": after}, device_id_type=MESH)
    pl.semaphore_signal(barrier, inc=1, device_id={"seq": before}, device_id_type=MESH)

    def block(i):
        return pl.ds(pl.multiple_of(i * CAP, CAP), CAP)

    def fwd_copy(a, d):
        peer = peer_of(d)
        return pltpu.make_async_remote_copy(
            src_ref=fsend.at[a, block(peer)],
            dst_ref=frecv.at[a, block(me)],
            send_sem=f_ssem.at[a, d],
            recv_sem=f_rsem.at[a, d],
            device_id={"head": peer},
            device_id_type=MESH,
        )

    def ret_copy(a, d):
        peer = peer_of(d)
        return pltpu.make_async_remote_copy(
            src_ref=rsend.at[a, block(peer)],
            dst_ref=rrecv.at[a, block(me)],
            send_sem=r_ssem.at[a, d],
            recv_sem=r_rsem.at[a, d],
            device_id={"head": peer},
            device_id_type=MESH,
        )

    def doc_rows(i):
        return pl.ds(pl.multiple_of(i * 16, 16), 16)

    def doc_copy(d):
        peer = peer_of(d)
        return pltpu.make_async_remote_copy(
            src_ref=doc_send.at[doc_rows(peer)],
            dst_ref=doc_recv.at[doc_rows(me)],
            send_sem=doc_ssem.at[d],
            recv_sem=doc_rsem.at[d],
            device_id={"head": peer},
            device_id_type=MESH,
        )

    doc_shift = pltpu.make_async_remote_copy(
        src_ref=doc_recv,
        dst_ref=doc_prev,
        send_sem=dp_sem.at[0],
        recv_sem=dp_sem.at[1],
        device_id={"seq": after},
        device_id_type=MESH,
    )

    def kv_copy(a):
        return pltpu.make_async_remote_copy(
            src_ref=frecv.at[a, :, pl.ds(HS, 2 * HS)],
            dst_ref=kv_prev.at[a],
            send_sem=kv_ssem.at[a],
            recv_sem=kv_rsem.at[a],
            device_id={"seq": after},
            device_id_type=MESH,
        )

    def d_copy(a):
        return pltpu.make_async_remote_copy(
            src_ref=dsend.at[a],
            dst_ref=drecv.at[a],
            send_sem=d_ssem.at[a],
            recv_sem=d_rsem.at[a],
            device_id={"seq": before},
            device_id_type=MESH,
        )

    gate = 1.0 / (1.0 + jnp.exp(-logits_ref[...]))
    pieces = thirds(gate)
    fields = jnp.concatenate(
        [heads_ref[...].astype(F32), slots_ref[...].astype(F32)] + pieces, axis=0
    ).astype(BF16)
    count = fields.shape[0]

    @pl.loop(0, routes // 256)
    def _(c):
        rows = pl.ds(pl.multiple_of(c * 256, 256), 256)
        r = lax.broadcasted_iota(jnp.int32, (256, tokens), 0)
        t = lax.broadcasted_iota(jnp.int32, (256, tokens), 1)
        token_hot[rows, :] = one_hot((r >> 3) + c * 32 == t)
        mixed = dot_nt(token_hot[rows, :], fields)
        r = lax.broadcasted_iota(jnp.int32, (256, count), 0)
        f = lax.broadcasted_iota(jnp.int32, (256, count), 1)
        mixed = jnp.where((r & 7) == (f & 7), mixed, 0.0).astype(BF16)
        f = lax.broadcasted_iota(jnp.int32, (count, 128), 0)
        dest_ref[rows, :] = dot(mixed, dest_weight(f))
        gate_col = dot(mixed, one_hot(f >= 16))
        gate_ref[rows, :] = gate_col
        f = lax.broadcasted_iota(jnp.int32, (8, count), 1)
        want = lax.broadcasted_iota(jnp.int32, (8, count), 0)
        as_head = (want == 1) & (f < 8)
        as_slot = (want == 2) & (f >= 8) & (f < 16)
        weight = jnp.where(want == 0, dest_weight(f).astype(F32), jnp.where(as_head | as_slot, 1.0, 0.0))
        rows_ref[:, rows] = dot_nt(weight.astype(BF16), mixed)

    cot_in.wait()

    @pl.loop(0, routes // 256)
    def _(c):
        rows = pl.ds(pl.multiple_of(c * 256, 256), 256)
        x_grad[rows, :] = (x_cot[rows, :].astype(F32) * gate_ref[rows, :]).astype(BF16)

    proj_in.wait()

    def dispatch(a, c):
        first = pl.multiple_of(lax.rem(me // 4 + c, 4) * (4 * CAP), 4 * CAP)
        rows = pl.ds(first, 4 * CAP)
        r = lax.broadcasted_iota(jnp.int32, (4 * CAP, 128), 0) + first
        source = div48(r)
        ids = (source * (OWN * CAP) + (r - source * CAP) + a * CAP).astype(F32)
        hot = one_hot(jnp.concatenate([ids] * tiles, axis=1) == rows_ref[0:1, :])
        fsend[a, rows, : 3 * HS] = dot(hot, x_proj[...]).astype(BF16)
        fsend[a, rows, 3 * HS :] = dot(hot, x_grad[...]).astype(BF16)

    def ship(a, c):
        @pl.loop(0, 4)
        def _(x):
            @pl.when(c * 4 + x > 0)
            def _():
                fwd_copy(a, c * 4 + x).start()

    dispatch(0, 0)
    pl.semaphore_wait(barrier, PEERS + 1)
    ship(0, 0)

    @pl.loop(1, 4)
    def _(n):
        dispatch(0, n)
        ship(0, n)

    lane_route = lax.broadcasted_iota(jnp.int32, (8, routes), 1)
    position = (lane_route >> 3) + (here * PEERS + me) * tokens
    docs = jnp.ones((8, routes), F32)
    end = lengths_ref[0]
    for n in range(lengths_ref.shape[0]):
        docs = docs + jnp.where(position >= end, 1.0, 0.0)
        if n + 1 < lengths_ref.shape[0]:
            end = end + lengths_ref[n + 1]
    row = lax.broadcasted_iota(jnp.int32, (256, 128), 0)
    row_head = (4 * (row >> 4) + (row & 3)).astype(F32)
    at_head = jnp.concatenate([row_head] * tiles, axis=1) == rows_ref[1:2, :]
    docs_wide = jnp.where(at_head, docs[0:1, :], 0.0).astype(BF16)
    lane_slot = lax.broadcasted_iota(jnp.int32, (128, 128), 0).astype(F32)
    at_slot = one_hot(jnp.concatenate([lane_slot] * tiles, axis=1) == rows_ref[2:3, :])
    doc_send[...] = dot_nt(docs_wide, at_slot).astype(BF16)
    doc_recv[doc_rows(me), :] = doc_send[doc_rows(me), :]

    @pl.loop(1, PEERS)
    def _(d):
        doc_copy(d).start()

    @pl.loop(4, 4 * OWN)
    def _(n):
        dispatch(n >> 2, n & 3)
        ship(n >> 2, n & 3)

    @pl.loop(0, OWN)
    def _(a):
        frecv[a, block(me), :] = fsend[a, block(me), :]

    @pl.loop(1, PEERS)
    def _(d):
        doc_copy(d).wait_recv()

    doc_shift.start()

    def take_head(a):
        @pl.loop(1, PEERS)
        def _(d):
            fwd_copy(a, d).wait_recv()

        kv_copy(a).start()

    def head_docs(a, docs_ref):
        r = lax.broadcasted_iota(jnp.int32, (SPAN, 128), 0)
        lane = lax.broadcasted_iota(jnp.int32, (SPAN, 128), 1)
        source = div48(r)
        wanted = source * 16 + a
        pick = one_hot(jnp.concatenate([lane, lane + 128], axis=1) == jnp.concatenate([wanted] * 2, axis=1))
        spread = dot(pick, docs_ref[...])
        return jnp.where(lane == r - source * CAP, spread, 0.0).astype(BF16)

    def attention(a):
        k_all[:SPAN, :] = kv_prev[a, :, :HS]
        v_all[:SPAN, :] = kv_prev[a, :, HS:]
        k_all[SPAN:, :] = frecv[a, :, HS : 2 * HS]
        v_all[SPAN:, :] = frecv[a, :, 2 * HS : 3 * HS]
        k_t[...] = k_all[...].T
        v_t[...] = v_all[...].T
        ones = jnp.ones((HS, HS), BF16)
        mine = head_docs(a, doc_recv)
        key_docs[:SPAN, :] = dot(head_docs(a, doc_prev), ones)
        key_docs[SPAN:, :] = dot(mine, ones)
        query_docs[...] = dot_nt(ones[:8], mine)
        dk_acc[a] = jnp.zeros((2 * SPAN, HS), F32)
        dv_acc[a] = jnp.zeros((2 * SPAN, HS), F32)

        @pl.loop(0, SPAN // QT)
        def _(i):
            first = pl.multiple_of(i * QT, QT)
            start = pl.multiple_of(((i * (i + 1)) >> 1) * 128, 128)
            q = frecv[a, pl.ds(first, QT), :HS]
            out_grad = frecv[a, pl.ds(first, QT), 3 * HS :]
            q_docs = query_docs[0:1, pl.ds(first, QT)]
            top = jnp.full((1, QT), MASKED, F32)
            for c in range(WIN // KC):
                keys = pl.ds(pl.multiple_of(start + c * KC, 128), KC)
                s = dot_nt(k_all[keys, :], q) * (scaling * math.log2(math.e))
                docs = key_docs[keys, :]
                seen = jnp.concatenate([docs, docs], axis=1) == q_docs
                if (c + 1) * KC > SPAN:
                    k_at = lax.broadcasted_iota(jnp.int32, (KC, QT), 0) + (start + c * KC - SPAN)
                    q_at = lax.broadcasted_iota(jnp.int32, (KC, QT), 1) + first
                    seen = seen & (k_at <= q_at)
                s = jnp.where(seen, s, MASKED)
                s_buf[c * KC : (c + 1) * KC, :] = s
                top = jnp.maximum(top, jnp.max(s, axis=0, keepdims=True))
            total = jnp.zeros((1, QT), F32)
            for c in range(WIN // KC):
                part = slice(c * KC, (c + 1) * KC)
                p = jnp.exp2(s_buf[part, :] - top)
                total = total + jnp.sum(p, axis=0, keepdims=True)
                s_buf[part, :] = p
                p_buf[part, :] = p.astype(BF16)
            inverse = 1.0 / total
            window = pl.ds(start, WIN)
            attended = (dot(v_t[:, window], p_buf[...]) * inverse).astype(BF16)
            out_grad_t = (out_grad.astype(F32).T * inverse).astype(BF16)
            delta = jnp.sum(out_grad_t.astype(F32) * attended.astype(F32), axis=0, keepdims=True)
            for c in range(WIN // KC):
                part = slice(c * KC, (c + 1) * KC)
                keys = pl.ds(pl.multiple_of(start + c * KC, 128), KC)
                dp = dot(v_all[keys, :], out_grad_t)
                ds = (s_buf[part, :] * (dp - delta)).astype(BF16)
                ds_buf[part, :] = ds
                dv_acc[a, keys, :] += dot_nt(p_buf[part, :], out_grad_t)
                dk_acc[a, keys, :] += dot(ds, q)
            dq = dot(k_t[:, window], ds_buf[...]) * scaling
            rsend[a, pl.ds(first, QT), :HS] = attended.astype(F32).T.astype(BF16)
            rsend[a, pl.ds(first, QT), HS : 2 * HS] = dq.T.astype(BF16)

        dsend[a, :, :HS] = (dk_acc[a, :SPAN, :] * scaling).astype(BF16)
        dsend[a, :, HS:] = dv_acc[a, :SPAN, :].astype(BF16)
        d_copy(a).start()

    def finish(a):
        d_copy(a).wait_recv()
        dk = dk_acc[a, SPAN:, :] * scaling + drecv[a, :, :HS].astype(F32)
        dv = dv_acc[a, SPAN:, :] + drecv[a, :, HS:].astype(F32)
        rsend[a, :, 2 * HS : 3 * HS] = dk.astype(BF16)
        rsend[a, :, 3 * HS :] = dv.astype(BF16)

        @pl.loop(1, PEERS)
        def _(d):
            ret_copy(a, d).start()

        rrecv[a, block(me), :] = rsend[a, block(me), :]

    take_head(0)
    doc_shift.wait_recv()

    @pl.loop(0, OWN)
    def _(a):
        @pl.when(a < OWN - 1)
        def _():
            take_head(a + 1)

        kv_copy(a).wait_recv()
        attention(a)

        @pl.when(a > 0)
        def _():
            finish(a - 1)

    finish(OWN - 1)

    def gathered(a, rows):
        lane = lax.broadcasted_iota(jnp.int32, (8, SPAN), 1)
        source = div48(lane)
        ids = (source * (OWN * CAP) + (lane - source * CAP) + a * CAP).astype(F32)
        dest = dest_ref[rows, :]
        hot = one_hot(jnp.concatenate([dest] * (SPAN // 128), axis=1) == ids[0:1, :])
        return dot(hot, rrecv[a])

    def await_home(a):
        @pl.loop(1, PEERS)
        def _(d):
            ret_copy(a, d).wait_recv()

    def out_rows(c):
        return pl.ds(pl.multiple_of(c * 256, 256), 256)

    def out_copies(c):
        rows = out_rows(c)
        head = pltpu.make_async_copy(out_head.at[rows], head_out_hbm.at[rows], out_sem.at[c, 0])
        proj = pltpu.make_async_copy(out_proj.at[rows], proj_out_hbm.at[rows], out_sem.at[c, 1])
        return head, proj

    @pl.loop(0, OWN - 1)
    def _(a):
        await_home(a)

        @pl.loop(0, routes // 256)
        def _(c):
            rows = out_rows(c)
            more = gathered(a, rows)

            @pl.when(a == 0)
            def _():
                out_acc[rows, :] = more.astype(BF16)

            @pl.when(a > 0)
            def _():
                out_acc[rows, :] = (out_acc[rows, :].astype(F32) + more).astype(BF16)

    await_home(OWN - 1)

    @pl.loop(0, routes // 256)
    def _(c):
        rows = out_rows(c)
        full = out_acc[rows, :].astype(F32) + gathered(OWN - 1, rows)
        out_proj[rows, :] = full[:, HS:].astype(BF16)
        attended = full[:, :HS]
        weight = gate_ref[rows, :]
        out_head[rows, :] = (attended * weight).astype(BF16)
        for copy in out_copies(c):
            copy.start()
        inner = jnp.sum(x_cot[rows, :].astype(F32) * attended, axis=1, keepdims=True)
        r = lax.broadcasted_iota(jnp.int32, (256, HS), 0)
        lane = lax.broadcasted_iota(jnp.int32, (256, HS), 1)
        dots[rows, :] = jnp.where((r & 7) == lane, inner * weight * (1.0 - weight), 0.0)

    eye = one_hot(
        lax.broadcasted_iota(jnp.int32, (8, HS), 0) == lax.broadcasted_iota(jnp.int32, (8, HS), 1)
    )
    by_route = sum(dot_nt(eye, part.astype(BF16)) for part in thirds(dots[...]))
    gate_out[...] = sum(dot(part.astype(BF16), token_hot[...]) for part in thirds(by_route))

    @pl.loop(0, routes // 256)
    def _(c):
        for copy in out_copies(c):
            copy.wait()

    @pl.loop(1, PEERS)
    def _(d):
        doc_copy(d).wait_send()

    doc_shift.wait_send()

    @pl.loop(0, OWN)
    def _(a):
        @pl.loop(1, PEERS)
        def _(d):
            fwd_copy(a, d).wait_send()
            ret_copy(a, d).wait_send()

        kv_copy(a).wait_send()
        d_copy(a).wait_send()


def per_device(projections, routed_heads, slot_index, gate_logits, doc_lengths, cotangent):
    tokens, top, width = projections.shape
    routes = tokens * top
    dma = pltpu.SemaphoreType.DMA
    vmem = pltpu.VMEM
    whole = pl.BlockSpec(memory_space=pltpu.VMEM)
    away = pl.BlockSpec(memory_space=pl.ANY)
    head_outputs, projection_grads, gate_grads = pl.pallas_call(
        kernel,
        out_shape=(
            jax.ShapeDtypeStruct((routes, HS), BF16),
            jax.ShapeDtypeStruct((routes, 3 * HS), BF16),
            jax.ShapeDtypeStruct((top, tokens), F32),
        ),
        in_specs=[away, away, whole, whole, whole, pl.BlockSpec(memory_space=pltpu.SMEM)],
        out_specs=(away, away, whole),
        scratch_shapes=[
            vmem((routes, 3 * HS), BF16),
            vmem((routes, HS), BF16),
            vmem((routes, HS), BF16),
            vmem((routes, tokens), BF16),
            vmem((routes, HS), F32),
            vmem((routes, HS), F32),
            vmem((8, routes), F32),
            vmem((routes, WIDE), BF16),
            vmem((routes, HS), BF16),
            vmem((routes, 3 * HS), BF16),
            vmem((routes, HS), F32),
            vmem((OWN, SPAN, WIDE), BF16),
            vmem((OWN, SPAN, WIDE), BF16),
            vmem((PEERS * 16, 128), BF16),
            vmem((PEERS * 16, 128), BF16),
            vmem((PEERS * 16, 128), BF16),
            vmem((OWN, SPAN, 2 * HS), BF16),
            vmem((OWN, SPAN, 2 * HS), BF16),
            vmem((OWN, SPAN, 2 * HS), BF16),
            vmem((OWN, SPAN, WIDE), BF16),
            vmem((OWN, SPAN, WIDE), BF16),
            vmem((2 * SPAN, HS), BF16),
            vmem((2 * SPAN, HS), BF16),
            vmem((HS, 2 * SPAN), BF16),
            vmem((HS, 2 * SPAN), BF16),
            vmem((2 * SPAN, HS), F32),
            vmem((8, SPAN), F32),
            vmem((WIN, QT), F32),
            vmem((WIN, QT), BF16),
            vmem((WIN, QT), BF16),
            vmem((OWN, 2 * SPAN, HS), F32),
            vmem((OWN, 2 * SPAN, HS), F32),
            dma((OWN, PEERS)),
            dma((OWN, PEERS)),
            dma((PEERS,)),
            dma((PEERS,)),
            dma((2,)),
            dma((OWN,)),
            dma((OWN,)),
            dma((OWN,)),
            dma((OWN,)),
            dma((OWN, PEERS)),
            dma((OWN, PEERS)),
            dma((2,)),
            dma((routes // 256, 2)),
        ],
        compiler_params=pltpu.CompilerParams(
            collective_id=0, has_side_effects=True, vmem_limit_bytes=60000 * 1024
        ),
    )(
        projections.reshape(routes, width),
        cotangent.reshape(routes, HS),
        routed_heads.T,
        slot_index.T,
        gate_logits.T,
        doc_lengths,
    )
    return (
        head_outputs.reshape(tokens, top, HS),
        projection_grads.reshape(tokens, top, width),
        gate_grads.T,
    )


def solution(mesh):
    tokens = P(("seq", "head"), None, None)
    routes = P(("seq", "head"), None)
    return jax.shard_map(
        per_device,
        mesh=mesh,
        in_specs=(tokens, routes, routes, routes, P(), tokens),
        out_specs=(tokens, tokens, routes),
        check_vma=False,
    )
```

```python
import math

import jax
import jax.numpy as jnp
from jax import lax
from jax.experimental import pallas as pl
from jax.experimental.pallas import tpu as pltpu
from jax.sharding import PartitionSpec as P

H = 64
CAP = 48
OWN = 4
PEERS = 16
SPAN = PEERS * CAP
HS = 128
WIDE = 4 * HS
QT = 256
WIN = 1152
KC = 384
MASKED = -1e30
F32 = jnp.float32
BF16 = jnp.bfloat16
MESH = pl.DeviceIdType.MESH


def dot_nt(a, b):
    return lax.dot_general(a, b, (((1,), (1,)), ((), ())), preferred_element_type=F32)


def dot(a, b):
    return jnp.dot(a, b, preferred_element_type=F32)


def one_hot(mask):
    return jnp.where(mask, 1.0, 0.0).astype(BF16)


def thirds(v):
    high = v.astype(BF16).astype(F32)
    middle = (v - high).astype(BF16).astype(F32)
    return [high, middle, v - high - middle]


def dest_weight(f):
    return jnp.where(f < 8, float(CAP), jnp.where(f < 16, 1.0, 0.0)).astype(BF16)


def div48(v):
    return (v * 1366) >> 16


def token_rows(c, tokens):
    r = lax.broadcasted_iota(jnp.int32, (256, tokens), 0)
    t = lax.broadcasted_iota(jnp.int32, (256, tokens), 1)
    return one_hot((r >> 3) + c * 32 == t)


def slot_rows(dest, a):
    lane = lax.broadcasted_iota(jnp.int32, (8, SPAN), 1)
    source = div48(lane)
    ids = (source * (OWN * CAP) + (lane - source * CAP) + a * CAP).astype(F32)
    return one_hot(jnp.concatenate([dest] * (SPAN // 128), axis=1) == ids[0:1, :])


def kernel(
    proj_hbm,
    cot_hbm,
    heads_ref,
    slots_ref,
    logits_ref,
    lengths_hbm,
    routes_out,
    last_out,
    dest_out,
    gate_out,
    lengths_ref,
    x_proj,
    x_cot,
    x_grad,
    dest_ref,
    gate_ref,
    rows_ref,
    out_acc,
    fsend,
    frecv,
    doc_send,
    doc_recv,
    doc_prev,
    kv_prev,
    dsend,
    drecv,
    rsend,
    rrecv,
    k_all,
    v_all,
    k_t,
    v_t,
    key_docs,
    query_docs,
    s_buf,
    p_buf,
    ds_buf,
    dk_acc,
    dv_acc,
    f_ssem,
    f_rsem,
    doc_ssem,
    doc_rsem,
    dp_sem,
    kv_ssem,
    kv_rsem,
    d_ssem,
    d_rsem,
    r_ssem,
    r_rsem,
    in_sem,
    out_sem,
):
    me = lax.axis_index("head")
    here = lax.axis_index("seq")
    after = lax.rem(here + 1, PEERS)
    before = lax.rem(here + PEERS - 1, PEERS)
    routes = proj_hbm.shape[0]
    tokens = heads_ref.shape[1]
    tiles = routes // 128
    scaling = HS ** (-0.5)
    proj_in = pltpu.make_async_copy(proj_hbm, x_proj, in_sem.at[0])
    cot_in = pltpu.make_async_copy(cot_hbm, x_cot, in_sem.at[1])
    lengths_in = pltpu.make_async_copy(lengths_hbm, lengths_ref, in_sem.at[2])
    cot_in.start()
    proj_in.start()
    lengths_in.start()

    barrier = pltpu.get_barrier_semaphore()

    def peer_of(d):
        px = lax.rem(lax.rem(me, 4) + lax.rem(d, 4), 4)
        py = lax.rem(me // 4 + d // 4, 4)
        return py * 4 + px

    @pl.loop(1, PEERS)
    def _(d):
        pl.semaphore_signal(barrier, inc=1, device_id={"head": peer_of(d)}, device_id_type=MESH)

    pl.semaphore_signal(barrier, inc=1, device_id={"seq": after}, device_id_type=MESH)
    pl.semaphore_signal(barrier, inc=1, device_id={"seq": before}, device_id_type=MESH)

    def block(i):
        return pl.ds(pl.multiple_of(i * CAP, CAP), CAP)

    def fwd_copy(a, d):
        peer = peer_of(d)
        return pltpu.make_async_remote_copy(
            src_ref=fsend.at[a, block(peer)],
            dst_ref=frecv.at[a, block(me)],
            send_sem=f_ssem.at[a, d],
            recv_sem=f_rsem.at[a, d],
            device_id={"head": peer},
            device_id_type=MESH,
        )

    def ret_copy(a, d):
        peer = peer_of(d)
        return pltpu.make_async_remote_copy(
            src_ref=rsend.at[a, block(peer)],
            dst_ref=rrecv.at[a, block(me)],
            send_sem=r_ssem.at[a, d],
            recv_sem=r_rsem.at[a, d],
            device_id={"head": peer},
            device_id_type=MESH,
        )

    def last_copy(d):
        peer = peer_of(d)
        return pltpu.make_async_remote_copy(
            src_ref=rsend.at[OWN - 1, block(peer)],
            dst_ref=last_out.at[block(me)],
            send_sem=r_ssem.at[OWN - 1, d],
            recv_sem=r_rsem.at[OWN - 1, d],
            device_id={"head": peer},
            device_id_type=MESH,
        )

    def doc_rows(i):
        return pl.ds(pl.multiple_of(i * 16, 16), 16)

    def doc_copy(d):
        peer = peer_of(d)
        return pltpu.make_async_remote_copy(
            src_ref=doc_send.at[doc_rows(peer)],
            dst_ref=doc_recv.at[doc_rows(me)],
            send_sem=doc_ssem.at[d],
            recv_sem=doc_rsem.at[d],
            device_id={"head": peer},
            device_id_type=MESH,
        )

    doc_shift = pltpu.make_async_remote_copy(
        src_ref=doc_recv,
        dst_ref=doc_prev,
        send_sem=dp_sem.at[0],
        recv_sem=dp_sem.at[1],
        device_id={"seq": after},
        device_id_type=MESH,
    )

    def kv_copy(a):
        return pltpu.make_async_remote_copy(
            src_ref=frecv.at[a, :, pl.ds(HS, 2 * HS)],
            dst_ref=kv_prev.at[a],
            send_sem=kv_ssem.at[a],
            recv_sem=kv_rsem.at[a],
            device_id={"seq": after},
            device_id_type=MESH,
        )

    def d_copy(a):
        return pltpu.make_async_remote_copy(
            src_ref=dsend.at[a],
            dst_ref=drecv.at[a],
            send_sem=d_ssem.at[a],
            recv_sem=d_rsem.at[a],
            device_id={"seq": before},
            device_id_type=MESH,
        )

    gate = 1.0 / (1.0 + jnp.exp(-logits_ref[...]))
    pieces = thirds(gate)
    fields = jnp.concatenate(
        [heads_ref[...].astype(F32), slots_ref[...].astype(F32)] + pieces, axis=0
    ).astype(BF16)
    count = fields.shape[0]

    for c in range(routes // 256):
        rows = pl.ds(c * 256, 256)
        mixed = dot_nt(token_rows(c, tokens), fields)
        r = lax.broadcasted_iota(jnp.int32, (256, count), 0)
        f = lax.broadcasted_iota(jnp.int32, (256, count), 1)
        mixed = jnp.where((r & 7) == (f & 7), mixed, 0.0).astype(BF16)
        f = lax.broadcasted_iota(jnp.int32, (count, 128), 0)
        dest_ref[rows, :] = dot(mixed, dest_weight(f))
        gate_ref[rows, :] = dot(mixed, one_hot(f >= 16))
        f = lax.broadcasted_iota(jnp.int32, (8, count), 1)
        want = lax.broadcasted_iota(jnp.int32, (8, count), 0)
        as_head = (want == 1) & (f < 8)
        as_slot = (want == 2) & (f >= 8) & (f < 16)
        weight = jnp.where(want == 0, dest_weight(f).astype(F32), jnp.where(as_head | as_slot, 1.0, 0.0))
        rows_ref[:, rows] = dot_nt(weight.astype(BF16), mixed)

    cot_in.wait()
    for c in range(routes // 256):
        rows = pl.ds(c * 256, 256)
        x_grad[rows, :] = (x_cot[rows, :].astype(F32) * gate_ref[rows, :]).astype(BF16)

    proj_in.wait()
    dest_copy = pltpu.make_async_copy(dest_ref, dest_out, out_sem.at[0])
    gate_copy = pltpu.make_async_copy(gate_ref, gate_out, out_sem.at[1])
    dest_copy.start()
    gate_copy.start()

    def dispatch(a, c):
        first = pl.multiple_of(lax.rem(me // 4 + c, 4) * (4 * CAP), 4 * CAP)
        rows = pl.ds(first, 4 * CAP)
        r = lax.broadcasted_iota(jnp.int32, (4 * CAP, 128), 0) + first
        source = div48(r)
        ids = (source * (OWN * CAP) + (r - source * CAP) + a * CAP).astype(F32)
        hot = one_hot(jnp.concatenate([ids] * tiles, axis=1) == rows_ref[0:1, :])
        fsend[a, rows, : 3 * HS] = dot(hot, x_proj[...]).astype(BF16)
        fsend[a, rows, 3 * HS :] = dot(hot, x_grad[...]).astype(BF16)

    def ship(a, c):
        @pl.loop(0, 4)
        def _(x):
            @pl.when(c * 4 + x > 0)
            def _():
                fwd_copy(a, c * 4 + x).start()

    dispatch(0, 0)
    pl.semaphore_wait(barrier, PEERS + 1)
    ship(0, 0)

    @pl.loop(1, 4)
    def _(n):
        dispatch(0, n)
        ship(0, n)

    lane_route = lax.broadcasted_iota(jnp.int32, (8, routes), 1)
    position = (lane_route >> 3) + (here * PEERS + me) * tokens
    docs = jnp.ones((8, routes), F32)
    lengths_in.wait()
    end = lengths_ref[0]
    for n in range(lengths_ref.shape[0]):
        docs = docs + jnp.where(position >= end, 1.0, 0.0)
        if n + 1 < lengths_ref.shape[0]:
            end = end + lengths_ref[n + 1]
    row = lax.broadcasted_iota(jnp.int32, (256, 128), 0)
    row_head = (4 * (row >> 4) + (row & 3)).astype(F32)
    at_head = jnp.concatenate([row_head] * tiles, axis=1) == rows_ref[1:2, :]
    docs_wide = jnp.where(at_head, docs[0:1, :], 0.0).astype(BF16)
    lane_slot = lax.broadcasted_iota(jnp.int32, (128, 128), 0).astype(F32)
    at_slot = one_hot(jnp.concatenate([lane_slot] * tiles, axis=1) == rows_ref[2:3, :])
    doc_send[...] = dot_nt(docs_wide, at_slot).astype(BF16)
    doc_recv[doc_rows(me), :] = doc_send[doc_rows(me), :]

    @pl.loop(1, PEERS)
    def _(d):
        doc_copy(d).start()

    @pl.loop(4, 4 * OWN)
    def _(n):
        dispatch(n >> 2, n & 3)
        ship(n >> 2, n & 3)

    @pl.loop(0, OWN)
    def _(a):
        frecv[a, block(me), :] = fsend[a, block(me), :]

    @pl.loop(1, PEERS)
    def _(d):
        doc_copy(d).wait_recv()

    doc_shift.start()

    def take_head(a):
        @pl.loop(1, PEERS)
        def _(d):
            fwd_copy(a, d).wait_recv()

        kv_copy(a).start()

    def head_docs(a, docs_ref):
        r = lax.broadcasted_iota(jnp.int32, (SPAN, 128), 0)
        lane = lax.broadcasted_iota(jnp.int32, (SPAN, 128), 1)
        source = div48(r)
        wanted = source * 16 + a
        pick = one_hot(jnp.concatenate([lane, lane + 128], axis=1) == jnp.concatenate([wanted] * 2, axis=1))
        spread = dot(pick, docs_ref[...])
        return jnp.where(lane == r - source * CAP, spread, 0.0).astype(BF16)

    def attention(a):
        k_all[:SPAN, :] = kv_prev[a, :, :HS]
        v_all[:SPAN, :] = kv_prev[a, :, HS:]
        k_all[SPAN:, :] = frecv[a, :, HS : 2 * HS]
        v_all[SPAN:, :] = frecv[a, :, 2 * HS : 3 * HS]
        k_t[...] = k_all[...].T
        v_t[...] = v_all[...].T
        ones = jnp.ones((HS, HS), BF16)
        mine = head_docs(a, doc_recv)
        key_docs[:SPAN, :] = dot(head_docs(a, doc_prev), ones)
        key_docs[SPAN:, :] = dot(mine, ones)
        query_docs[...] = dot_nt(ones[:8], mine)
        dk_acc[a] = jnp.zeros((2 * SPAN, HS), F32)
        dv_acc[a] = jnp.zeros((2 * SPAN, HS), F32)

        @pl.loop(0, SPAN // QT)
        def _(i):
            first = pl.multiple_of(i * QT, QT)
            start = pl.multiple_of(((i * (i + 1)) >> 1) * 128, 128)
            q = frecv[a, pl.ds(first, QT), :HS]
            out_grad = frecv[a, pl.ds(first, QT), 3 * HS :]
            q_docs = query_docs[0:1, pl.ds(first, QT)]
            top = jnp.full((1, QT), MASKED, F32)
            for c in range(WIN // KC):
                keys = pl.ds(pl.multiple_of(start + c * KC, 128), KC)
                s = dot_nt(k_all[keys, :], q) * (scaling * math.log2(math.e))
                docs = key_docs[keys, :]
                seen = jnp.concatenate([docs, docs], axis=1) == q_docs
                if (c + 1) * KC > SPAN:
                    k_at = lax.broadcasted_iota(jnp.int32, (KC, QT), 0) + (start + c * KC - SPAN)
                    q_at = lax.broadcasted_iota(jnp.int32, (KC, QT), 1) + first
                    seen = seen & (k_at <= q_at)
                s = jnp.where(seen, s, MASKED)
                s_buf[c * KC : (c + 1) * KC, :] = s
                top = jnp.maximum(top, jnp.max(s, axis=0, keepdims=True))
            total = jnp.zeros((1, QT), F32)
            for c in range(WIN // KC):
                part = slice(c * KC, (c + 1) * KC)
                p = jnp.exp2(s_buf[part, :] - top)
                total = total + jnp.sum(p, axis=0, keepdims=True)
                s_buf[part, :] = p
                p_buf[part, :] = p.astype(BF16)
            inverse = 1.0 / total
            window = pl.ds(start, WIN)
            attended = (dot(v_t[:, window], p_buf[...]) * inverse).astype(BF16)
            out_grad_t = (out_grad.astype(F32).T * inverse).astype(BF16)
            delta = jnp.sum(out_grad_t.astype(F32) * attended.astype(F32), axis=0, keepdims=True)
            for c in range(WIN // KC):
                part = slice(c * KC, (c + 1) * KC)
                keys = pl.ds(pl.multiple_of(start + c * KC, 128), KC)
                dp = dot(v_all[keys, :], out_grad_t)
                ds = (s_buf[part, :] * (dp - delta)).astype(BF16)
                ds_buf[part, :] = ds
                dv_acc[a, keys, :] += dot_nt(p_buf[part, :], out_grad_t)
                dk_acc[a, keys, :] += dot(ds, q)
            dq = dot(k_t[:, window], ds_buf[...]) * scaling
            rsend[a, pl.ds(first, QT), :HS] = attended.astype(F32).T.astype(BF16)
            rsend[a, pl.ds(first, QT), HS : 2 * HS] = dq.T.astype(BF16)

        dsend[a, :, :HS] = (dk_acc[a, :SPAN, :] * scaling).astype(BF16)
        dsend[a, :, HS:] = dv_acc[a, :SPAN, :].astype(BF16)
        d_copy(a).start()

    def finish(a):
        d_copy(a).wait_recv()
        dk = dk_acc[a, SPAN:, :] * scaling + drecv[a, :, :HS].astype(F32)
        dv = dv_acc[a, SPAN:, :] + drecv[a, :, HS:].astype(F32)
        rsend[a, :, 2 * HS : 3 * HS] = dk.astype(BF16)
        rsend[a, :, 3 * HS :] = dv.astype(BF16)

    take_head(0)
    doc_shift.wait_recv()

    @pl.loop(0, OWN)
    def _(a):
        @pl.when(a < OWN - 1)
        def _():
            take_head(a + 1)

        kv_copy(a).wait_recv()
        attention(a)

        @pl.when(a > 0)
        def _():
            finish(a - 1)

            @pl.loop(1, PEERS)
            def _(d):
                ret_copy(a - 1, d).start()

            rrecv[a - 1, block(me), :] = rsend[a - 1, block(me), :]

    finish(OWN - 1)

    @pl.loop(1, PEERS)
    def _(d):
        last_copy(d).start()

    own_last = pltpu.make_async_copy(
        rsend.at[OWN - 1, block(me)], last_out.at[block(me)], out_sem.at[3]
    )
    own_last.start()

    @pl.loop(0, OWN - 1)
    def _(a):
        @pl.loop(1, PEERS)
        def _(d):
            ret_copy(a, d).wait_recv()

        @pl.loop(0, routes // 256)
        def _(c):
            rows = pl.ds(pl.multiple_of(c * 256, 256), 256)
            more = dot(slot_rows(dest_ref[rows, :], a), rrecv[a])

            @pl.when(a == 0)
            def _():
                out_acc[rows, :] = more.astype(BF16)

            @pl.when(a > 0)
            def _():
                out_acc[rows, :] = (out_acc[rows, :].astype(F32) + more).astype(BF16)

    routes_copy = pltpu.make_async_copy(out_acc, routes_out, out_sem.at[2])
    routes_copy.start()

    @pl.loop(1, PEERS)
    def _(d):
        doc_copy(d).wait_send()

    doc_shift.wait_send()

    @pl.loop(0, OWN)
    def _(a):
        @pl.loop(1, PEERS)
        def _(d):
            fwd_copy(a, d).wait_send()

        kv_copy(a).wait_send()
        d_copy(a).wait_send()

    @pl.loop(0, OWN - 1)
    def _(a):
        @pl.loop(1, PEERS)
        def _(d):
            ret_copy(a, d).wait_send()

    dest_copy.wait()
    gate_copy.wait()
    routes_copy.wait()
    own_last.wait()

    @pl.loop(1, PEERS)
    def _(d):
        last_copy(d).wait()


def home_kernel(
    routes_ref,
    last_ref,
    dest_ref,
    gate_ref,
    cot_ref,
    logits_ref,
    head_out_hbm,
    proj_out_hbm,
    grad_out,
    out_head,
    out_proj,
    out_sem,
):
    tokens = logits_ref.shape[1]
    lane = lax.broadcasted_iota(jnp.int32, (8, HS), 1)
    eye = one_hot(lax.broadcasted_iota(jnp.int32, (8, HS), 0) == lane)
    grads = jnp.zeros((8, tokens), F32)
    copies = []
    for c in range(routes_ref.shape[0] // 256):
        rows = pl.ds(c * 256, 256)
        more = dot(slot_rows(dest_ref[rows, :], OWN - 1), last_ref[...])
        full = routes_ref[rows, :].astype(F32) + more
        out_proj[rows, :] = full[:, HS:].astype(BF16)
        attended = full[:, :HS]
        out_head[rows, :] = (attended * gate_ref[rows, :]).astype(BF16)
        for n, (source, target) in enumerate(((out_head, head_out_hbm), (out_proj, proj_out_hbm))):
            copies.append(pltpu.make_async_copy(source.at[rows], target.at[rows], out_sem.at[c, n]))
            copies[-1].start()
        inner = jnp.sum(cot_ref[rows, :].astype(F32) * attended, axis=1, keepdims=True)
        r = lax.broadcasted_iota(jnp.int32, (256, HS), 0)
        lane = lax.broadcasted_iota(jnp.int32, (256, HS), 1)
        dots = jnp.where((r & 7) == lane, inner, 0.0)
        by_route = sum(dot_nt(eye, part.astype(BF16)) for part in thirds(dots))
        hot = token_rows(c, tokens)
        grads = grads + sum(dot(part.astype(BF16), hot) for part in thirds(by_route))
    gate = 1.0 / (1.0 + jnp.exp(-logits_ref[...]))
    grad_out[...] = grads * gate * (1.0 - gate)
    for copy in copies:
        copy.wait()


def per_device(projections, routed_heads, slot_index, gate_logits, doc_lengths, cotangent):
    tokens, top, width = projections.shape
    routes = tokens * top
    dma = pltpu.SemaphoreType.DMA
    vmem = pltpu.VMEM
    whole = pl.BlockSpec(memory_space=pltpu.VMEM)
    away = pl.BlockSpec(memory_space=pl.ANY)
    hbm = pl.BlockSpec(memory_space=pltpu.HBM)
    cot_rows = cotangent.reshape(routes, HS)
    logits = gate_logits.T
    handed = pl.pallas_call(
        kernel,
        out_shape=(
            jax.ShapeDtypeStruct((routes, WIDE), BF16),
            jax.ShapeDtypeStruct((SPAN, WIDE), BF16),
            jax.ShapeDtypeStruct((routes, HS), F32),
            jax.ShapeDtypeStruct((routes, HS), F32),
        ),
        in_specs=[hbm, hbm, whole, whole, whole, hbm],
        out_specs=(away, away, away, away),
        scratch_shapes=[
            pltpu.SMEM(doc_lengths.shape, jnp.int32),
            vmem((routes, 3 * HS), BF16),
            vmem((routes, HS), BF16),
            vmem((routes, HS), BF16),
            vmem((routes, HS), F32),
            vmem((routes, HS), F32),
            vmem((8, routes), F32),
            vmem((routes, WIDE), BF16),
            vmem((OWN, SPAN, WIDE), BF16),
            vmem((OWN, SPAN, WIDE), BF16),
            vmem((PEERS * 16, 128), BF16),
            vmem((PEERS * 16, 128), BF16),
            vmem((PEERS * 16, 128), BF16),
            vmem((OWN, SPAN, 2 * HS), BF16),
            vmem((OWN, SPAN, 2 * HS), BF16),
            vmem((OWN, SPAN, 2 * HS), BF16),
            vmem((OWN, SPAN, WIDE), BF16),
            vmem((OWN, SPAN, WIDE), BF16),
            vmem((2 * SPAN, HS), BF16),
            vmem((2 * SPAN, HS), BF16),
            vmem((HS, 2 * SPAN), BF16),
            vmem((HS, 2 * SPAN), BF16),
            vmem((2 * SPAN, HS), F32),
            vmem((8, SPAN), F32),
            vmem((WIN, QT), F32),
            vmem((WIN, QT), BF16),
            vmem((WIN, QT), BF16),
            vmem((OWN, 2 * SPAN, HS), F32),
            vmem((OWN, 2 * SPAN, HS), F32),
            dma((OWN, PEERS)),
            dma((OWN, PEERS)),
            dma((PEERS,)),
            dma((PEERS,)),
            dma((2,)),
            dma((OWN,)),
            dma((OWN,)),
            dma((OWN,)),
            dma((OWN,)),
            dma((OWN, PEERS)),
            dma((OWN, PEERS)),
            dma((3,)),
            dma((4,)),
        ],
        compiler_params=pltpu.CompilerParams(
            collective_id=0, has_side_effects=True, vmem_limit_bytes=44000 * 1024
        ),
    )(
        *(
            pltpu.with_memory_space_constraint(v, pltpu.HBM)
            for v in (
                projections.reshape(routes, width),
                cot_rows,
                routed_heads.T,
                slot_index.T,
                logits,
                doc_lengths,
            )
        ),
    )
    head_outputs, projection_grads, gate_grads = pl.pallas_call(
        home_kernel,
        out_shape=(
            jax.ShapeDtypeStruct((routes, HS), BF16),
            jax.ShapeDtypeStruct((routes, 3 * HS), BF16),
            jax.ShapeDtypeStruct((top, tokens), F32),
        ),
        in_specs=[whole] * 6,
        out_specs=(hbm, hbm, whole),
        scratch_shapes=[
            vmem((routes, HS), BF16),
            vmem((routes, 3 * HS), BF16),
            dma((routes // 256, 2)),
        ],
        compiler_params=pltpu.CompilerParams(vmem_limit_bytes=16000 * 1024),
    )(*handed, cot_rows, logits)
    return (
        head_outputs.reshape(tokens, top, HS),
        projection_grads.reshape(tokens, top, width),
        gate_grads.T,
    )


def solution(mesh):
    tokens = P(("seq", "head"), None, None)
    routes = P(("seq", "head"), None)
    return jax.shard_map(
        per_device,
        mesh=mesh,
        in_specs=(tokens, routes, routes, routes, P(), tokens),
        out_specs=(tokens, tokens, routes),
        check_vma=False,
    )
```

```python
import math

import jax
import jax.numpy as jnp
from jax import lax
from jax.experimental import pallas as pl
from jax.experimental.pallas import tpu as pltpu
from jax.sharding import PartitionSpec as P

H = 64
CAP = 48
OWN = 4
PEERS = 16
SPAN = PEERS * CAP
HS = 128
WIDE = 4 * HS
QT = 256
WIN = 1152
KC = 384
EARLY = 512
READY = 11
MASKED = -1e30
F32 = jnp.float32
BF16 = jnp.bfloat16
MESH = pl.DeviceIdType.MESH


def dot_nt(a, b):
    return lax.dot_general(a, b, (((1,), (1,)), ((), ())), preferred_element_type=F32)


def dot(a, b):
    return jnp.dot(a, b, preferred_element_type=F32)


def one_hot(mask):
    return jnp.where(mask, 1.0, 0.0).astype(BF16)


def thirds(v):
    high = v.astype(BF16).astype(F32)
    middle = (v - high).astype(BF16).astype(F32)
    return [high, middle, v - high - middle]


def dest_weight(f):
    return jnp.where(f < 8, float(CAP), jnp.where(f < 16, 1.0, 0.0)).astype(BF16)


def div48(v):
    return (v * 1366) >> 16


def token_rows(c, tokens):
    r = lax.broadcasted_iota(jnp.int32, (256, tokens), 0)
    t = lax.broadcasted_iota(jnp.int32, (256, tokens), 1)
    return one_hot((r >> 3) + c * 32 == t)


def head_slots(a):
    lane = lax.broadcasted_iota(jnp.int32, (8, SPAN), 1)
    source = div48(lane)
    return (source * (OWN * CAP) + (lane - source * CAP) + a * CAP).astype(F32)


def last_slots(me, start, length):
    lane = lax.broadcasted_iota(jnp.int32, (8, length), 1) + start
    d = div48(lane)
    owner_x = (lax.rem(me, 4) + 4 - (d & 3)) & 3
    owner_y = (me // 4 + 4 - (d >> 2)) & 3
    owner = owner_y * 4 + owner_x
    return (owner * (OWN * CAP) + (lane - d * CAP) + (OWN - 1) * CAP).astype(F32)


def chosen(dest, ids):
    return one_hot(jnp.concatenate([dest] * (ids.shape[1] // 128), axis=1) == ids[0:1, :])


def kernel(
    proj_hbm,
    cot_hbm,
    heads_ref,
    slots_ref,
    logits_ref,
    lengths_hbm,
    out_acc,
    last_out,
    dest_ref,
    gate_ref,
    lengths_ref,
    x_proj,
    x_cot,
    x_grad,
    rows_ref,
    fsend,
    frecv,
    doc_send,
    doc_recv,
    doc_prev,
    kv_prev,
    dsend,
    drecv,
    rsend,
    rrecv,
    k_all,
    v_all,
    k_t,
    v_t,
    key_docs,
    query_docs,
    s_buf,
    p_buf,
    ds_buf,
    dk_acc,
    dv_acc,
    f_ssem,
    f_rsem,
    doc_ssem,
    doc_rsem,
    dp_sem,
    kv_ssem,
    kv_rsem,
    d_ssem,
    d_rsem,
    r_ssem,
    r_rsem,
    in_sem,
):
    me = lax.axis_index("head")
    here = lax.axis_index("seq")
    after = lax.rem(here + 1, PEERS)
    before = lax.rem(here + PEERS - 1, PEERS)
    routes = proj_hbm.shape[0]
    tokens = heads_ref.shape[1]
    tiles = routes // 128
    scaling = HS ** (-0.5)
    proj_in = pltpu.make_async_copy(proj_hbm, x_proj, in_sem.at[0])
    cot_in = pltpu.make_async_copy(cot_hbm, x_cot, in_sem.at[1])
    lengths_in = pltpu.make_async_copy(lengths_hbm, lengths_ref, in_sem.at[2])
    cot_in.start()
    proj_in.start()
    lengths_in.start()

    barrier = pltpu.get_barrier_semaphore()

    def peer_of(d):
        px = lax.rem(lax.rem(me, 4) + lax.rem(d, 4), 4)
        py = lax.rem(me // 4 + d // 4, 4)
        return py * 4 + px

    @pl.loop(1, PEERS)
    def _(d):
        pl.semaphore_signal(barrier, inc=1, device_id={"head": peer_of(d)}, device_id_type=MESH)

    pl.semaphore_signal(barrier, inc=1, device_id={"seq": after}, device_id_type=MESH)
    pl.semaphore_signal(barrier, inc=1, device_id={"seq": before}, device_id_type=MESH)

    def block(i):
        return pl.ds(pl.multiple_of(i * CAP, CAP), CAP)

    def fwd_copy(a, d):
        peer = peer_of(d)
        return pltpu.make_async_remote_copy(
            src_ref=fsend.at[a, block(peer)],
            dst_ref=frecv.at[a, block(me)],
            send_sem=f_ssem.at[a, d],
            recv_sem=f_rsem.at[a, d],
            device_id={"head": peer},
            device_id_type=MESH,
        )

    def ret_copy(a, d):
        peer = peer_of(d)
        return pltpu.make_async_remote_copy(
            src_ref=rsend.at[a, block(peer)],
            dst_ref=rrecv.at[a, block(me)],
            send_sem=r_ssem.at[a, d],
            recv_sem=r_rsem.at[a, d],
            device_id={"head": peer},
            device_id_type=MESH,
        )

    def last_copy(d):
        peer = peer_of(d)
        return pltpu.make_async_remote_copy(
            src_ref=rsend.at[OWN - 1, block(peer)],
            dst_ref=last_out.at[block(d)],
            send_sem=r_ssem.at[OWN - 1, d],
            recv_sem=r_rsem.at[OWN - 1, d],
            device_id={"head": peer},
            device_id_type=MESH,
        )

    def doc_rows(i):
        return pl.ds(pl.multiple_of(i * 16, 16), 16)

    def doc_copy(d):
        peer = peer_of(d)
        return pltpu.make_async_remote_copy(
            src_ref=doc_send.at[doc_rows(peer)],
            dst_ref=doc_recv.at[doc_rows(me)],
            send_sem=doc_ssem.at[d],
            recv_sem=doc_rsem.at[d],
            device_id={"head": peer},
            device_id_type=MESH,
        )

    doc_shift = pltpu.make_async_remote_copy(
        src_ref=doc_recv,
        dst_ref=doc_prev,
        send_sem=dp_sem.at[0],
        recv_sem=dp_sem.at[1],
        device_id={"seq": after},
        device_id_type=MESH,
    )

    def kv_copy(a):
        return pltpu.make_async_remote_copy(
            src_ref=frecv.at[a, :, pl.ds(HS, 2 * HS)],
            dst_ref=kv_prev.at[a],
            send_sem=kv_ssem.at[a],
            recv_sem=kv_rsem.at[a],
            device_id={"seq": after},
            device_id_type=MESH,
        )

    def d_copy(a):
        return pltpu.make_async_remote_copy(
            src_ref=dsend.at[a],
            dst_ref=drecv.at[a],
            send_sem=d_ssem.at[a],
            recv_sem=d_rsem.at[a],
            device_id={"seq": before},
            device_id_type=MESH,
        )

    gate = 1.0 / (1.0 + jnp.exp(-logits_ref[...]))
    pieces = thirds(gate)
    fields = jnp.concatenate(
        [heads_ref[...].astype(F32), slots_ref[...].astype(F32)] + pieces, axis=0
    ).astype(BF16)
    count = fields.shape[0]

    for c in range(routes // 256):
        rows = pl.ds(c * 256, 256)
        mixed = dot_nt(token_rows(c, tokens), fields)
        r = lax.broadcasted_iota(jnp.int32, (256, count), 0)
        f = lax.broadcasted_iota(jnp.int32, (256, count), 1)
        mixed = jnp.where((r & 7) == (f & 7), mixed, 0.0).astype(BF16)
        f = lax.broadcasted_iota(jnp.int32, (count, 128), 0)
        dest_ref[rows, :] = dot(mixed, dest_weight(f))
        gate_ref[rows, :] = dot(mixed, one_hot(f >= 16))
        f = lax.broadcasted_iota(jnp.int32, (8, count), 1)
        want = lax.broadcasted_iota(jnp.int32, (8, count), 0)
        as_head = (want == 1) & (f < 8)
        as_slot = (want == 2) & (f >= 8) & (f < 16)
        weight = jnp.where(want == 0, dest_weight(f).astype(F32), jnp.where(as_head | as_slot, 1.0, 0.0))
        rows_ref[:, rows] = dot_nt(weight.astype(BF16), mixed)

    cot_in.wait()
    for c in range(routes // 256):
        rows = pl.ds(c * 256, 256)
        x_grad[rows, :] = (x_cot[rows, :].astype(F32) * gate_ref[rows, :]).astype(BF16)

    proj_in.wait()

    def dispatch(a, c):
        first = pl.multiple_of(lax.rem(me // 4 + c, 4) * (4 * CAP), 4 * CAP)
        rows = pl.ds(first, 4 * CAP)
        r = lax.broadcasted_iota(jnp.int32, (4 * CAP, 128), 0) + first
        source = div48(r)
        ids = (source * (OWN * CAP) + (r - source * CAP) + a * CAP).astype(F32)
        hot = one_hot(jnp.concatenate([ids] * tiles, axis=1) == rows_ref[0:1, :])
        fsend[a, rows, : 3 * HS] = dot(hot, x_proj[...]).astype(BF16)
        fsend[a, rows, 3 * HS :] = dot(hot, x_grad[...]).astype(BF16)

    def ship(a, c):
        @pl.when(c == 0)
        def _():
            frecv[a, block(me), :] = fsend[a, block(me), :]

        @pl.loop(0, 4)
        def _(x):
            @pl.when(c * 4 + x > 0)
            def _():
                fwd_copy(a, c * 4 + x).start()

    dispatch(0, 0)
    pl.semaphore_wait(barrier, PEERS + 1)
    ship(0, 0)

    @pl.loop(1, 4)
    def _(n):
        dispatch(0, n)
        ship(0, n)

    lane_route = lax.broadcasted_iota(jnp.int32, (8, routes), 1)
    position = (lane_route >> 3) + (here * PEERS + me) * tokens
    docs = jnp.ones((8, routes), F32)
    lengths_in.wait()
    end = lengths_ref[0]
    for n in range(lengths_ref.shape[0]):
        docs = docs + jnp.where(position >= end, 1.0, 0.0)
        if n + 1 < lengths_ref.shape[0]:
            end = end + lengths_ref[n + 1]
    row = lax.broadcasted_iota(jnp.int32, (256, 128), 0)
    row_head = (4 * (row >> 4) + (row & 3)).astype(F32)
    at_head = jnp.concatenate([row_head] * tiles, axis=1) == rows_ref[1:2, :]
    docs_wide = jnp.where(at_head, docs[0:1, :], 0.0).astype(BF16)
    lane_slot = lax.broadcasted_iota(jnp.int32, (128, 128), 0).astype(F32)
    at_slot = one_hot(jnp.concatenate([lane_slot] * tiles, axis=1) == rows_ref[2:3, :])
    doc_send[...] = dot_nt(docs_wide, at_slot).astype(BF16)
    doc_recv[doc_rows(me), :] = doc_send[doc_rows(me), :]

    @pl.loop(1, PEERS)
    def _(d):
        doc_copy(d).start()

    def take_head(a):
        @pl.loop(1, PEERS)
        def _(d):
            fwd_copy(a, d).wait_recv()

        kv_copy(a).start()

    @pl.loop(4, 4 * OWN)
    def _(n):
        @pl.when(n == 4 * OWN - 4)
        def _():
            @pl.loop(1, PEERS)
            def _(d):
                doc_copy(d).wait_recv()

            doc_shift.start()
            take_head(0)

        dispatch(n >> 2, n & 3)
        ship(n >> 2, n & 3)

    def head_docs(a, docs_ref):
        r = lax.broadcasted_iota(jnp.int32, (SPAN, 128), 0)
        lane = lax.broadcasted_iota(jnp.int32, (SPAN, 128), 1)
        source = div48(r)
        wanted = source * 16 + a
        pick = one_hot(jnp.concatenate([lane, lane + 128], axis=1) == jnp.concatenate([wanted] * 2, axis=1))
        spread = dot(pick, docs_ref[...])
        return jnp.where(lane == r - source * CAP, spread, 0.0).astype(BF16)

    def attention(a):
        k_all[:SPAN, :] = kv_prev[a, :, :HS]
        v_all[:SPAN, :] = kv_prev[a, :, HS:]
        k_all[SPAN:, :] = frecv[a, :, HS : 2 * HS]
        v_all[SPAN:, :] = frecv[a, :, 2 * HS : 3 * HS]
        k_t[...] = k_all[...].T
        v_t[...] = v_all[...].T
        ones = jnp.ones((HS, HS), BF16)
        mine = head_docs(a, doc_recv)
        key_docs[:SPAN, :] = dot(head_docs(a, doc_prev), ones)
        key_docs[SPAN:, :] = dot(mine, ones)
        query_docs[...] = dot_nt(ones[:8], mine)
        dk_acc[a] = jnp.zeros((2 * SPAN, HS), F32)
        dv_acc[a] = jnp.zeros((2 * SPAN, HS), F32)

        @pl.loop(0, SPAN // QT)
        def _(i):
            first = pl.multiple_of(i * QT, QT)
            start = pl.multiple_of(((i * (i + 1)) >> 1) * 128, 128)
            q = frecv[a, pl.ds(first, QT), :HS]
            out_grad = frecv[a, pl.ds(first, QT), 3 * HS :]
            q_docs = query_docs[0:1, pl.ds(first, QT)]
            top = jnp.full((1, QT), MASKED, F32)
            for c in range(WIN // KC):
                keys = pl.ds(pl.multiple_of(start + c * KC, 128), KC)
                s = dot_nt(k_all[keys, :], q) * (scaling * math.log2(math.e))
                docs = key_docs[keys, :]
                seen = jnp.concatenate([docs, docs], axis=1) == q_docs
                if (c + 1) * KC > SPAN:
                    k_at = lax.broadcasted_iota(jnp.int32, (KC, QT), 0) + (start + c * KC - SPAN)
                    q_at = lax.broadcasted_iota(jnp.int32, (KC, QT), 1) + first
                    seen = seen & (k_at <= q_at)
                s = jnp.where(seen, s, MASKED)
                s_buf[c * KC : (c + 1) * KC, :] = s
                top = jnp.maximum(top, jnp.max(s, axis=0, keepdims=True))
            total = jnp.zeros((1, QT), F32)
            for c in range(WIN // KC):
                part = slice(c * KC, (c + 1) * KC)
                p = jnp.exp2(s_buf[part, :] - top)
                total = total + jnp.sum(p, axis=0, keepdims=True)
                s_buf[part, :] = p
                p_buf[part, :] = p.astype(BF16)
            inverse = 1.0 / total
            window = pl.ds(start, WIN)
            attended = (dot(v_t[:, window], p_buf[...]) * inverse).astype(BF16)
            out_grad_t = (out_grad.astype(F32).T * inverse).astype(BF16)
            delta = jnp.sum(out_grad_t.astype(F32) * attended.astype(F32), axis=0, keepdims=True)
            for c in range(WIN // KC):
                part = slice(c * KC, (c + 1) * KC)
                keys = pl.ds(pl.multiple_of(start + c * KC, 128), KC)
                dp = dot(v_all[keys, :], out_grad_t)
                ds = (s_buf[part, :] * (dp - delta)).astype(BF16)
                ds_buf[part, :] = ds
                dv_acc[a, keys, :] += dot_nt(p_buf[part, :], out_grad_t)
                dk_acc[a, keys, :] += dot(ds, q)
            dq = dot(k_t[:, window], ds_buf[...]) * scaling
            rsend[a, pl.ds(first, QT), :HS] = attended.astype(F32).T.astype(BF16)
            rsend[a, pl.ds(first, QT), HS : 2 * HS] = dq.T.astype(BF16)

        dsend[a, :, :HS] = (dk_acc[a, :SPAN, :] * scaling).astype(BF16)
        dsend[a, :, HS:] = dv_acc[a, :SPAN, :].astype(BF16)
        d_copy(a).start()

    def finish(a):
        d_copy(a).wait_recv()
        dk = dk_acc[a, SPAN:, :] * scaling + drecv[a, :, :HS].astype(F32)
        dv = dv_acc[a, SPAN:, :] + drecv[a, :, HS:].astype(F32)
        rsend[a, :, 2 * HS : 3 * HS] = dk.astype(BF16)
        rsend[a, :, 3 * HS :] = dv.astype(BF16)

    doc_shift.wait_recv()

    @pl.loop(0, OWN)
    def _(a):
        @pl.when(a < OWN - 1)
        def _():
            take_head(a + 1)

        kv_copy(a).wait_recv()
        attention(a)

        @pl.when(a > 0)
        def _():
            finish(a - 1)

            @pl.loop(1, PEERS)
            def _(d):
                ret_copy(a - 1, d).start()

            rrecv[a - 1, block(me), :] = rsend[a - 1, block(me), :]

    finish(OWN - 1)

    @pl.loop(1, PEERS)
    def _(d):
        last_copy(d).start()

    last_out[:CAP, :] = rsend[OWN - 1, block(me), :]

    @pl.loop(0, OWN - 1)
    def _(a):
        @pl.loop(1, PEERS)
        def _(d):
            ret_copy(a, d).wait_recv()

        @pl.loop(0, routes // 256)
        def _(c):
            rows = pl.ds(pl.multiple_of(c * 256, 256), 256)
            more = dot(chosen(dest_ref[rows, :], head_slots(a)), rrecv[a])

            @pl.when(a == 0)
            def _():
                out_acc[rows, :] = more.astype(BF16)

            @pl.when(a > 0)
            def _():
                out_acc[rows, :] = (out_acc[rows, :].astype(F32) + more).astype(BF16)

    @pl.loop(1, READY)
    def _(d):
        last_copy(d).wait_recv()

    early = last_slots(me, 0, EARLY)

    @pl.loop(0, routes // 256)
    def _(c):
        rows = pl.ds(pl.multiple_of(c * 256, 256), 256)
        more = dot(chosen(dest_ref[rows, :], early), last_out[:EARLY, :])
        out_acc[rows, :] = (out_acc[rows, :].astype(F32) + more).astype(BF16)

    @pl.loop(1, PEERS)
    def _(d):
        doc_copy(d).wait_send()

    doc_shift.wait_send()

    @pl.loop(0, OWN)
    def _(a):
        @pl.loop(1, PEERS)
        def _(d):
            fwd_copy(a, d).wait_send()

        kv_copy(a).wait_send()
        d_copy(a).wait_send()

    @pl.loop(0, OWN - 1)
    def _(a):
        @pl.loop(1, PEERS)
        def _(d):
            ret_copy(a, d).wait_send()

    @pl.loop(1, PEERS)
    def _(d):
        last_copy(d).wait_send()

    @pl.loop(READY, PEERS)
    def _(d):
        last_copy(d).wait_recv()


def home_kernel(
    routes_ref,
    last_ref,
    dest_ref,
    gate_ref,
    cot_ref,
    logits_ref,
    head_out_hbm,
    proj_out_hbm,
    grad_out,
    out_head,
    out_proj,
    out_sem,
):
    tokens = logits_ref.shape[1]
    late = last_slots(lax.axis_index("head"), EARLY, SPAN - EARLY)
    lane = lax.broadcasted_iota(jnp.int32, (8, HS), 1)
    eye = one_hot(lax.broadcasted_iota(jnp.int32, (8, HS), 0) == lane)
    grads = jnp.zeros((8, tokens), F32)
    copies = []
    for c in range(routes_ref.shape[0] // 256):
        rows = pl.ds(c * 256, 256)
        more = dot(chosen(dest_ref[rows, :], late), last_ref[EARLY:, :])
        full = routes_ref[rows, :].astype(F32) + more
        out_proj[rows, :] = full[:, HS:].astype(BF16)
        attended = full[:, :HS]
        out_head[rows, :] = (attended * gate_ref[rows, :]).astype(BF16)
        for n, (source, target) in enumerate(((out_head, head_out_hbm), (out_proj, proj_out_hbm))):
            copies.append(pltpu.make_async_copy(source.at[rows], target.at[rows], out_sem.at[c, n]))
            copies[-1].start()
        inner = jnp.sum(cot_ref[rows, :].astype(F32) * attended, axis=1, keepdims=True)
        r = lax.broadcasted_iota(jnp.int32, (256, HS), 0)
        lane = lax.broadcasted_iota(jnp.int32, (256, HS), 1)
        dots = jnp.where((r & 7) == lane, inner, 0.0)
        by_route = sum(dot_nt(eye, part.astype(BF16)) for part in thirds(dots))
        hot = token_rows(c, tokens)
        grads = grads + sum(dot(part.astype(BF16), hot) for part in thirds(by_route))
    gate = 1.0 / (1.0 + jnp.exp(-logits_ref[...]))
    grad_out[...] = grads * gate * (1.0 - gate)
    for copy in copies:
        copy.wait()


def per_device(projections, routed_heads, slot_index, gate_logits, doc_lengths, cotangent):
    tokens, top, width = projections.shape
    routes = tokens * top
    dma = pltpu.SemaphoreType.DMA
    vmem = pltpu.VMEM
    whole = pl.BlockSpec(memory_space=pltpu.VMEM)
    hbm = pl.BlockSpec(memory_space=pltpu.HBM)
    cot_rows = cotangent.reshape(routes, HS)
    logits = gate_logits.T
    handed = pl.pallas_call(
        kernel,
        out_shape=(
            jax.ShapeDtypeStruct((routes, WIDE), BF16),
            jax.ShapeDtypeStruct((SPAN, WIDE), BF16),
            jax.ShapeDtypeStruct((routes, HS), F32),
            jax.ShapeDtypeStruct((routes, HS), F32),
        ),
        in_specs=[hbm, hbm, whole, whole, whole, hbm],
        out_specs=(whole, whole, whole, whole),
        scratch_shapes=[
            pltpu.SMEM(doc_lengths.shape, jnp.int32),
            vmem((routes, 3 * HS), BF16),
            vmem((routes, HS), BF16),
            vmem((routes, HS), BF16),
            vmem((8, routes), F32),
            vmem((OWN, SPAN, WIDE), BF16),
            vmem((OWN, SPAN, WIDE), BF16),
            vmem((PEERS * 16, 128), BF16),
            vmem((PEERS * 16, 128), BF16),
            vmem((PEERS * 16, 128), BF16),
            vmem((OWN, SPAN, 2 * HS), BF16),
            vmem((OWN, SPAN, 2 * HS), BF16),
            vmem((OWN, SPAN, 2 * HS), BF16),
            vmem((OWN, SPAN, WIDE), BF16),
            vmem((OWN, SPAN, WIDE), BF16),
            vmem((2 * SPAN, HS), BF16),
            vmem((2 * SPAN, HS), BF16),
            vmem((HS, 2 * SPAN), BF16),
            vmem((HS, 2 * SPAN), BF16),
            vmem((2 * SPAN, HS), F32),
            vmem((8, SPAN), F32),
            vmem((WIN, QT), F32),
            vmem((WIN, QT), BF16),
            vmem((WIN, QT), BF16),
            vmem((OWN, 2 * SPAN, HS), F32),
            vmem((OWN, 2 * SPAN, HS), F32),
            dma((OWN, PEERS)),
            dma((OWN, PEERS)),
            dma((PEERS,)),
            dma((PEERS,)),
            dma((2,)),
            dma((OWN,)),
            dma((OWN,)),
            dma((OWN,)),
            dma((OWN,)),
            dma((OWN, PEERS)),
            dma((OWN, PEERS)),
            dma((3,)),
        ],
        compiler_params=pltpu.CompilerParams(
            collective_id=0, has_side_effects=True, vmem_limit_bytes=44000 * 1024
        ),
    )(
        *(
            pltpu.with_memory_space_constraint(v, pltpu.HBM)
            for v in (
                projections.reshape(routes, width),
                cot_rows,
                routed_heads.T,
                slot_index.T,
                logits,
                doc_lengths,
            )
        ),
    )
    head_outputs, projection_grads, gate_grads = pl.pallas_call(
        home_kernel,
        out_shape=(
            jax.ShapeDtypeStruct((routes, HS), BF16),
            jax.ShapeDtypeStruct((routes, 3 * HS), BF16),
            jax.ShapeDtypeStruct((top, tokens), F32),
        ),
        in_specs=[whole] * 6,
        out_specs=(hbm, hbm, whole),
        scratch_shapes=[
            vmem((routes, HS), BF16),
            vmem((routes, 3 * HS), BF16),
            dma((routes // 256, 2)),
        ],
        compiler_params=pltpu.CompilerParams(vmem_limit_bytes=16000 * 1024),
    )(*handed, cot_rows, logits)
    return (
        head_outputs.reshape(tokens, top, HS),
        projection_grads.reshape(tokens, top, width),
        gate_grads.T,
    )


def solution(mesh):
    tokens = P(("seq", "head"), None, None)
    routes = P(("seq", "head"), None)
    return jax.shard_map(
        per_device,
        mesh=mesh,
        in_specs=(tokens, routes, routes, routes, P(), tokens),
        out_specs=(tokens, tokens, routes),
        check_vma=False,
    )
```

```python
import math

import jax
import jax.numpy as jnp
from jax import lax
from jax.experimental import pallas as pl
from jax.experimental.pallas import tpu as pltpu
from jax.sharding import PartitionSpec as P

H = 64
CAP = 48
OWN = 4
PEERS = 16
SPAN = PEERS * CAP
HS = 128
WIDE = 4 * HS
QT = 256
WIN = 1152
KC = 384
MASKED = -1e30
F32 = jnp.float32
BF16 = jnp.bfloat16
MESH = pl.DeviceIdType.MESH


def dot_nt(a, b):
    return lax.dot_general(a, b, (((1,), (1,)), ((), ())), preferred_element_type=F32)


def dot(a, b):
    return jnp.dot(a, b, preferred_element_type=F32)


def one_hot(mask):
    return jnp.where(mask, 1.0, 0.0).astype(BF16)


def thirds(v):
    high = v.astype(BF16).astype(F32)
    middle = (v - high).astype(BF16).astype(F32)
    return [high, middle, v - high - middle]


def dest_weight(f):
    return jnp.where(f < 8, float(CAP), jnp.where(f < 16, 1.0, 0.0)).astype(BF16)


def div48(v):
    return (v * 1366) >> 16


def token_rows(c, tokens):
    r = lax.broadcasted_iota(jnp.int32, (256, tokens), 0)
    t = lax.broadcasted_iota(jnp.int32, (256, tokens), 1)
    return one_hot((r >> 3) + c * 32 == t)


def head_slots(a):
    lane = lax.broadcasted_iota(jnp.int32, (8, SPAN), 1)
    source = div48(lane)
    return (source * (OWN * CAP) + (lane - source * CAP) + a * CAP).astype(F32)


def chosen(dest, ids):
    return one_hot(jnp.concatenate([dest] * (ids.shape[1] // 128), axis=1) == ids[0:1, :])


def kernel(
    proj_hbm,
    cot_hbm,
    heads_ref,
    slots_ref,
    logits_ref,
    lengths_hbm,
    out_acc,
    rrecv,
    dest_ref,
    gate_ref,
    lengths_ref,
    x_proj,
    x_cot,
    x_grad,
    rows_ref,
    fsend,
    frecv,
    doc_send,
    doc_recv,
    doc_prev,
    kv_prev,
    dsend,
    drecv,
    rsend,
    k_all,
    v_all,
    k_t,
    v_t,
    key_docs,
    query_docs,
    s_buf,
    p_buf,
    ds_buf,
    dk_acc,
    dv_acc,
    f_ssem,
    f_rsem,
    doc_ssem,
    doc_rsem,
    dp_sem,
    kv_ssem,
    kv_rsem,
    d_ssem,
    d_rsem,
    r_ssem,
    r_rsem,
    in_sem,
):
    me = lax.axis_index("head")
    here = lax.axis_index("seq")
    after = lax.rem(here + 1, PEERS)
    before = lax.rem(here + PEERS - 1, PEERS)
    routes = proj_hbm.shape[0]
    tokens = heads_ref.shape[1]
    tiles = routes // 128
    scaling = HS ** (-0.5)
    proj_in = pltpu.make_async_copy(proj_hbm, x_proj, in_sem.at[0])
    cot_in = pltpu.make_async_copy(cot_hbm, x_cot, in_sem.at[1])
    lengths_in = pltpu.make_async_copy(lengths_hbm, lengths_ref, in_sem.at[2])
    cot_in.start()
    proj_in.start()
    lengths_in.start()

    barrier = pltpu.get_barrier_semaphore()

    def peer_of(d):
        px = lax.rem(lax.rem(me, 4) + lax.rem(d, 4), 4)
        py = lax.rem(me // 4 + d // 4, 4)
        return py * 4 + px

    @pl.loop(1, PEERS)
    def _(d):
        pl.semaphore_signal(barrier, inc=1, device_id={"head": peer_of(d)}, device_id_type=MESH)

    pl.semaphore_signal(barrier, inc=1, device_id={"seq": after}, device_id_type=MESH)
    pl.semaphore_signal(barrier, inc=1, device_id={"seq": before}, device_id_type=MESH)

    def block(i):
        return pl.ds(pl.multiple_of(i * CAP, CAP), CAP)

    def fwd_copy(a, d):
        peer = peer_of(d)
        return pltpu.make_async_remote_copy(
            src_ref=fsend.at[a, block(peer)],
            dst_ref=frecv.at[a, block(me)],
            send_sem=f_ssem.at[a, d],
            recv_sem=f_rsem.at[a, d],
            device_id={"head": peer},
            device_id_type=MESH,
        )

    def ret_copy(a, half, d):
        peer = peer_of(d)
        return pltpu.make_async_remote_copy(
            src_ref=rsend.at[a, half, block(peer)],
            dst_ref=rrecv.at[a, half, block(me)],
            send_sem=r_ssem.at[a, half, d],
            recv_sem=r_rsem.at[a, half, d],
            device_id={"head": peer},
            device_id_type=MESH,
        )

    def send_home(a, half):
        @pl.loop(1, PEERS)
        def _(d):
            ret_copy(a, half, d).start()

        rrecv[a, half, block(me), :] = rsend[a, half, block(me), :]

    def doc_rows(i):
        return pl.ds(pl.multiple_of(i * 16, 16), 16)

    def doc_copy(d):
        peer = peer_of(d)
        return pltpu.make_async_remote_copy(
            src_ref=doc_send.at[doc_rows(peer)],
            dst_ref=doc_recv.at[doc_rows(me)],
            send_sem=doc_ssem.at[d],
            recv_sem=doc_rsem.at[d],
            device_id={"head": peer},
            device_id_type=MESH,
        )

    doc_shift = pltpu.make_async_remote_copy(
        src_ref=doc_recv,
        dst_ref=doc_prev,
        send_sem=dp_sem.at[0],
        recv_sem=dp_sem.at[1],
        device_id={"seq": after},
        device_id_type=MESH,
    )

    def kv_copy(a):
        return pltpu.make_async_remote_copy(
            src_ref=frecv.at[a, :, pl.ds(HS, 2 * HS)],
            dst_ref=kv_prev.at[a],
            send_sem=kv_ssem.at[a],
            recv_sem=kv_rsem.at[a],
            device_id={"seq": after},
            device_id_type=MESH,
        )

    def d_copy(a):
        return pltpu.make_async_remote_copy(
            src_ref=dsend.at[a],
            dst_ref=drecv.at[a],
            send_sem=d_ssem.at[a],
            recv_sem=d_rsem.at[a],
            device_id={"seq": before},
            device_id_type=MESH,
        )

    gate = 1.0 / (1.0 + jnp.exp(-logits_ref[...]))
    pieces = thirds(gate)
    fields = jnp.concatenate(
        [heads_ref[...].astype(F32), slots_ref[...].astype(F32)] + pieces, axis=0
    ).astype(BF16)
    count = fields.shape[0]

    for c in range(routes // 256):
        rows = pl.ds(c * 256, 256)
        mixed = dot_nt(token_rows(c, tokens), fields)
        r = lax.broadcasted_iota(jnp.int32, (256, count), 0)
        f = lax.broadcasted_iota(jnp.int32, (256, count), 1)
        mixed = jnp.where((r & 7) == (f & 7), mixed, 0.0).astype(BF16)
        f = lax.broadcasted_iota(jnp.int32, (count, 128), 0)
        dest_ref[rows, :] = dot(mixed, dest_weight(f))
        gate_ref[rows, :] = dot(mixed, one_hot(f >= 16))
        f = lax.broadcasted_iota(jnp.int32, (8, count), 1)
        want = lax.broadcasted_iota(jnp.int32, (8, count), 0)
        as_head = (want == 1) & (f < 8)
        as_slot = (want == 2) & (f >= 8) & (f < 16)
        weight = jnp.where(want == 0, dest_weight(f).astype(F32), jnp.where(as_head | as_slot, 1.0, 0.0))
        rows_ref[:, rows] = dot_nt(weight.astype(BF16), mixed)

    cot_in.wait()
    for c in range(routes // 256):
        rows = pl.ds(c * 256, 256)
        x_grad[rows, :] = (x_cot[rows, :].astype(F32) * gate_ref[rows, :]).astype(BF16)

    proj_in.wait()

    def dispatch(a, c):
        first = pl.multiple_of(lax.rem(me // 4 + c, 4) * (4 * CAP), 4 * CAP)
        rows = pl.ds(first, 4 * CAP)
        r = lax.broadcasted_iota(jnp.int32, (4 * CAP, 128), 0) + first
        source = div48(r)
        ids = (source * (OWN * CAP) + (r - source * CAP) + a * CAP).astype(F32)
        hot = one_hot(jnp.concatenate([ids] * tiles, axis=1) == rows_ref[0:1, :])
        fsend[a, rows, : 3 * HS] = dot(hot, x_proj[...]).astype(BF16)
        fsend[a, rows, 3 * HS :] = dot(hot, x_grad[...]).astype(BF16)

    def ship(a, c):
        @pl.when(c == 0)
        def _():
            frecv[a, block(me), :] = fsend[a, block(me), :]

        @pl.loop(0, 4)
        def _(x):
            @pl.when(c * 4 + x > 0)
            def _():
                fwd_copy(a, c * 4 + x).start()

    dispatch(0, 0)
    pl.semaphore_wait(barrier, PEERS + 1)
    ship(0, 0)

    @pl.loop(1, 4)
    def _(n):
        dispatch(0, n)
        ship(0, n)

    lane_route = lax.broadcasted_iota(jnp.int32, (8, routes), 1)
    position = (lane_route >> 3) + (here * PEERS + me) * tokens
    docs = jnp.ones((8, routes), F32)
    lengths_in.wait()
    end = lengths_ref[0]
    for n in range(lengths_ref.shape[0]):
        docs = docs + jnp.where(position >= end, 1.0, 0.0)
        if n + 1 < lengths_ref.shape[0]:
            end = end + lengths_ref[n + 1]
    row = lax.broadcasted_iota(jnp.int32, (256, 128), 0)
    row_head = (4 * (row >> 4) + (row & 3)).astype(F32)
    at_head = jnp.concatenate([row_head] * tiles, axis=1) == rows_ref[1:2, :]
    docs_wide = jnp.where(at_head, docs[0:1, :], 0.0).astype(BF16)
    lane_slot = lax.broadcasted_iota(jnp.int32, (128, 128), 0).astype(F32)
    at_slot = one_hot(jnp.concatenate([lane_slot] * tiles, axis=1) == rows_ref[2:3, :])
    doc_send[...] = dot_nt(docs_wide, at_slot).astype(BF16)
    doc_recv[doc_rows(me), :] = doc_send[doc_rows(me), :]

    @pl.loop(1, PEERS)
    def _(d):
        doc_copy(d).start()

    def take_head(a):
        @pl.loop(1, PEERS)
        def _(d):
            fwd_copy(a, d).wait_recv()

        kv_copy(a).start()

    @pl.loop(4, 4 * OWN)
    def _(n):
        dispatch(n >> 2, n & 3)
        ship(n >> 2, n & 3)

    @pl.loop(1, PEERS)
    def _(d):
        doc_copy(d).wait_recv()

    doc_shift.start()
    take_head(0)

    def head_docs(a, docs_ref):
        r = lax.broadcasted_iota(jnp.int32, (SPAN, 128), 0)
        lane = lax.broadcasted_iota(jnp.int32, (SPAN, 128), 1)
        source = div48(r)
        wanted = source * 16 + a
        pick = one_hot(jnp.concatenate([lane, lane + 128], axis=1) == jnp.concatenate([wanted] * 2, axis=1))
        spread = dot(pick, docs_ref[...])
        return jnp.where(lane == r - source * CAP, spread, 0.0).astype(BF16)

    def finish(a):
        d_copy(a).wait_recv()
        dk = dk_acc[a, SPAN:, :] * scaling + drecv[a, :, :HS].astype(F32)
        dv = dv_acc[a, SPAN:, :] + drecv[a, :, HS:].astype(F32)
        rsend[a, 1, :, :HS] = dk.astype(BF16)
        rsend[a, 1, :, HS:] = dv.astype(BF16)
        send_home(a, 1)

    def attention(a):
        k_all[:SPAN, :] = kv_prev[a, :, :HS]
        v_all[:SPAN, :] = kv_prev[a, :, HS:]
        k_all[SPAN:, :] = frecv[a, :, HS : 2 * HS]
        v_all[SPAN:, :] = frecv[a, :, 2 * HS : 3 * HS]
        k_t[...] = k_all[...].T
        v_t[...] = v_all[...].T
        ones = jnp.ones((HS, HS), BF16)
        mine = head_docs(a, doc_recv)
        key_docs[:SPAN, :] = dot(head_docs(a, doc_prev), ones)
        key_docs[SPAN:, :] = dot(mine, ones)
        query_docs[...] = dot_nt(ones[:8], mine)
        dk_acc[a] = jnp.zeros((2 * SPAN, HS), F32)
        dv_acc[a] = jnp.zeros((2 * SPAN, HS), F32)

        @pl.loop(0, SPAN // QT)
        def _(i):
            @pl.when((i == 1) & (a < OWN - 1))
            def _():
                take_head(a + 1)

            @pl.when((i == 2) & (a > 0))
            def _():
                finish(a - 1)

            first = pl.multiple_of(i * QT, QT)
            start = pl.multiple_of(((i * (i + 1)) >> 1) * 128, 128)
            q = frecv[a, pl.ds(first, QT), :HS]
            out_grad = frecv[a, pl.ds(first, QT), 3 * HS :]
            q_docs = query_docs[0:1, pl.ds(first, QT)]
            top = jnp.full((1, QT), MASKED, F32)
            for c in range(WIN // KC):
                keys = pl.ds(pl.multiple_of(start + c * KC, 128), KC)
                s = dot_nt(k_all[keys, :], q) * (scaling * math.log2(math.e))
                docs = key_docs[keys, :]
                seen = jnp.concatenate([docs, docs], axis=1) == q_docs
                if (c + 1) * KC > SPAN:
                    k_at = lax.broadcasted_iota(jnp.int32, (KC, QT), 0) + (start + c * KC - SPAN)
                    q_at = lax.broadcasted_iota(jnp.int32, (KC, QT), 1) + first
                    seen = seen & (k_at <= q_at)
                s = jnp.where(seen, s, MASKED)
                s_buf[c * KC : (c + 1) * KC, :] = s
                top = jnp.maximum(top, jnp.max(s, axis=0, keepdims=True))
            total = jnp.zeros((1, QT), F32)
            for c in range(WIN // KC):
                part = slice(c * KC, (c + 1) * KC)
                p = jnp.exp2(s_buf[part, :] - top)
                total = total + jnp.sum(p, axis=0, keepdims=True)
                s_buf[part, :] = p
                p_buf[part, :] = p.astype(BF16)
            inverse = 1.0 / total
            window = pl.ds(start, WIN)
            attended = (dot(v_t[:, window], p_buf[...]) * inverse).astype(BF16)
            out_grad_t = (out_grad.astype(F32).T * inverse).astype(BF16)
            delta = jnp.sum(out_grad_t.astype(F32) * attended.astype(F32), axis=0, keepdims=True)
            for c in range(WIN // KC):
                part = slice(c * KC, (c + 1) * KC)
                keys = pl.ds(pl.multiple_of(start + c * KC, 128), KC)
                dp = dot(v_all[keys, :], out_grad_t)
                ds = (s_buf[part, :] * (dp - delta)).astype(BF16)
                ds_buf[part, :] = ds
                dv_acc[a, keys, :] += dot_nt(p_buf[part, :], out_grad_t)
                dk_acc[a, keys, :] += dot(ds, q)
            dq = dot(k_t[:, window], ds_buf[...]) * scaling
            rsend[a, 0, pl.ds(first, QT), :HS] = attended.astype(F32).T.astype(BF16)
            rsend[a, 0, pl.ds(first, QT), HS:] = dq.T.astype(BF16)

        dsend[a, :, :HS] = (dk_acc[a, :SPAN, :] * scaling).astype(BF16)
        dsend[a, :, HS:] = dv_acc[a, :SPAN, :].astype(BF16)
        d_copy(a).start()
        send_home(a, 0)

    doc_shift.wait_recv()

    @pl.loop(0, OWN)
    def _(a):
        kv_copy(a).wait_recv()
        attention(a)

    finish(OWN - 1)

    def await_home(a):
        @pl.loop(1, PEERS)
        def _(d):
            ret_copy(a, 0, d).wait_recv()
            ret_copy(a, 1, d).wait_recv()

    @pl.loop(0, OWN - 1)
    def _(a):
        await_home(a)

        @pl.loop(0, routes // 256)
        def _(c):
            rows = pl.ds(pl.multiple_of(c * 256, 256), 256)
            hot = chosen(dest_ref[rows, :], head_slots(a))
            more = jnp.concatenate([dot(hot, rrecv[a, 0]), dot(hot, rrecv[a, 1])], axis=1)

            @pl.when(a == 0)
            def _():
                out_acc[rows, :] = more.astype(BF16)

            @pl.when(a > 0)
            def _():
                out_acc[rows, :] = (out_acc[rows, :].astype(F32) + more).astype(BF16)

    @pl.loop(1, PEERS)
    def _(d):
        doc_copy(d).wait_send()

    doc_shift.wait_send()

    @pl.loop(0, OWN)
    def _(a):
        @pl.loop(1, PEERS)
        def _(d):
            fwd_copy(a, d).wait_send()

        kv_copy(a).wait_send()
        d_copy(a).wait_send()

    @pl.loop(0, OWN)
    def _(a):
        @pl.loop(1, PEERS)
        def _(d):
            ret_copy(a, 0, d).wait_send()
            ret_copy(a, 1, d).wait_send()

    await_home(OWN - 1)


def home_kernel(
    routes_ref,
    last_ref,
    dest_ref,
    gate_ref,
    cot_ref,
    logits_ref,
    head_out_hbm,
    proj_out_hbm,
    grad_out,
    out_head,
    out_proj,
    out_sem,
):
    tokens = logits_ref.shape[1]
    late = head_slots(OWN - 1)
    lane = lax.broadcasted_iota(jnp.int32, (8, HS), 1)
    eye = one_hot(lax.broadcasted_iota(jnp.int32, (8, HS), 0) == lane)
    grads = jnp.zeros((8, tokens), F32)
    copies = []
    for c in range(routes_ref.shape[0] // 256):
        rows = pl.ds(c * 256, 256)
        hot = chosen(dest_ref[rows, :], late)
        full = routes_ref[rows, : 2 * HS].astype(F32) + dot(hot, last_ref[OWN - 1, 0])
        rest = routes_ref[rows, 2 * HS :].astype(F32) + dot(hot, last_ref[OWN - 1, 1])
        out_proj[rows, :HS] = full[:, HS:].astype(BF16)
        out_proj[rows, HS:] = rest.astype(BF16)
        attended = full[:, :HS]
        out_head[rows, :] = (attended * gate_ref[rows, :]).astype(BF16)
        for n, (source, target) in enumerate(((out_head, head_out_hbm), (out_proj, proj_out_hbm))):
            copies.append(pltpu.make_async_copy(source.at[rows], target.at[rows], out_sem.at[c, n]))
            copies[-1].start()
        inner = jnp.sum(cot_ref[rows, :].astype(F32) * attended, axis=1, keepdims=True)
        r = lax.broadcasted_iota(jnp.int32, (256, HS), 0)
        lane = lax.broadcasted_iota(jnp.int32, (256, HS), 1)
        dots = jnp.where((r & 7) == lane, inner, 0.0)
        by_route = sum(dot_nt(eye, part.astype(BF16)) for part in thirds(dots))
        hot = token_rows(c, tokens)
        grads = grads + sum(dot(part.astype(BF16), hot) for part in thirds(by_route))
    gate = 1.0 / (1.0 + jnp.exp(-logits_ref[...]))
    grad_out[...] = grads * gate * (1.0 - gate)
    for copy in copies:
        copy.wait()


def per_device(projections, routed_heads, slot_index, gate_logits, doc_lengths, cotangent):
    tokens, top, width = projections.shape
    routes = tokens * top
    dma = pltpu.SemaphoreType.DMA
    vmem = pltpu.VMEM
    whole = pl.BlockSpec(memory_space=pltpu.VMEM)
    hbm = pl.BlockSpec(memory_space=pltpu.HBM)
    cot_rows = cotangent.reshape(routes, HS)
    logits = gate_logits.T
    handed = pl.pallas_call(
        kernel,
        out_shape=(
            jax.ShapeDtypeStruct((routes, WIDE), BF16),
            jax.ShapeDtypeStruct((OWN, 2, SPAN, 2 * HS), BF16),
            jax.ShapeDtypeStruct((routes, HS), F32),
            jax.ShapeDtypeStruct((routes, HS), F32),
        ),
        in_specs=[hbm, hbm, whole, whole, whole, hbm],
        out_specs=(whole, whole, whole, whole),
        scratch_shapes=[
            pltpu.SMEM(doc_lengths.shape, jnp.int32),
            vmem((routes, 3 * HS), BF16),
            vmem((routes, HS), BF16),
            vmem((routes, HS), BF16),
            vmem((8, routes), F32),
            vmem((OWN, SPAN, WIDE), BF16),
            vmem((OWN, SPAN, WIDE), BF16),
            vmem((PEERS * 16, 128), BF16),
            vmem((PEERS * 16, 128), BF16),
            vmem((PEERS * 16, 128), BF16),
            vmem((OWN, SPAN, 2 * HS), BF16),
            vmem((OWN, SPAN, 2 * HS), BF16),
            vmem((OWN, SPAN, 2 * HS), BF16),
            vmem((OWN, 2, SPAN, 2 * HS), BF16),
            vmem((2 * SPAN, HS), BF16),
            vmem((2 * SPAN, HS), BF16),
            vmem((HS, 2 * SPAN), BF16),
            vmem((HS, 2 * SPAN), BF16),
            vmem((2 * SPAN, HS), F32),
            vmem((8, SPAN), F32),
            vmem((WIN, QT), F32),
            vmem((WIN, QT), BF16),
            vmem((WIN, QT), BF16),
            vmem((OWN, 2 * SPAN, HS), F32),
            vmem((OWN, 2 * SPAN, HS), F32),
            dma((OWN, PEERS)),
            dma((OWN, PEERS)),
            dma((PEERS,)),
            dma((PEERS,)),
            dma((2,)),
            dma((OWN,)),
            dma((OWN,)),
            dma((OWN,)),
            dma((OWN,)),
            dma((OWN, 2, PEERS)),
            dma((OWN, 2, PEERS)),
            dma((3,)),
        ],
        compiler_params=pltpu.CompilerParams(
            collective_id=0, has_side_effects=True, vmem_limit_bytes=44000 * 1024
        ),
    )(
        *(
            pltpu.with_memory_space_constraint(v, pltpu.HBM)
            for v in (
                projections.reshape(routes, width),
                cot_rows,
                routed_heads.T,
                slot_index.T,
                logits,
                doc_lengths,
            )
        ),
    )
    head_outputs, projection_grads, gate_grads = pl.pallas_call(
        home_kernel,
        out_shape=(
            jax.ShapeDtypeStruct((routes, HS), BF16),
            jax.ShapeDtypeStruct((routes, 3 * HS), BF16),
            jax.ShapeDtypeStruct((top, tokens), F32),
        ),
        in_specs=[whole] * 6,
        out_specs=(hbm, hbm, whole),
        scratch_shapes=[
            vmem((routes, HS), BF16),
            vmem((routes, 3 * HS), BF16),
            dma((routes // 256, 2)),
        ],
        compiler_params=pltpu.CompilerParams(vmem_limit_bytes=16000 * 1024),
    )(*handed, cot_rows, logits)
    return (
        head_outputs.reshape(tokens, top, HS),
        projection_grads.reshape(tokens, top, width),
        gate_grads.T,
    )


def solution(mesh):
    tokens = P(("seq", "head"), None, None)
    routes = P(("seq", "head"), None)
    return jax.shard_map(
        per_device,
        mesh=mesh,
        in_specs=(tokens, routes, routes, routes, P(), tokens),
        out_specs=(tokens, tokens, routes),
        check_vma=False,
    )
```

```python
import math

import jax
import jax.numpy as jnp
from jax import lax
from jax.experimental import pallas as pl
from jax.experimental.pallas import tpu as pltpu
from jax.sharding import PartitionSpec as P

H = 64
CAP = 48
OWN = 4
PEERS = 16
SPAN = PEERS * CAP
HS = 128
WIDE = 4 * HS
QT = 256
WIN = 1152
KC = 384
MASKED = -1e30
F32 = jnp.float32
BF16 = jnp.bfloat16
MESH = pl.DeviceIdType.MESH


def dot_nt(a, b):
    return lax.dot_general(a, b, (((1,), (1,)), ((), ())), preferred_element_type=F32)


def dot(a, b):
    return jnp.dot(a, b, preferred_element_type=F32)


def one_hot(mask):
    return jnp.where(mask, 1.0, 0.0).astype(BF16)


def thirds(v):
    high = v.astype(BF16).astype(F32)
    middle = (v - high).astype(BF16).astype(F32)
    return [high, middle, v - high - middle]


def dest_weight(f):
    return jnp.where(f < 8, float(CAP), jnp.where(f < 16, 1.0, 0.0)).astype(BF16)


def div48(v):
    return (v * 1366) >> 16


def token_rows(c, tokens):
    r = lax.broadcasted_iota(jnp.int32, (256, tokens), 0)
    t = lax.broadcasted_iota(jnp.int32, (256, tokens), 1)
    return one_hot((r >> 3) + c * 32 == t)


def head_slots(a):
    lane = lax.broadcasted_iota(jnp.int32, (8, SPAN), 1)
    source = div48(lane)
    return (source * (OWN * CAP) + (lane - source * CAP) + a * CAP).astype(F32)


def chosen(dest, ids):
    return one_hot(jnp.concatenate([dest] * (ids.shape[1] // 128), axis=1) == ids[0:1, :])


def kernel(
    proj_hbm,
    cot_hbm,
    heads_ref,
    slots_ref,
    logits_ref,
    lengths_hbm,
    out_acc,
    rrecv,
    dest_ref,
    gate_ref,
    lengths_ref,
    x_proj,
    x_cot,
    x_grad,
    rows_ref,
    fsend,
    frecv,
    doc_send,
    doc_recv,
    doc_prev,
    kv_prev,
    dsend,
    drecv,
    rsend,
    k_all,
    v_all,
    k_t,
    v_t,
    key_docs,
    query_docs,
    s_buf,
    p_buf,
    ds_buf,
    dk_acc,
    dv_acc,
    f_ssem,
    f_rsem,
    doc_ssem,
    doc_rsem,
    dp_sem,
    kv_ssem,
    kv_rsem,
    d_ssem,
    d_rsem,
    r_ssem,
    r_rsem,
    in_sem,
):
    me = lax.axis_index("head")
    here = lax.axis_index("seq")
    after = lax.rem(here + 1, PEERS)
    before = lax.rem(here + PEERS - 1, PEERS)
    routes = proj_hbm.shape[0]
    tokens = heads_ref.shape[1]
    tiles = routes // 128
    scaling = HS ** (-0.5)
    proj_in = pltpu.make_async_copy(proj_hbm, x_proj, in_sem.at[0])
    cot_in = pltpu.make_async_copy(cot_hbm, x_cot, in_sem.at[1])
    lengths_in = pltpu.make_async_copy(lengths_hbm, lengths_ref, in_sem.at[2])
    cot_in.start()
    proj_in.start()
    lengths_in.start()

    barrier = pltpu.get_barrier_semaphore()

    def peer_of(d):
        px = lax.rem(lax.rem(me, 4) + lax.rem(d, 4), 4)
        py = lax.rem(me // 4 + d // 4, 4)
        return py * 4 + px

    @pl.loop(1, PEERS)
    def _(d):
        pl.semaphore_signal(barrier, inc=1, device_id={"head": peer_of(d)}, device_id_type=MESH)

    pl.semaphore_signal(barrier, inc=1, device_id={"seq": after}, device_id_type=MESH)
    pl.semaphore_signal(barrier, inc=1, device_id={"seq": before}, device_id_type=MESH)

    def block(i):
        return pl.ds(pl.multiple_of(i * CAP, CAP), CAP)

    def fwd_copy(a, d):
        peer = peer_of(d)
        return pltpu.make_async_remote_copy(
            src_ref=fsend.at[a, block(peer)],
            dst_ref=frecv.at[a, block(me)],
            send_sem=f_ssem.at[a, d],
            recv_sem=f_rsem.at[a, d],
            device_id={"head": peer},
            device_id_type=MESH,
        )

    def ret_copy(a, half, d):
        peer = peer_of(d)
        return pltpu.make_async_remote_copy(
            src_ref=rsend.at[a, half, block(peer)],
            dst_ref=rrecv.at[a, half, block(me)],
            send_sem=r_ssem.at[a, half, d],
            recv_sem=r_rsem.at[a, half, d],
            device_id={"head": peer},
            device_id_type=MESH,
        )

    def send_home(a, half):
        @pl.loop(1, PEERS)
        def _(d):
            ret_copy(a, half, d).start()

        rrecv[a, half, block(me), :] = rsend[a, half, block(me), :]

    def doc_rows(i):
        return pl.ds(pl.multiple_of(i * 16, 16), 16)

    def doc_copy(d):
        peer = peer_of(d)
        return pltpu.make_async_remote_copy(
            src_ref=doc_send.at[doc_rows(peer)],
            dst_ref=doc_recv.at[doc_rows(me)],
            send_sem=doc_ssem.at[d],
            recv_sem=doc_rsem.at[d],
            device_id={"head": peer},
            device_id_type=MESH,
        )

    doc_shift = pltpu.make_async_remote_copy(
        src_ref=doc_recv,
        dst_ref=doc_prev,
        send_sem=dp_sem.at[0],
        recv_sem=dp_sem.at[1],
        device_id={"seq": after},
        device_id_type=MESH,
    )

    def kv_copy(a):
        return pltpu.make_async_remote_copy(
            src_ref=frecv.at[a, :, pl.ds(HS, 2 * HS)],
            dst_ref=kv_prev.at[a],
            send_sem=kv_ssem.at[a],
            recv_sem=kv_rsem.at[a],
            device_id={"seq": after},
            device_id_type=MESH,
        )

    def d_copy(a):
        return pltpu.make_async_remote_copy(
            src_ref=dsend.at[a],
            dst_ref=drecv.at[a],
            send_sem=d_ssem.at[a],
            recv_sem=d_rsem.at[a],
            device_id={"seq": before},
            device_id_type=MESH,
        )

    gate = 1.0 / (1.0 + jnp.exp(-logits_ref[...]))
    pieces = thirds(gate)
    fields = jnp.concatenate(
        [heads_ref[...].astype(F32), slots_ref[...].astype(F32)] + pieces, axis=0
    ).astype(BF16)
    count = fields.shape[0]

    for c in range(routes // 256):
        rows = pl.ds(c * 256, 256)
        mixed = dot_nt(token_rows(c, tokens), fields)
        r = lax.broadcasted_iota(jnp.int32, (256, count), 0)
        f = lax.broadcasted_iota(jnp.int32, (256, count), 1)
        mixed = jnp.where((r & 7) == (f & 7), mixed, 0.0).astype(BF16)
        f = lax.broadcasted_iota(jnp.int32, (count, 128), 0)
        dest_ref[rows, :] = dot(mixed, dest_weight(f))
        gate_ref[rows, :] = dot(mixed, one_hot(f >= 16))
        f = lax.broadcasted_iota(jnp.int32, (8, count), 1)
        want = lax.broadcasted_iota(jnp.int32, (8, count), 0)
        as_head = (want == 1) & (f < 8)
        as_slot = (want == 2) & (f >= 8) & (f < 16)
        weight = jnp.where(want == 0, dest_weight(f).astype(F32), jnp.where(as_head | as_slot, 1.0, 0.0))
        rows_ref[:, rows] = dot_nt(weight.astype(BF16), mixed)

    cot_in.wait()
    for c in range(routes // 256):
        rows = pl.ds(c * 256, 256)
        x_grad[rows, :] = (x_cot[rows, :].astype(F32) * gate_ref[rows, :]).astype(BF16)

    proj_in.wait()

    def dispatch(a, c):
        first = pl.multiple_of(lax.rem(me // 4 + c, 4) * (4 * CAP), 4 * CAP)
        rows = pl.ds(first, 4 * CAP)
        r = lax.broadcasted_iota(jnp.int32, (4 * CAP, 128), 0) + first
        source = div48(r)
        ids = (source * (OWN * CAP) + (r - source * CAP) + a * CAP).astype(F32)
        hot = one_hot(jnp.concatenate([ids] * tiles, axis=1) == rows_ref[0:1, :])
        fsend[a, rows, : 3 * HS] = dot(hot, x_proj[...]).astype(BF16)
        fsend[a, rows, 3 * HS :] = dot(hot, x_grad[...]).astype(BF16)

    def ship(a, c):
        @pl.when(c == 0)
        def _():
            frecv[a, block(me), :] = fsend[a, block(me), :]

        @pl.loop(0, 4)
        def _(x):
            @pl.when(c * 4 + x > 0)
            def _():
                fwd_copy(a, c * 4 + x).start()

    dispatch(0, 0)
    pl.semaphore_wait(barrier, PEERS + 1)
    ship(0, 0)

    @pl.loop(1, 4)
    def _(n):
        dispatch(0, n)
        ship(0, n)

    lane_route = lax.broadcasted_iota(jnp.int32, (8, routes), 1)
    position = (lane_route >> 3) + (here * PEERS + me) * tokens
    docs = jnp.ones((8, routes), F32)
    lengths_in.wait()
    end = lengths_ref[0]
    for n in range(lengths_ref.shape[0]):
        docs = docs + jnp.where(position >= end, 1.0, 0.0)
        if n + 1 < lengths_ref.shape[0]:
            end = end + lengths_ref[n + 1]
    row = lax.broadcasted_iota(jnp.int32, (256, 128), 0)
    row_head = (4 * (row >> 4) + (row & 3)).astype(F32)
    at_head = jnp.concatenate([row_head] * tiles, axis=1) == rows_ref[1:2, :]
    docs_wide = jnp.where(at_head, docs[0:1, :], 0.0).astype(BF16)
    lane_slot = lax.broadcasted_iota(jnp.int32, (128, 128), 0).astype(F32)
    at_slot = one_hot(jnp.concatenate([lane_slot] * tiles, axis=1) == rows_ref[2:3, :])
    doc_send[...] = dot_nt(docs_wide, at_slot).astype(BF16)
    doc_recv[doc_rows(me), :] = doc_send[doc_rows(me), :]

    @pl.loop(1, PEERS)
    def _(d):
        doc_copy(d).start()

    def take_head(a):
        @pl.loop(1, PEERS)
        def _(d):
            fwd_copy(a, d).wait_recv()

        kv_copy(a).start()

    @pl.loop(4, 4 * OWN)
    def _(n):
        dispatch(n >> 2, n & 3)
        ship(n >> 2, n & 3)

    @pl.loop(1, PEERS)
    def _(d):
        doc_copy(d).wait_recv()

    doc_shift.start()
    take_head(0)

    def head_docs(a, docs_ref):
        r = lax.broadcasted_iota(jnp.int32, (SPAN, 128), 0)
        lane = lax.broadcasted_iota(jnp.int32, (SPAN, 128), 1)
        source = div48(r)
        wanted = source * 16 + a
        pick = one_hot(jnp.concatenate([lane, lane + 128], axis=1) == jnp.concatenate([wanted] * 2, axis=1))
        spread = dot(pick, docs_ref[...])
        return jnp.where(lane == r - source * CAP, spread, 0.0).astype(BF16)

    def finish(a):
        d_copy(a).wait_recv()
        dk = dk_acc[a, SPAN:, :] * scaling + drecv[a, :, :HS].astype(F32)
        dv = dv_acc[a, SPAN:, :] + drecv[a, :, HS:].astype(F32)
        rsend[a, 1, :, :HS] = dk.astype(BF16)
        rsend[a, 1, :, HS:] = dv.astype(BF16)
        send_home(a, 1)

    def attention(a):
        k_all[:SPAN, :] = kv_prev[a, :, :HS]
        v_all[:SPAN, :] = kv_prev[a, :, HS:]
        k_all[SPAN:, :] = frecv[a, :, HS : 2 * HS]
        v_all[SPAN:, :] = frecv[a, :, 2 * HS : 3 * HS]
        k_t[...] = k_all[...].T
        v_t[...] = v_all[...].T
        ones = jnp.ones((HS, HS), BF16)
        mine = head_docs(a, doc_recv)
        key_docs[:SPAN, :] = dot(head_docs(a, doc_prev), ones)
        key_docs[SPAN:, :] = dot(mine, ones)
        query_docs[...] = dot_nt(ones[:8], mine)
        dk_acc[a] = jnp.zeros((2 * SPAN, HS), F32)
        dv_acc[a] = jnp.zeros((2 * SPAN, HS), F32)

        for i in range(SPAN // QT):
            if i == 1:

                @pl.when(a < OWN - 1)
                def _():
                    take_head(a + 1)

            if i == 2:

                @pl.when(a > 0)
                def _():
                    finish(a - 1)

            first = i * QT
            left = first // CAP * CAP
            right = SPAN + first + QT
            start = left // 128 * 128
            skip = left - start
            cuts = [min(left + c * KC, right) for c in range((right - left - 1) // KC + 2)]
            chunks = list(zip(cuts, cuts[1:]))
            if skip:
                p_buf[:skip, :] = jnp.zeros((skip, QT), BF16)
                ds_buf[:skip, :] = jnp.zeros((skip, QT), BF16)
            q = frecv[a, first : first + QT, :HS]
            out_grad = frecv[a, first : first + QT, 3 * HS :]
            q_docs = query_docs[0:1, first : first + QT]
            top = jnp.full((1, QT), MASKED, F32)
            for low, high in chunks:
                s = dot_nt(k_all[low:high, :], q) * (scaling * math.log2(math.e))
                docs = key_docs[low:high, :]
                seen = jnp.concatenate([docs, docs], axis=1) == q_docs
                if high > SPAN + first:
                    k_at = lax.broadcasted_iota(jnp.int32, s.shape, 0) + (low - SPAN)
                    q_at = lax.broadcasted_iota(jnp.int32, s.shape, 1) + first
                    seen = seen & (k_at <= q_at)
                s = jnp.where(seen, s, MASKED)
                s_buf[low - start : high - start, :] = s
                top = jnp.maximum(top, jnp.max(s, axis=0, keepdims=True))
            total = jnp.zeros((1, QT), F32)
            for low, high in chunks:
                part = slice(low - start, high - start)
                p = jnp.exp2(s_buf[part, :] - top)
                total = total + jnp.sum(p, axis=0, keepdims=True)
                s_buf[part, :] = p
                p_buf[part, :] = p.astype(BF16)
            inverse = 1.0 / total
            attended = (dot(v_t[:, start:right], p_buf[: right - start, :]) * inverse).astype(BF16)
            out_grad_t = (out_grad.astype(F32).T * inverse).astype(BF16)
            delta = jnp.sum(out_grad_t.astype(F32) * attended.astype(F32), axis=0, keepdims=True)
            for low, high in chunks:
                part = slice(low - start, high - start)
                dp = dot(v_all[low:high, :], out_grad_t)
                ds = (s_buf[part, :] * (dp - delta)).astype(BF16)
                ds_buf[part, :] = ds
                dv_acc[a, low:high, :] += dot_nt(p_buf[part, :], out_grad_t)
                dk_acc[a, low:high, :] += dot(ds, q)
            dq = dot(k_t[:, start:right], ds_buf[: right - start, :]) * scaling
            rsend[a, 0, first : first + QT, :HS] = attended.astype(F32).T.astype(BF16)
            rsend[a, 0, first : first + QT, HS:] = dq.T.astype(BF16)

        dsend[a, :, :HS] = (dk_acc[a, :SPAN, :] * scaling).astype(BF16)
        dsend[a, :, HS:] = dv_acc[a, :SPAN, :].astype(BF16)
        d_copy(a).start()
        send_home(a, 0)

    doc_shift.wait_recv()

    @pl.loop(0, OWN)
    def _(a):
        kv_copy(a).wait_recv()
        attention(a)

    def await_half(a, half):
        @pl.loop(1, PEERS)
        def _(d):
            ret_copy(a, half, d).wait_recv()

    def combine(a):
        await_half(a, 0)
        await_half(a, 1)

        @pl.loop(0, routes // 256)
        def _(c):
            rows = pl.ds(pl.multiple_of(c * 256, 256), 256)
            hot = chosen(dest_ref[rows, :], head_slots(a))
            more = jnp.concatenate([dot(hot, rrecv[a, 0]), dot(hot, rrecv[a, 1])], axis=1)

            @pl.when(a == 0)
            def _():
                out_acc[rows, :] = more.astype(BF16)

            @pl.when(a > 0)
            def _():
                out_acc[rows, :] = (out_acc[rows, :].astype(F32) + more).astype(BF16)

    @pl.loop(0, OWN - 1)
    def _(a):
        @pl.when(a == OWN - 2)
        def _():
            finish(OWN - 1)

        combine(a)

    await_half(OWN - 1, 0)

    @pl.loop(0, routes // 256)
    def _(c):
        rows = pl.ds(pl.multiple_of(c * 256, 256), 256)
        hot = chosen(dest_ref[rows, :], head_slots(OWN - 1))
        more = dot(hot, rrecv[OWN - 1, 0])
        out_acc[rows, : 2 * HS] = (out_acc[rows, : 2 * HS].astype(F32) + more).astype(BF16)

    @pl.loop(1, PEERS)
    def _(d):
        doc_copy(d).wait_send()

    doc_shift.wait_send()

    @pl.loop(0, OWN)
    def _(a):
        @pl.loop(1, PEERS)
        def _(d):
            fwd_copy(a, d).wait_send()

        kv_copy(a).wait_send()
        d_copy(a).wait_send()

    @pl.loop(0, OWN)
    def _(a):
        @pl.loop(1, PEERS)
        def _(d):
            ret_copy(a, 0, d).wait_send()
            ret_copy(a, 1, d).wait_send()

    await_half(OWN - 1, 1)


def home_kernel(
    routes_ref,
    last_ref,
    dest_ref,
    gate_ref,
    cot_ref,
    logits_ref,
    head_out_hbm,
    proj_out_hbm,
    grad_out,
    out_head,
    out_proj,
    out_sem,
):
    tokens = logits_ref.shape[1]
    late = head_slots(OWN - 1)
    lane = lax.broadcasted_iota(jnp.int32, (8, HS), 1)
    eye = one_hot(lax.broadcasted_iota(jnp.int32, (8, HS), 0) == lane)
    grads = jnp.zeros((8, tokens), F32)
    copies = []
    for c in range(routes_ref.shape[0] // 256):
        rows = pl.ds(c * 256, 256)
        hot = chosen(dest_ref[rows, :], late)
        rest = routes_ref[rows, 2 * HS :].astype(F32) + dot(hot, last_ref[OWN - 1, 1])
        out_proj[rows, :HS] = routes_ref[rows, HS : 2 * HS]
        out_proj[rows, HS:] = rest.astype(BF16)
        attended = routes_ref[rows, :HS].astype(F32)
        out_head[rows, :] = (attended * gate_ref[rows, :]).astype(BF16)
        for n, (source, target) in enumerate(((out_head, head_out_hbm), (out_proj, proj_out_hbm))):
            copies.append(pltpu.make_async_copy(source.at[rows], target.at[rows], out_sem.at[c, n]))
            copies[-1].start()
        inner = jnp.sum(cot_ref[rows, :].astype(F32) * attended, axis=1, keepdims=True)
        r = lax.broadcasted_iota(jnp.int32, (256, HS), 0)
        lane = lax.broadcasted_iota(jnp.int32, (256, HS), 1)
        dots = jnp.where((r & 7) == lane, inner, 0.0)
        by_route = sum(dot_nt(eye, part.astype(BF16)) for part in thirds(dots))
        hot = token_rows(c, tokens)
        grads = grads + sum(dot(part.astype(BF16), hot) for part in thirds(by_route))
    gate = 1.0 / (1.0 + jnp.exp(-logits_ref[...]))
    grad_out[...] = grads * gate * (1.0 - gate)
    for copy in copies:
        copy.wait()


def per_device(projections, routed_heads, slot_index, gate_logits, doc_lengths, cotangent):
    tokens, top, width = projections.shape
    routes = tokens * top
    dma = pltpu.SemaphoreType.DMA
    vmem = pltpu.VMEM
    whole = pl.BlockSpec(memory_space=pltpu.VMEM)
    hbm = pl.BlockSpec(memory_space=pltpu.HBM)
    cot_rows = cotangent.reshape(routes, HS)
    logits = gate_logits.T
    handed = pl.pallas_call(
        kernel,
        out_shape=(
            jax.ShapeDtypeStruct((routes, WIDE), BF16),
            jax.ShapeDtypeStruct((OWN, 2, SPAN, 2 * HS), BF16),
            jax.ShapeDtypeStruct((routes, HS), F32),
            jax.ShapeDtypeStruct((routes, HS), F32),
        ),
        in_specs=[hbm, hbm, whole, whole, whole, hbm],
        out_specs=(whole, whole, whole, whole),
        scratch_shapes=[
            pltpu.SMEM(doc_lengths.shape, jnp.int32),
            vmem((routes, 3 * HS), BF16),
            vmem((routes, HS), BF16),
            vmem((routes, HS), BF16),
            vmem((8, routes), F32),
            vmem((OWN, SPAN, WIDE), BF16),
            vmem((OWN, SPAN, WIDE), BF16),
            vmem((PEERS * 16, 128), BF16),
            vmem((PEERS * 16, 128), BF16),
            vmem((PEERS * 16, 128), BF16),
            vmem((OWN, SPAN, 2 * HS), BF16),
            vmem((OWN, SPAN, 2 * HS), BF16),
            vmem((OWN, SPAN, 2 * HS), BF16),
            vmem((OWN, 2, SPAN, 2 * HS), BF16),
            vmem((2 * SPAN, HS), BF16),
            vmem((2 * SPAN, HS), BF16),
            vmem((HS, 2 * SPAN), BF16),
            vmem((HS, 2 * SPAN), BF16),
            vmem((2 * SPAN, HS), F32),
            vmem((8, SPAN), F32),
            vmem((WIN, QT), F32),
            vmem((WIN, QT), BF16),
            vmem((WIN, QT), BF16),
            vmem((OWN, 2 * SPAN, HS), F32),
            vmem((OWN, 2 * SPAN, HS), F32),
            dma((OWN, PEERS)),
            dma((OWN, PEERS)),
            dma((PEERS,)),
            dma((PEERS,)),
            dma((2,)),
            dma((OWN,)),
            dma((OWN,)),
            dma((OWN,)),
            dma((OWN,)),
            dma((OWN, 2, PEERS)),
            dma((OWN, 2, PEERS)),
            dma((3,)),
        ],
        compiler_params=pltpu.CompilerParams(
            collective_id=0, has_side_effects=True, vmem_limit_bytes=44000 * 1024
        ),
    )(
        *(
            pltpu.with_memory_space_constraint(v, pltpu.HBM)
            for v in (
                projections.reshape(routes, width),
                cot_rows,
                routed_heads.T,
                slot_index.T,
                logits,
                doc_lengths,
            )
        ),
    )
    head_outputs, projection_grads, gate_grads = pl.pallas_call(
        home_kernel,
        out_shape=(
            jax.ShapeDtypeStruct((routes, HS), BF16),
            jax.ShapeDtypeStruct((routes, 3 * HS), BF16),
            jax.ShapeDtypeStruct((top, tokens), F32),
        ),
        in_specs=[whole] * 6,
        out_specs=(hbm, hbm, whole),
        scratch_shapes=[
            vmem((routes, HS), BF16),
            vmem((routes, 3 * HS), BF16),
            dma((routes // 256, 2)),
        ],
        compiler_params=pltpu.CompilerParams(vmem_limit_bytes=16000 * 1024),
    )(*handed, cot_rows, logits)
    return (
        head_outputs.reshape(tokens, top, HS),
        projection_grads.reshape(tokens, top, width),
        gate_grads.T,
    )


def solution(mesh):
    tokens = P(("seq", "head"), None, None)
    routes = P(("seq", "head"), None)
    return jax.shard_map(
        per_device,
        mesh=mesh,
        in_specs=(tokens, routes, routes, routes, P(), tokens),
        out_specs=(tokens, tokens, routes),
        check_vma=False,
    )
```

```python
import math

import jax
import jax.numpy as jnp
from jax import lax
from jax.experimental import pallas as pl
from jax.experimental.pallas import tpu as pltpu
from jax.sharding import PartitionSpec as P

H = 64
CAP = 48
OWN = 4
PEERS = 16
SPAN = PEERS * CAP
HS = 128
WIDE = 4 * HS
QT = 256
WIN = 1152
KC = 384
MASKED = -1e30
F32 = jnp.float32
BF16 = jnp.bfloat16
MESH = pl.DeviceIdType.MESH


def dot_nt(a, b):
    return lax.dot_general(a, b, (((1,), (1,)), ((), ())), preferred_element_type=F32)


def dot(a, b):
    return jnp.dot(a, b, preferred_element_type=F32)


def one_hot(mask):
    return jnp.where(mask, 1.0, 0.0).astype(BF16)


def thirds(v):
    high = v.astype(BF16).astype(F32)
    middle = (v - high).astype(BF16).astype(F32)
    return [high, middle, v - high - middle]


def dest_weight(f):
    return jnp.where(f < 8, float(CAP), jnp.where(f < 16, 1.0, 0.0)).astype(BF16)


def div48(v):
    return (v * 1366) >> 16


def token_rows(c, tokens):
    r = lax.broadcasted_iota(jnp.int32, (256, tokens), 0)
    t = lax.broadcasted_iota(jnp.int32, (256, tokens), 1)
    return one_hot((r >> 3) + c * 32 == t)


def head_slots(a):
    lane = lax.broadcasted_iota(jnp.int32, (8, SPAN), 1)
    source = div48(lane)
    return (source * (OWN * CAP) + (lane - source * CAP) + a * CAP).astype(F32)


def chosen(dest, ids):
    return one_hot(jnp.concatenate([dest] * (ids.shape[1] // 128), axis=1) == ids[0:1, :])


def kernel(
    proj_hbm,
    cot_hbm,
    heads_ref,
    slots_ref,
    logits_ref,
    lengths_hbm,
    out_acc,
    rrecv,
    dest_ref,
    gate_ref,
    lengths_ref,
    x_proj,
    x_cot,
    x_grad,
    mixed_ref,
    rows_ref,
    fsend,
    frecv,
    doc_send,
    doc_recv,
    doc_prev,
    kv_prev,
    dsend,
    drecv,
    rsend,
    k_all,
    v_all,
    k_t,
    v_t,
    key_docs,
    query_docs,
    s_buf,
    p_buf,
    ds_buf,
    dk_acc,
    dv_acc,
    f_ssem,
    f_rsem,
    doc_ssem,
    doc_rsem,
    dp_sem,
    kv_ssem,
    kv_rsem,
    d_ssem,
    d_rsem,
    r_ssem,
    r_rsem,
    in_sem,
):
    me = lax.axis_index("head")
    here = lax.axis_index("seq")
    after = (here + 1) & (PEERS - 1)
    before = (here + PEERS - 1) & (PEERS - 1)
    routes = proj_hbm.shape[0]
    tokens = heads_ref.shape[1]
    tiles = routes // 128
    scaling = HS ** (-0.5)
    proj_in = pltpu.make_async_copy(proj_hbm, x_proj, in_sem.at[0])
    cot_in = pltpu.make_async_copy(cot_hbm, x_cot, in_sem.at[1])
    lengths_in = pltpu.make_async_copy(lengths_hbm, lengths_ref, in_sem.at[2])
    cot_in.start()
    proj_in.start()
    lengths_in.start()

    barrier = pltpu.get_barrier_semaphore()

    def peer_of(d):
        px = (me + d) & 3
        py = ((me >> 2) + (d >> 2)) & 3
        return py * 4 + px

    @pl.loop(1, PEERS)
    def _(d):
        pl.semaphore_signal(barrier, inc=1, device_id={"head": peer_of(d)}, device_id_type=MESH)

    pl.semaphore_signal(barrier, inc=1, device_id={"seq": after}, device_id_type=MESH)
    pl.semaphore_signal(barrier, inc=1, device_id={"seq": before}, device_id_type=MESH)

    def block(i):
        return pl.ds(pl.multiple_of(i * CAP, CAP), CAP)

    def fwd_copy(a, d):
        peer = peer_of(d)
        return pltpu.make_async_remote_copy(
            src_ref=fsend.at[a, block(peer)],
            dst_ref=frecv.at[a, block(me)],
            send_sem=f_ssem.at[a, d],
            recv_sem=f_rsem.at[a, d],
            device_id={"head": peer},
            device_id_type=MESH,
        )

    def ret_copy(a, half, d):
        peer = peer_of(d)
        return pltpu.make_async_remote_copy(
            src_ref=rsend.at[a, half, block(peer)],
            dst_ref=rrecv.at[a, half, block(me)],
            send_sem=r_ssem.at[a, half, d],
            recv_sem=r_rsem.at[a, half, d],
            device_id={"head": peer},
            device_id_type=MESH,
        )

    def send_home(a, half):
        @pl.loop(1, PEERS)
        def _(d):
            ret_copy(a, half, d).start()

        rrecv[a, half, block(me), :] = rsend[a, half, block(me), :]

    def doc_rows(i):
        return pl.ds(pl.multiple_of(i * 16, 16), 16)

    def doc_copy(d):
        peer = peer_of(d)
        return pltpu.make_async_remote_copy(
            src_ref=doc_send.at[doc_rows(peer)],
            dst_ref=doc_recv.at[doc_rows(me)],
            send_sem=doc_ssem.at[d],
            recv_sem=doc_rsem.at[d],
            device_id={"head": peer},
            device_id_type=MESH,
        )

    doc_shift = pltpu.make_async_remote_copy(
        src_ref=doc_recv,
        dst_ref=doc_prev,
        send_sem=dp_sem.at[0],
        recv_sem=dp_sem.at[1],
        device_id={"seq": after},
        device_id_type=MESH,
    )

    def kv_copy(a):
        return pltpu.make_async_remote_copy(
            src_ref=frecv.at[a, :, pl.ds(HS, 2 * HS)],
            dst_ref=kv_prev.at[a],
            send_sem=kv_ssem.at[a],
            recv_sem=kv_rsem.at[a],
            device_id={"seq": after},
            device_id_type=MESH,
        )

    def d_copy(a):
        return pltpu.make_async_remote_copy(
            src_ref=dsend.at[a],
            dst_ref=drecv.at[a],
            send_sem=d_ssem.at[a],
            recv_sem=d_rsem.at[a],
            device_id={"seq": before},
            device_id_type=MESH,
        )

    gate = 1.0 / (1.0 + jnp.exp(-logits_ref[...]))
    pieces = thirds(gate)
    fields = jnp.concatenate(
        [heads_ref[...].astype(F32), slots_ref[...].astype(F32)] + pieces, axis=0
    ).astype(BF16)
    count = fields.shape[0]

    for c in range(routes // 256):
        rows = pl.ds(c * 256, 256)
        mixed = dot_nt(token_rows(c, tokens), fields)
        r = lax.broadcasted_iota(jnp.int32, (256, count), 0)
        f = lax.broadcasted_iota(jnp.int32, (256, count), 1)
        mixed = jnp.where((r & 7) == (f & 7), mixed, 0.0).astype(BF16)
        mixed_ref[rows, :] = mixed
        f = lax.broadcasted_iota(jnp.int32, (count, 128), 0)
        gate_ref[rows, :] = dot(mixed, one_hot(f >= 16))
        f = lax.broadcasted_iota(jnp.int32, (8, count), 1)
        want = lax.broadcasted_iota(jnp.int32, (8, count), 0)
        as_head = (want == 1) & (f < 8)
        as_slot = (want == 2) & (f >= 8) & (f < 16)
        weight = jnp.where(want == 0, dest_weight(f).astype(F32), jnp.where(as_head | as_slot, 1.0, 0.0))
        rows_ref[:, rows] = dot_nt(weight.astype(BF16), mixed)

    cot_in.wait()
    for c in range(routes // 256):
        rows = pl.ds(c * 256, 256)
        x_grad[rows, :] = (x_cot[rows, :].astype(F32) * gate_ref[rows, :]).astype(BF16)

    proj_in.wait()

    def dispatch(a, c):
        first = pl.multiple_of((((me >> 2) + c) & 3) * (4 * CAP), 4 * CAP)
        rows = pl.ds(first, 4 * CAP)
        r = lax.broadcasted_iota(jnp.int32, (4 * CAP, 128), 0) + first
        source = div48(r)
        ids = (source * (OWN * CAP) + (r - source * CAP) + a * CAP).astype(F32)
        hot = one_hot(jnp.concatenate([ids] * tiles, axis=1) == rows_ref[0:1, :])
        fsend[a, rows, : 3 * HS] = dot(hot, x_proj[...]).astype(BF16)
        fsend[a, rows, 3 * HS :] = dot(hot, x_grad[...]).astype(BF16)

    def ship(a, c):
        @pl.when(c == 0)
        def _():
            frecv[a, block(me), :] = fsend[a, block(me), :]

        @pl.loop(0, 4)
        def _(x):
            @pl.when(c * 4 + x > 0)
            def _():
                fwd_copy(a, c * 4 + x).start()

    dispatch(0, 0)
    pl.semaphore_wait(barrier, PEERS + 1)
    ship(0, 0)

    @pl.loop(1, 4)
    def _(n):
        dispatch(0, n)
        ship(0, n)

    lane_route = lax.broadcasted_iota(jnp.int32, (8, routes), 1)
    position = (lane_route >> 3) + (here * PEERS + me) * tokens
    docs = jnp.ones((8, routes), F32)
    lengths_in.wait()
    end = lengths_ref[0]
    for n in range(lengths_ref.shape[0]):
        docs = docs + jnp.where(position >= end, 1.0, 0.0)
        if n + 1 < lengths_ref.shape[0]:
            end = end + lengths_ref[n + 1]
    row = lax.broadcasted_iota(jnp.int32, (256, 128), 0)
    row_head = (4 * (row >> 4) + (row & 3)).astype(F32)
    at_head = jnp.concatenate([row_head] * tiles, axis=1) == rows_ref[1:2, :]
    docs_wide = jnp.where(at_head, docs[0:1, :], 0.0).astype(BF16)
    lane_slot = lax.broadcasted_iota(jnp.int32, (128, 128), 0).astype(F32)
    at_slot = one_hot(jnp.concatenate([lane_slot] * tiles, axis=1) == rows_ref[2:3, :])
    doc_send[...] = dot_nt(docs_wide, at_slot).astype(BF16)
    doc_recv[doc_rows(me), :] = doc_send[doc_rows(me), :]

    @pl.loop(1, PEERS)
    def _(d):
        doc_copy(d).start()

    def take_head(a):
        @pl.loop(1, PEERS)
        def _(d):
            fwd_copy(a, d).wait_recv()

        kv_copy(a).start()

    @pl.loop(0, routes // 256)
    def _(c):
        rows = pl.ds(pl.multiple_of(c * 256, 256), 256)
        f = lax.broadcasted_iota(jnp.int32, (count, 128), 0)
        dest_ref[rows, :] = dot(mixed_ref[rows, :], dest_weight(f))

    @pl.loop(4, 4 * OWN)
    def _(n):
        dispatch(n >> 2, n & 3)
        ship(n >> 2, n & 3)

    @pl.loop(1, PEERS)
    def _(d):
        doc_copy(d).wait_recv()

    doc_shift.start()
    take_head(0)

    def head_docs(a, docs_ref):
        r = lax.broadcasted_iota(jnp.int32, (SPAN, 128), 0)
        lane = lax.broadcasted_iota(jnp.int32, (SPAN, 128), 1)
        source = div48(r)
        wanted = source * 16 + a
        pick = one_hot(jnp.concatenate([lane, lane + 128], axis=1) == jnp.concatenate([wanted] * 2, axis=1))
        spread = dot(pick, docs_ref[...])
        return jnp.where(lane == r - source * CAP, spread, 0.0).astype(BF16)

    def finish(a):
        d_copy(a).wait_recv()
        dk = dk_acc[a, SPAN:, :] * scaling + drecv[a, :, :HS].astype(F32)
        dv = dv_acc[a, SPAN:, :] + drecv[a, :, HS:].astype(F32)
        rsend[a, 1, :, :HS] = dk.astype(BF16)
        rsend[a, 1, :, HS:] = dv.astype(BF16)
        send_home(a, 1)

    def attention(a):
        k_all[:SPAN, :] = kv_prev[a, :, :HS]
        v_all[:SPAN, :] = kv_prev[a, :, HS:]
        k_all[SPAN:, :] = frecv[a, :, HS : 2 * HS]
        v_all[SPAN:, :] = frecv[a, :, 2 * HS : 3 * HS]
        k_t[...] = k_all[...].T
        v_t[...] = v_all[...].T
        ones = jnp.ones((HS, HS), BF16)
        mine = head_docs(a, doc_recv)
        key_docs[:SPAN, :] = dot(head_docs(a, doc_prev), ones)
        key_docs[SPAN:, :] = dot(mine, ones)
        query_docs[...] = dot_nt(ones[:8], mine)
        dk_acc[a] = jnp.zeros((2 * SPAN, HS), F32)
        dv_acc[a] = jnp.zeros((2 * SPAN, HS), F32)

        for i in range(SPAN // QT):
            if i == 1:

                @pl.when(a < OWN - 1)
                def _():
                    take_head(a + 1)

            if i == 2:

                @pl.when(a > 0)
                def _():
                    finish(a - 1)

            first = i * QT
            left = first // CAP * CAP
            right = SPAN + first + QT
            start = left // 128 * 128
            skip = left - start
            cuts = [min(left + c * KC, right) for c in range((right - left - 1) // KC + 2)]
            chunks = list(zip(cuts, cuts[1:]))
            if skip:
                p_buf[:skip, :] = jnp.zeros((skip, QT), BF16)
                ds_buf[:skip, :] = jnp.zeros((skip, QT), BF16)
            q = frecv[a, first : first + QT, :HS]
            out_grad = frecv[a, first : first + QT, 3 * HS :]
            q_docs = query_docs[0:1, first : first + QT]
            top = jnp.full((1, QT), MASKED, F32)
            for low, high in chunks:
                s = dot_nt(k_all[low:high, :], q) * (scaling * math.log2(math.e))
                docs = key_docs[low:high, :]
                seen = jnp.concatenate([docs, docs], axis=1) == q_docs
                if high > SPAN + first:
                    k_at = lax.broadcasted_iota(jnp.int32, s.shape, 0) + (low - SPAN)
                    q_at = lax.broadcasted_iota(jnp.int32, s.shape, 1) + first
                    seen = seen & (k_at <= q_at)
                s = jnp.where(seen, s, MASKED)
                s_buf[low - start : high - start, :] = s
                top = jnp.maximum(top, jnp.max(s, axis=0, keepdims=True))
            total = jnp.zeros((1, QT), F32)
            for low, high in chunks:
                part = slice(low - start, high - start)
                p = jnp.exp2(s_buf[part, :] - top)
                total = total + jnp.sum(p, axis=0, keepdims=True)
                s_buf[part, :] = p
                p_buf[part, :] = p.astype(BF16)
            inverse = 1.0 / total
            attended = (dot(v_t[:, start:right], p_buf[: right - start, :]) * inverse).astype(BF16)
            out_grad_t = (out_grad.astype(F32).T * inverse).astype(BF16)
            delta = jnp.sum(out_grad_t.astype(F32) * attended.astype(F32), axis=0, keepdims=True)
            for low, high in chunks:
                part = slice(low - start, high - start)
                dp = dot(v_all[low:high, :], out_grad_t)
                ds = (s_buf[part, :] * (dp - delta)).astype(BF16)
                ds_buf[part, :] = ds
                dv_acc[a, low:high, :] += dot_nt(p_buf[part, :], out_grad_t)
                dk_acc[a, low:high, :] += dot(ds, q)
            dq = dot(k_t[:, start:right], ds_buf[: right - start, :]) * scaling
            rsend[a, 0, first : first + QT, :HS] = attended.astype(F32).T.astype(BF16)
            rsend[a, 0, first : first + QT, HS:] = dq.T.astype(BF16)

        dsend[a, :, :HS] = (dk_acc[a, :SPAN, :] * scaling).astype(BF16)
        dsend[a, :, HS:] = dv_acc[a, :SPAN, :].astype(BF16)
        d_copy(a).start()
        send_home(a, 0)

    doc_shift.wait_recv()

    @pl.loop(0, OWN)
    def _(a):
        kv_copy(a).wait_recv()
        attention(a)

    def await_half(a, half):
        @pl.loop(1, PEERS)
        def _(d):
            ret_copy(a, half, d).wait_recv()

    def combine(a):
        await_half(a, 0)
        await_half(a, 1)

        @pl.loop(0, routes // 256)
        def _(c):
            rows = pl.ds(pl.multiple_of(c * 256, 256), 256)
            hot = chosen(dest_ref[rows, :], head_slots(a))
            more = jnp.concatenate([dot(hot, rrecv[a, 0]), dot(hot, rrecv[a, 1])], axis=1)

            @pl.when(a == 0)
            def _():
                out_acc[rows, :] = more.astype(BF16)

            @pl.when(a > 0)
            def _():
                out_acc[rows, :] = (out_acc[rows, :].astype(F32) + more).astype(BF16)

    @pl.loop(0, OWN - 1)
    def _(a):
        @pl.when(a == OWN - 2)
        def _():
            finish(OWN - 1)

        combine(a)

    await_half(OWN - 1, 0)

    @pl.loop(0, routes // 256)
    def _(c):
        rows = pl.ds(pl.multiple_of(c * 256, 256), 256)
        hot = chosen(dest_ref[rows, :], head_slots(OWN - 1))
        more = dot(hot, rrecv[OWN - 1, 0])
        out_acc[rows, : 2 * HS] = (out_acc[rows, : 2 * HS].astype(F32) + more).astype(BF16)

    @pl.loop(1, PEERS)
    def _(d):
        doc_copy(d).wait_send()

    doc_shift.wait_send()

    @pl.loop(0, OWN)
    def _(a):
        @pl.loop(1, PEERS)
        def _(d):
            fwd_copy(a, d).wait_send()

        kv_copy(a).wait_send()
        d_copy(a).wait_send()

    @pl.loop(0, OWN)
    def _(a):
        @pl.loop(1, PEERS)
        def _(d):
            ret_copy(a, 0, d).wait_send()
            ret_copy(a, 1, d).wait_send()

    await_half(OWN - 1, 1)


def home_kernel(
    routes_ref,
    last_ref,
    dest_ref,
    gate_ref,
    cot_ref,
    logits_ref,
    head_out_hbm,
    proj_out_hbm,
    grad_out,
    out_head,
    out_proj,
    out_sem,
):
    tokens = logits_ref.shape[1]
    late = head_slots(OWN - 1)
    lane = lax.broadcasted_iota(jnp.int32, (8, HS), 1)
    eye = one_hot(lax.broadcasted_iota(jnp.int32, (8, HS), 0) == lane)
    grads = jnp.zeros((8, tokens), F32)
    copies = []
    for c in range(routes_ref.shape[0] // 256):
        rows = pl.ds(c * 256, 256)
        hot = chosen(dest_ref[rows, :], late)
        rest = routes_ref[rows, 2 * HS :].astype(F32) + dot(hot, last_ref[OWN - 1, 1])
        out_proj[rows, :HS] = routes_ref[rows, HS : 2 * HS]
        out_proj[rows, HS:] = rest.astype(BF16)
        attended = routes_ref[rows, :HS].astype(F32)
        out_head[rows, :] = (attended * gate_ref[rows, :]).astype(BF16)
        for n, (source, target) in enumerate(((out_head, head_out_hbm), (out_proj, proj_out_hbm))):
            copies.append(pltpu.make_async_copy(source.at[rows], target.at[rows], out_sem.at[c, n]))
            copies[-1].start()
        inner = jnp.sum(cot_ref[rows, :].astype(F32) * attended, axis=1, keepdims=True)
        r = lax.broadcasted_iota(jnp.int32, (256, HS), 0)
        lane = lax.broadcasted_iota(jnp.int32, (256, HS), 1)
        dots = jnp.where((r & 7) == lane, inner, 0.0)
        by_route = sum(dot_nt(eye, part.astype(BF16)) for part in thirds(dots))
        hot = token_rows(c, tokens)
        grads = grads + sum(dot(part.astype(BF16), hot) for part in thirds(by_route))
    gate = 1.0 / (1.0 + jnp.exp(-logits_ref[...]))
    grad_out[...] = grads * gate * (1.0 - gate)
    for copy in copies:
        copy.wait()


def per_device(projections, routed_heads, slot_index, gate_logits, doc_lengths, cotangent):
    tokens, top, width = projections.shape
    routes = tokens * top
    dma = pltpu.SemaphoreType.DMA
    vmem = pltpu.VMEM
    whole = pl.BlockSpec(memory_space=pltpu.VMEM)
    hbm = pl.BlockSpec(memory_space=pltpu.HBM)
    cot_rows = cotangent.reshape(routes, HS)
    logits = gate_logits.T
    handed = pl.pallas_call(
        kernel,
        out_shape=(
            jax.ShapeDtypeStruct((routes, WIDE), BF16),
            jax.ShapeDtypeStruct((OWN, 2, SPAN, 2 * HS), BF16),
            jax.ShapeDtypeStruct((routes, HS), F32),
            jax.ShapeDtypeStruct((routes, HS), F32),
        ),
        in_specs=[hbm, hbm, whole, whole, whole, hbm],
        out_specs=(whole, whole, whole, whole),
        scratch_shapes=[
            pltpu.SMEM(doc_lengths.shape, jnp.int32),
            vmem((routes, 3 * HS), BF16),
            vmem((routes, HS), BF16),
            vmem((routes, HS), BF16),
            vmem((routes, 5 * top), BF16),
            vmem((8, routes), F32),
            vmem((OWN, SPAN, WIDE), BF16),
            vmem((OWN, SPAN, WIDE), BF16),
            vmem((PEERS * 16, 128), BF16),
            vmem((PEERS * 16, 128), BF16),
            vmem((PEERS * 16, 128), BF16),
            vmem((OWN, SPAN, 2 * HS), BF16),
            vmem((OWN, SPAN, 2 * HS), BF16),
            vmem((OWN, SPAN, 2 * HS), BF16),
            vmem((OWN, 2, SPAN, 2 * HS), BF16),
            vmem((2 * SPAN, HS), BF16),
            vmem((2 * SPAN, HS), BF16),
            vmem((HS, 2 * SPAN), BF16),
            vmem((HS, 2 * SPAN), BF16),
            vmem((2 * SPAN, HS), F32),
            vmem((8, SPAN), F32),
            vmem((WIN, QT), F32),
            vmem((WIN, QT), BF16),
            vmem((WIN, QT), BF16),
            vmem((OWN, 2 * SPAN, HS), F32),
            vmem((OWN, 2 * SPAN, HS), F32),
            dma((OWN, PEERS)),
            dma((OWN, PEERS)),
            dma((PEERS,)),
            dma((PEERS,)),
            dma((2,)),
            dma((OWN,)),
            dma((OWN,)),
            dma((OWN,)),
            dma((OWN,)),
            dma((OWN, 2, PEERS)),
            dma((OWN, 2, PEERS)),
            dma((3,)),
        ],
        compiler_params=pltpu.CompilerParams(
            collective_id=0, has_side_effects=True, vmem_limit_bytes=44000 * 1024
        ),
    )(
        *(
            pltpu.with_memory_space_constraint(v, pltpu.HBM)
            for v in (
                projections.reshape(routes, width),
                cot_rows,
                routed_heads.T,
                slot_index.T,
                logits,
                doc_lengths,
            )
        ),
    )
    head_outputs, projection_grads, gate_grads = pl.pallas_call(
        home_kernel,
        out_shape=(
            jax.ShapeDtypeStruct((routes, HS), BF16),
            jax.ShapeDtypeStruct((routes, 3 * HS), BF16),
            jax.ShapeDtypeStruct((top, tokens), F32),
        ),
        in_specs=[whole] * 6,
        out_specs=(hbm, hbm, whole),
        scratch_shapes=[
            vmem((routes, HS), BF16),
            vmem((routes, 3 * HS), BF16),
            dma((routes // 256, 2)),
        ],
        compiler_params=pltpu.CompilerParams(vmem_limit_bytes=16000 * 1024),
    )(*handed, cot_rows, logits)
    return (
        head_outputs.reshape(tokens, top, HS),
        projection_grads.reshape(tokens, top, width),
        gate_grads.T,
    )


def solution(mesh):
    tokens = P(("seq", "head"), None, None)
    routes = P(("seq", "head"), None)
    return jax.shard_map(
        per_device,
        mesh=mesh,
        in_specs=(tokens, routes, routes, routes, P(), tokens),
        out_specs=(tokens, tokens, routes),
        check_vma=False,
    )
```

```python
import math

import jax
import jax.numpy as jnp
from jax import lax
from jax.experimental import pallas as pl
from jax.experimental.pallas import tpu as pltpu
from jax.sharding import PartitionSpec as P

H = 64
CAP = 48
OWN = 4
PEERS = 16
SPAN = PEERS * CAP
HS = 128
WIDE = 4 * HS
QT = 256
WIN = 1152
KC = 384
MASKED = -1e30
F32 = jnp.float32
BF16 = jnp.bfloat16
MESH = pl.DeviceIdType.MESH


def dot_nt(a, b):
    return lax.dot_general(a, b, (((1,), (1,)), ((), ())), preferred_element_type=F32)


def dot(a, b):
    return jnp.dot(a, b, preferred_element_type=F32)


def one_hot(mask):
    return jnp.where(mask, 1.0, 0.0).astype(BF16)


def thirds(v):
    high = v.astype(BF16).astype(F32)
    middle = (v - high).astype(BF16).astype(F32)
    return [high, middle, v - high - middle]


def dest_weight(f):
    return jnp.where(f < 8, float(CAP), jnp.where(f < 16, 1.0, 0.0)).astype(BF16)


def div48(v):
    return (v * 1366) >> 16


def token_rows(c, tokens):
    r = lax.broadcasted_iota(jnp.int32, (256, tokens), 0)
    t = lax.broadcasted_iota(jnp.int32, (256, tokens), 1)
    return one_hot((r >> 3) + c * 32 == t)


def head_slots(a):
    lane = lax.broadcasted_iota(jnp.int32, (8, SPAN), 1)
    source = div48(lane)
    return (source * (OWN * CAP) + (lane - source * CAP) + a * CAP).astype(F32)


def chosen(dest, ids):
    return one_hot(jnp.concatenate([dest] * (ids.shape[1] // 128), axis=1) == ids[0:1, :])


def kernel(
    proj_hbm,
    cot_hbm,
    heads_ref,
    slots_ref,
    logits_ref,
    lengths_hbm,
    out_acc,
    rrecv,
    dest_ref,
    gate_ref,
    lengths_ref,
    x_proj,
    x_cot,
    x_grad,
    mixed_ref,
    rows_ref,
    fsend,
    frecv,
    doc_send,
    doc_recv,
    doc_prev,
    kv_prev,
    dsend,
    drecv,
    rsend,
    k_all,
    v_all,
    k_t,
    v_t,
    key_docs,
    query_docs,
    s_buf,
    p_buf,
    ds_buf,
    dk_acc,
    dv_acc,
    f_ssem,
    f_rsem,
    doc_ssem,
    doc_rsem,
    dp_sem,
    kv_ssem,
    kv_rsem,
    d_ssem,
    d_rsem,
    r_ssem,
    r_rsem,
    in_sem,
):
    me = lax.axis_index("head")
    here = lax.axis_index("seq")
    after = (here + 1) & (PEERS - 1)
    before = (here + PEERS - 1) & (PEERS - 1)
    routes = proj_hbm.shape[0]
    tokens = heads_ref.shape[1]
    tiles = routes // 128
    scaling = HS ** (-0.5)
    proj_in = pltpu.make_async_copy(proj_hbm, x_proj, in_sem.at[0])
    cot_in = pltpu.make_async_copy(cot_hbm, x_cot, in_sem.at[1])
    lengths_in = pltpu.make_async_copy(lengths_hbm, lengths_ref, in_sem.at[2])
    cot_in.start()
    proj_in.start()
    lengths_in.start()

    barrier = pltpu.get_barrier_semaphore()

    def peer_of(d):
        px = (me + d) & 3
        py = ((me >> 2) + (d >> 2)) & 3
        return py * 4 + px

    @pl.loop(1, PEERS)
    def _(d):
        pl.semaphore_signal(barrier, inc=1, device_id={"head": peer_of(d)}, device_id_type=MESH)

    pl.semaphore_signal(barrier, inc=1, device_id={"seq": after}, device_id_type=MESH)
    pl.semaphore_signal(barrier, inc=1, device_id={"seq": before}, device_id_type=MESH)

    def block(i):
        return pl.ds(pl.multiple_of(i * CAP, CAP), CAP)

    def fwd_copy(a, d):
        peer = peer_of(d)
        return pltpu.make_async_remote_copy(
            src_ref=fsend.at[a, block(peer)],
            dst_ref=frecv.at[a, block(me)],
            send_sem=f_ssem.at[a, d],
            recv_sem=f_rsem.at[a, d],
            device_id={"head": peer},
            device_id_type=MESH,
        )

    def ret_copy(a, half, d):
        peer = peer_of(d)
        return pltpu.make_async_remote_copy(
            src_ref=rsend.at[a, half, block(peer)],
            dst_ref=rrecv.at[a, half, block(me)],
            send_sem=r_ssem.at[a, half, d],
            recv_sem=r_rsem.at[a, half, d],
            device_id={"head": peer},
            device_id_type=MESH,
        )

    def send_home(a, half):
        @pl.loop(1, PEERS)
        def _(d):
            ret_copy(a, half, d).start()

        rrecv[a, half, block(me), :] = rsend[a, half, block(me), :]

    def doc_rows(i):
        return pl.ds(pl.multiple_of(i * 16, 16), 16)

    def doc_copy(d):
        peer = peer_of(d)
        return pltpu.make_async_remote_copy(
            src_ref=doc_send.at[doc_rows(peer)],
            dst_ref=doc_recv.at[doc_rows(me)],
            send_sem=doc_ssem.at[d],
            recv_sem=doc_rsem.at[d],
            device_id={"head": peer},
            device_id_type=MESH,
        )

    doc_shift = pltpu.make_async_remote_copy(
        src_ref=doc_recv,
        dst_ref=doc_prev,
        send_sem=dp_sem.at[0],
        recv_sem=dp_sem.at[1],
        device_id={"seq": after},
        device_id_type=MESH,
    )

    def kv_copy(a):
        return pltpu.make_async_remote_copy(
            src_ref=frecv.at[a, :, pl.ds(HS, 2 * HS)],
            dst_ref=kv_prev.at[a],
            send_sem=kv_ssem.at[a],
            recv_sem=kv_rsem.at[a],
            device_id={"seq": after},
            device_id_type=MESH,
        )

    def d_copy(a):
        return pltpu.make_async_remote_copy(
            src_ref=dsend.at[a],
            dst_ref=drecv.at[a],
            send_sem=d_ssem.at[a],
            recv_sem=d_rsem.at[a],
            device_id={"seq": before},
            device_id_type=MESH,
        )

    gate = 1.0 / (1.0 + jnp.exp(-logits_ref[...]))
    pieces = thirds(gate)
    fields = jnp.concatenate(
        [heads_ref[...].astype(F32), slots_ref[...].astype(F32)] + pieces, axis=0
    ).astype(BF16)
    count = fields.shape[0]

    for c in range(routes // 256):
        rows = pl.ds(c * 256, 256)
        mixed = dot_nt(token_rows(c, tokens), fields)
        r = lax.broadcasted_iota(jnp.int32, (256, count), 0)
        f = lax.broadcasted_iota(jnp.int32, (256, count), 1)
        mixed = jnp.where((r & 7) == (f & 7), mixed, 0.0).astype(BF16)
        mixed_ref[rows, :] = mixed
        f = lax.broadcasted_iota(jnp.int32, (count, 128), 0)
        gate_ref[rows, :] = dot(mixed, one_hot(f >= 16))
        f = lax.broadcasted_iota(jnp.int32, (8, count), 1)
        want = lax.broadcasted_iota(jnp.int32, (8, count), 0)
        as_head = (want == 1) & (f < 8)
        as_slot = (want == 2) & (f >= 8) & (f < 16)
        weight = jnp.where(want == 0, dest_weight(f).astype(F32), jnp.where(as_head | as_slot, 1.0, 0.0))
        rows_ref[:, rows] = dot_nt(weight.astype(BF16), mixed)

    cot_in.wait()
    for c in range(routes // 256):
        rows = pl.ds(c * 256, 256)
        x_grad[rows, :] = (x_cot[rows, :].astype(F32) * gate_ref[rows, :]).astype(BF16)

    proj_in.wait()

    def dispatch(a, c):
        first = pl.multiple_of((((me >> 2) + c) & 3) * (4 * CAP), 4 * CAP)
        rows = pl.ds(first, 4 * CAP)
        r = lax.broadcasted_iota(jnp.int32, (4 * CAP, 128), 0) + first
        source = div48(r)
        ids = (source * (OWN * CAP) + (r - source * CAP) + a * CAP).astype(F32)
        hot = one_hot(jnp.concatenate([ids] * tiles, axis=1) == rows_ref[0:1, :])
        fsend[a, rows, : 3 * HS] = dot(hot, x_proj[...]).astype(BF16)
        fsend[a, rows, 3 * HS :] = dot(hot, x_grad[...]).astype(BF16)

    def ship(a, c):
        @pl.when(c == 0)
        def _():
            frecv[a, block(me), :] = fsend[a, block(me), :]

        @pl.loop(0, 4)
        def _(x):
            @pl.when(c * 4 + x > 0)
            def _():
                fwd_copy(a, c * 4 + x).start()

    dispatch(0, 0)
    pl.semaphore_wait(barrier, PEERS + 1)
    ship(0, 0)

    @pl.loop(1, 4)
    def _(n):
        dispatch(0, n)
        ship(0, n)

    lane_route = lax.broadcasted_iota(jnp.int32, (8, routes), 1)
    position = (lane_route >> 3) + (here * PEERS + me) * tokens
    docs = jnp.ones((8, routes), F32)
    lengths_in.wait()
    end = lengths_ref[0]
    for n in range(lengths_ref.shape[0]):
        docs = docs + jnp.where(position >= end, 1.0, 0.0)
        if n + 1 < lengths_ref.shape[0]:
            end = end + lengths_ref[n + 1]
    row = lax.broadcasted_iota(jnp.int32, (256, 128), 0)
    row_head = (4 * (row >> 4) + (row & 3)).astype(F32)
    at_head = jnp.concatenate([row_head] * tiles, axis=1) == rows_ref[1:2, :]
    docs_wide = jnp.where(at_head, docs[0:1, :], 0.0).astype(BF16)
    lane_slot = lax.broadcasted_iota(jnp.int32, (128, 128), 0).astype(F32)
    at_slot = one_hot(jnp.concatenate([lane_slot] * tiles, axis=1) == rows_ref[2:3, :])
    doc_send[...] = dot_nt(docs_wide, at_slot).astype(BF16)
    doc_recv[doc_rows(me), :] = doc_send[doc_rows(me), :]

    @pl.loop(1, PEERS)
    def _(d):
        doc_copy(d).start()

    def take_head(a):
        @pl.loop(1, PEERS)
        def _(d):
            fwd_copy(a, d).wait_recv()

        kv_copy(a).start()

    @pl.loop(0, routes // 256)
    def _(c):
        rows = pl.ds(pl.multiple_of(c * 256, 256), 256)
        f = lax.broadcasted_iota(jnp.int32, (count, 128), 0)
        dest_ref[rows, :] = dot(mixed_ref[rows, :], dest_weight(f))

    @pl.loop(4, 4 * OWN)
    def _(n):
        dispatch(n >> 2, n & 3)
        ship(n >> 2, n & 3)

    @pl.loop(1, PEERS)
    def _(d):
        doc_copy(d).wait_recv()

    doc_shift.start()
    take_head(0)

    def head_docs(a, docs_ref):
        r = lax.broadcasted_iota(jnp.int32, (SPAN, 128), 0)
        lane = lax.broadcasted_iota(jnp.int32, (SPAN, 128), 1)
        source = div48(r)
        wanted = source * 16 + a
        pick = one_hot(jnp.concatenate([lane, lane + 128], axis=1) == jnp.concatenate([wanted] * 2, axis=1))
        spread = dot(pick, docs_ref[...])
        return jnp.where(lane == r - source * CAP, spread, 0.0).astype(BF16)

    def finish(a):
        d_copy(a).wait_recv()
        dk = dk_acc[a, SPAN:, :] * scaling + drecv[a, :, :HS].astype(F32)
        dv = dv_acc[a, SPAN:, :] + drecv[a, :, HS:].astype(F32)
        rsend[a, 1, :, :HS] = dk.astype(BF16)
        rsend[a, 1, :, HS:] = dv.astype(BF16)
        send_home(a, 1)

    def attention(a):
        k_all[:SPAN, :] = kv_prev[a, :, :HS]
        v_all[:SPAN, :] = kv_prev[a, :, HS:]
        k_all[SPAN:, :] = frecv[a, :, HS : 2 * HS]
        v_all[SPAN:, :] = frecv[a, :, 2 * HS : 3 * HS]
        k_t[...] = k_all[...].T
        v_t[...] = v_all[...].T
        ones = jnp.ones((HS, HS), BF16)
        mine = head_docs(a, doc_recv)
        key_docs[:SPAN, :] = dot(head_docs(a, doc_prev), ones)
        key_docs[SPAN:, :] = dot(mine, ones)
        query_docs[...] = dot_nt(ones[:8], mine)
        dk_acc[a] = jnp.zeros((2 * SPAN, HS), F32)
        dv_acc[a] = jnp.zeros((2 * SPAN, HS), F32)

        for i in range(SPAN // QT):
            if i == 1:

                @pl.when(a < OWN - 1)
                def _():
                    take_head(a + 1)

            if i == 2:

                @pl.when(a > 0)
                def _():
                    finish(a - 1)

            first = i * QT
            left = first // CAP * CAP
            right = SPAN + first + QT
            start = left // 128 * 128
            skip = left - start
            cuts = [min(left + c * KC, right) for c in range((right - left - 1) // KC + 2)]
            chunks = list(zip(cuts, cuts[1:]))
            if skip:
                p_buf[:skip, :] = jnp.zeros((skip, QT), BF16)
                ds_buf[:skip, :] = jnp.zeros((skip, QT), BF16)
            q = frecv[a, first : first + QT, :HS]
            out_grad = frecv[a, first : first + QT, 3 * HS :]
            q_docs = query_docs[0:1, first : first + QT]
            top = jnp.full((1, QT), MASKED, F32)
            for low, high in chunks:
                s = dot_nt(k_all[low:high, :], q) * (scaling * math.log2(math.e))
                docs = key_docs[low:high, :]
                seen = jnp.concatenate([docs, docs], axis=1) == q_docs
                if high > SPAN + first:
                    k_at = lax.broadcasted_iota(jnp.int32, s.shape, 0) + (low - SPAN)
                    q_at = lax.broadcasted_iota(jnp.int32, s.shape, 1) + first
                    seen = seen & (k_at <= q_at)
                s = jnp.where(seen, s, MASKED)
                s_buf[low - start : high - start, :] = s
                top = jnp.maximum(top, jnp.max(s, axis=0, keepdims=True))
            total = jnp.zeros((1, QT), F32)
            for low, high in chunks:
                part = slice(low - start, high - start)
                p = jnp.exp2(s_buf[part, :] - top)
                total = total + jnp.sum(p, axis=0, keepdims=True)
                s_buf[part, :] = p
                p_buf[part, :] = p.astype(BF16)
            inverse = 1.0 / total
            attended = (dot(v_t[:, start:right], p_buf[: right - start, :]) * inverse).astype(BF16)
            out_grad_t = (out_grad.astype(F32).T * inverse).astype(BF16)
            delta = jnp.sum(out_grad_t.astype(F32) * attended.astype(F32), axis=0, keepdims=True)
            for low, high in chunks:
                part = slice(low - start, high - start)
                dp = dot(v_all[low:high, :], out_grad_t)
                ds = (s_buf[part, :] * (dp - delta)).astype(BF16)
                ds_buf[part, :] = ds
                dv_acc[a, low:high, :] += dot_nt(p_buf[part, :], out_grad_t)
                dk_acc[a, low:high, :] += dot(ds, q)
            dq = dot(k_t[:, start:right], ds_buf[: right - start, :]) * scaling
            rsend[a, 0, first : first + QT, :HS] = attended.astype(F32).T.astype(BF16)
            rsend[a, 0, first : first + QT, HS:] = dq.T.astype(BF16)

        dsend[a, :, :HS] = (dk_acc[a, :SPAN, :] * scaling).astype(BF16)
        dsend[a, :, HS:] = dv_acc[a, :SPAN, :].astype(BF16)
        d_copy(a).start()
        send_home(a, 0)

    doc_shift.wait_recv()

    @pl.loop(0, OWN)
    def _(a):
        kv_copy(a).wait_recv()
        attention(a)

    def await_half(a, half):
        @pl.loop(1, PEERS)
        def _(d):
            ret_copy(a, half, d).wait_recv()

    def combine(a):
        await_half(a, 0)
        await_half(a, 1)

        @pl.loop(0, routes // 256)
        def _(c):
            rows = pl.ds(pl.multiple_of(c * 256, 256), 256)
            hot = chosen(dest_ref[rows, :], head_slots(a))
            more = jnp.concatenate([dot(hot, rrecv[a, 0]), dot(hot, rrecv[a, 1])], axis=1)

            @pl.when(a == 0)
            def _():
                out_acc[rows, :] = more.astype(BF16)

            @pl.when(a > 0)
            def _():
                out_acc[rows, :] = (out_acc[rows, :].astype(F32) + more).astype(BF16)

    @pl.loop(0, OWN - 1)
    def _(a):
        @pl.when(a == 1)
        def _():
            finish(OWN - 1)

        combine(a)

    await_half(OWN - 1, 0)

    @pl.loop(0, routes // 256)
    def _(c):
        rows = pl.ds(pl.multiple_of(c * 256, 256), 256)
        hot = chosen(dest_ref[rows, :], head_slots(OWN - 1))
        more = dot(hot, rrecv[OWN - 1, 0])
        out_acc[rows, : 2 * HS] = (out_acc[rows, : 2 * HS].astype(F32) + more).astype(BF16)

    @pl.loop(1, PEERS)
    def _(d):
        doc_copy(d).wait_send()

    doc_shift.wait_send()

    @pl.loop(0, OWN)
    def _(a):
        @pl.loop(1, PEERS)
        def _(d):
            fwd_copy(a, d).wait_send()

        kv_copy(a).wait_send()
        d_copy(a).wait_send()

    @pl.loop(0, OWN)
    def _(a):
        @pl.loop(1, PEERS)
        def _(d):
            ret_copy(a, 0, d).wait_send()
            ret_copy(a, 1, d).wait_send()

    await_half(OWN - 1, 1)


def home_kernel(
    routes_ref,
    last_ref,
    dest_ref,
    gate_ref,
    cot_ref,
    logits_ref,
    head_out_hbm,
    proj_out_hbm,
    grad_out,
    out_head,
    out_proj,
    out_sem,
):
    tokens = logits_ref.shape[1]
    late = head_slots(OWN - 1)
    lane = lax.broadcasted_iota(jnp.int32, (8, HS), 1)
    eye = one_hot(lax.broadcasted_iota(jnp.int32, (8, HS), 0) == lane)
    grads = jnp.zeros((8, tokens), F32)
    copies = []
    for c in range(routes_ref.shape[0] // 256):
        rows = pl.ds(c * 256, 256)
        hot = chosen(dest_ref[rows, :], late)
        rest = routes_ref[rows, 2 * HS :].astype(F32) + dot(hot, last_ref[OWN - 1, 1])
        out_proj[rows, :HS] = routes_ref[rows, HS : 2 * HS]
        out_proj[rows, HS:] = rest.astype(BF16)
        attended = routes_ref[rows, :HS].astype(F32)
        out_head[rows, :] = (attended * gate_ref[rows, :]).astype(BF16)
        for n, (source, target) in enumerate(((out_head, head_out_hbm), (out_proj, proj_out_hbm))):
            copies.append(pltpu.make_async_copy(source.at[rows], target.at[rows], out_sem.at[c, n]))
            copies[-1].start()
        inner = jnp.sum(cot_ref[rows, :].astype(F32) * attended, axis=1, keepdims=True)
        r = lax.broadcasted_iota(jnp.int32, (256, HS), 0)
        lane = lax.broadcasted_iota(jnp.int32, (256, HS), 1)
        dots = jnp.where((r & 7) == lane, inner, 0.0)
        by_route = sum(dot_nt(eye, part.astype(BF16)) for part in thirds(dots))
        hot = token_rows(c, tokens)
        grads = grads + sum(dot(part.astype(BF16), hot) for part in thirds(by_route))
    gate = 1.0 / (1.0 + jnp.exp(-logits_ref[...]))
    grad_out[...] = grads * gate * (1.0 - gate)
    for copy in copies:
        copy.wait()


def per_device(projections, routed_heads, slot_index, gate_logits, doc_lengths, cotangent):
    tokens, top, width = projections.shape
    routes = tokens * top
    dma = pltpu.SemaphoreType.DMA
    vmem = pltpu.VMEM
    whole = pl.BlockSpec(memory_space=pltpu.VMEM)
    hbm = pl.BlockSpec(memory_space=pltpu.HBM)
    cot_rows = cotangent.reshape(routes, HS)
    logits = gate_logits.T
    handed = pl.pallas_call(
        kernel,
        out_shape=(
            jax.ShapeDtypeStruct((routes, WIDE), BF16),
            jax.ShapeDtypeStruct((OWN, 2, SPAN, 2 * HS), BF16),
            jax.ShapeDtypeStruct((routes, HS), F32),
            jax.ShapeDtypeStruct((routes, HS), F32),
        ),
        in_specs=[hbm, hbm, whole, whole, whole, hbm],
        out_specs=(whole, whole, whole, whole),
        scratch_shapes=[
            pltpu.SMEM(doc_lengths.shape, jnp.int32),
            vmem((routes, 3 * HS), BF16),
            vmem((routes, HS), BF16),
            vmem((routes, HS), BF16),
            vmem((routes, 5 * top), BF16),
            vmem((8, routes), F32),
            vmem((OWN, SPAN, WIDE), BF16),
            vmem((OWN, SPAN, WIDE), BF16),
            vmem((PEERS * 16, 128), BF16),
            vmem((PEERS * 16, 128), BF16),
            vmem((PEERS * 16, 128), BF16),
            vmem((OWN, SPAN, 2 * HS), BF16),
            vmem((OWN, SPAN, 2 * HS), BF16),
            vmem((OWN, SPAN, 2 * HS), BF16),
            vmem((OWN, 2, SPAN, 2 * HS), BF16),
            vmem((2 * SPAN, HS), BF16),
            vmem((2 * SPAN, HS), BF16),
            vmem((HS, 2 * SPAN), BF16),
            vmem((HS, 2 * SPAN), BF16),
            vmem((2 * SPAN, HS), F32),
            vmem((8, SPAN), F32),
            vmem((WIN, QT), F32),
            vmem((WIN, QT), BF16),
            vmem((WIN, QT), BF16),
            vmem((OWN, 2 * SPAN, HS), F32),
            vmem((OWN, 2 * SPAN, HS), F32),
            dma((OWN, PEERS)),
            dma((OWN, PEERS)),
            dma((PEERS,)),
            dma((PEERS,)),
            dma((2,)),
            dma((OWN,)),
            dma((OWN,)),
            dma((OWN,)),
            dma((OWN,)),
            dma((OWN, 2, PEERS)),
            dma((OWN, 2, PEERS)),
            dma((3,)),
        ],
        compiler_params=pltpu.CompilerParams(
            collective_id=0, has_side_effects=True, vmem_limit_bytes=44000 * 1024
        ),
    )(
        *(
            pltpu.with_memory_space_constraint(v, pltpu.HBM)
            for v in (
                projections.reshape(routes, width),
                cot_rows,
                routed_heads.T,
                slot_index.T,
                logits,
                doc_lengths,
            )
        ),
    )
    head_outputs, projection_grads, gate_grads = pl.pallas_call(
        home_kernel,
        out_shape=(
            jax.ShapeDtypeStruct((routes, HS), BF16),
            jax.ShapeDtypeStruct((routes, 3 * HS), BF16),
            jax.ShapeDtypeStruct((top, tokens), F32),
        ),
        in_specs=[whole] * 6,
        out_specs=(hbm, hbm, whole),
        scratch_shapes=[
            vmem((routes, HS), BF16),
            vmem((routes, 3 * HS), BF16),
            dma((routes // 256, 2)),
        ],
        compiler_params=pltpu.CompilerParams(vmem_limit_bytes=16000 * 1024),
    )(*handed, cot_rows, logits)
    return (
        head_outputs.reshape(tokens, top, HS),
        projection_grads.reshape(tokens, top, width),
        gate_grads.T,
    )


def solution(mesh):
    tokens = P(("seq", "head"), None, None)
    routes = P(("seq", "head"), None)
    return jax.shard_map(
        per_device,
        mesh=mesh,
        in_specs=(tokens, routes, routes, routes, P(), tokens),
        out_specs=(tokens, tokens, routes),
        check_vma=False,
    )
```

```python
import math

import jax
import jax.numpy as jnp
from jax import lax
from jax.experimental import pallas as pl
from jax.experimental.pallas import tpu as pltpu
from jax.sharding import PartitionSpec as P

H = 64
CAP = 48
OWN = 4
PEERS = 16
SPAN = PEERS * CAP
HS = 128
WIDE = 4 * HS
QT = 256
WIN = 1152
KC = 544
MASKED = -1e30
F32 = jnp.float32
BF16 = jnp.bfloat16
MESH = pl.DeviceIdType.MESH


def dot_nt(a, b):
    return lax.dot_general(a, b, (((1,), (1,)), ((), ())), preferred_element_type=F32)


def dot(a, b):
    return jnp.dot(a, b, preferred_element_type=F32)


def one_hot(mask):
    return jnp.where(mask, 1.0, 0.0).astype(BF16)


def thirds(v):
    high = v.astype(BF16).astype(F32)
    middle = (v - high).astype(BF16).astype(F32)
    return [high, middle, v - high - middle]


def dest_weight(f):
    return jnp.where(f < 8, float(CAP), jnp.where(f < 16, 1.0, 0.0)).astype(BF16)


def div48(v):
    return (v * 1366) >> 16


def token_rows(c, tokens):
    r = lax.broadcasted_iota(jnp.int32, (256, tokens), 0)
    t = lax.broadcasted_iota(jnp.int32, (256, tokens), 1)
    return one_hot((r >> 3) + c * 32 == t)


def head_slots(a):
    lane = lax.broadcasted_iota(jnp.int32, (8, SPAN), 1)
    source = div48(lane)
    return (source * (OWN * CAP) + (lane - source * CAP) + a * CAP).astype(F32)


def chosen(dest, ids):
    return one_hot(jnp.concatenate([dest] * (ids.shape[1] // 128), axis=1) == ids[0:1, :])


def kernel(
    proj_hbm,
    cot_hbm,
    heads_ref,
    slots_ref,
    logits_ref,
    lengths_hbm,
    out_acc,
    rrecv,
    dest_ref,
    gate_ref,
    lengths_ref,
    x_proj,
    x_cot,
    x_grad,
    mixed_ref,
    rows_ref,
    fsend,
    frecv,
    doc_send,
    doc_recv,
    doc_prev,
    kv_prev,
    dsend,
    drecv,
    rsend,
    k_all,
    v_all,
    k_t,
    v_t,
    key_docs,
    query_docs,
    s_buf,
    p_buf,
    ds_buf,
    dk_acc,
    dv_acc,
    f_ssem,
    f_rsem,
    doc_ssem,
    doc_rsem,
    dp_sem,
    kv_ssem,
    kv_rsem,
    d_ssem,
    d_rsem,
    r_ssem,
    r_rsem,
    in_sem,
):
    me = lax.axis_index("head")
    here = lax.axis_index("seq")
    after = (here + 1) & (PEERS - 1)
    before = (here + PEERS - 1) & (PEERS - 1)
    routes = proj_hbm.shape[0]
    tokens = heads_ref.shape[1]
    tiles = routes // 128
    scaling = HS ** (-0.5)
    proj_in = pltpu.make_async_copy(proj_hbm, x_proj, in_sem.at[0])
    cot_in = pltpu.make_async_copy(cot_hbm, x_cot, in_sem.at[1])
    lengths_in = pltpu.make_async_copy(lengths_hbm, lengths_ref, in_sem.at[2])
    cot_in.start()
    proj_in.start()
    lengths_in.start()

    barrier = pltpu.get_barrier_semaphore()

    def peer_of(d):
        px = (me + d) & 3
        py = ((me >> 2) + (d >> 2)) & 3
        return py * 4 + px

    @pl.loop(1, PEERS)
    def _(d):
        pl.semaphore_signal(barrier, inc=1, device_id={"head": peer_of(d)}, device_id_type=MESH)

    pl.semaphore_signal(barrier, inc=1, device_id={"seq": after}, device_id_type=MESH)
    pl.semaphore_signal(barrier, inc=1, device_id={"seq": before}, device_id_type=MESH)

    def block(i):
        return pl.ds(pl.multiple_of(i * CAP, CAP), CAP)

    def fwd_copy(a, d):
        peer = peer_of(d)
        return pltpu.make_async_remote_copy(
            src_ref=fsend.at[a, block(peer)],
            dst_ref=frecv.at[a, block(me)],
            send_sem=f_ssem.at[a, d],
            recv_sem=f_rsem.at[a, d],
            device_id={"head": peer},
            device_id_type=MESH,
        )

    def ret_copy(a, half, d):
        peer = peer_of(d)
        return pltpu.make_async_remote_copy(
            src_ref=rsend.at[a, half, block(peer)],
            dst_ref=rrecv.at[a, half, block(me)],
            send_sem=r_ssem.at[a, half, d],
            recv_sem=r_rsem.at[a, half, d],
            device_id={"head": peer},
            device_id_type=MESH,
        )

    def send_home(a, half):
        @pl.loop(1, PEERS)
        def _(d):
            ret_copy(a, half, d).start()

        rrecv[a, half, block(me), :] = rsend[a, half, block(me), :]

    def doc_rows(i):
        return pl.ds(pl.multiple_of(i * 16, 16), 16)

    def doc_copy(d):
        peer = peer_of(d)
        return pltpu.make_async_remote_copy(
            src_ref=doc_send.at[doc_rows(peer)],
            dst_ref=doc_recv.at[doc_rows(me)],
            send_sem=doc_ssem.at[d],
            recv_sem=doc_rsem.at[d],
            device_id={"head": peer},
            device_id_type=MESH,
        )

    doc_shift = pltpu.make_async_remote_copy(
        src_ref=doc_recv,
        dst_ref=doc_prev,
        send_sem=dp_sem.at[0],
        recv_sem=dp_sem.at[1],
        device_id={"seq": after},
        device_id_type=MESH,
    )

    def kv_copy(a):
        return pltpu.make_async_remote_copy(
            src_ref=frecv.at[a, :, pl.ds(HS, 2 * HS)],
            dst_ref=kv_prev.at[a],
            send_sem=kv_ssem.at[a],
            recv_sem=kv_rsem.at[a],
            device_id={"seq": after},
            device_id_type=MESH,
        )

    def d_copy(a):
        return pltpu.make_async_remote_copy(
            src_ref=dsend.at[a],
            dst_ref=drecv.at[a],
            send_sem=d_ssem.at[a],
            recv_sem=d_rsem.at[a],
            device_id={"seq": before},
            device_id_type=MESH,
        )

    gate = 1.0 / (1.0 + jnp.exp(-logits_ref[...]))
    pieces = thirds(gate)
    fields = jnp.concatenate(
        [heads_ref[...].astype(F32), slots_ref[...].astype(F32)] + pieces, axis=0
    ).astype(BF16)
    count = fields.shape[0]

    for c in range(routes // 256):
        rows = pl.ds(c * 256, 256)
        mixed = dot_nt(token_rows(c, tokens), fields)
        r = lax.broadcasted_iota(jnp.int32, (256, count), 0)
        f = lax.broadcasted_iota(jnp.int32, (256, count), 1)
        mixed = jnp.where((r & 7) == (f & 7), mixed, 0.0).astype(BF16)
        mixed_ref[rows, :] = mixed
        f = lax.broadcasted_iota(jnp.int32, (count, 128), 0)
        gate_ref[rows, :] = dot(mixed, one_hot(f >= 16))
        f = lax.broadcasted_iota(jnp.int32, (8, count), 1)
        want = lax.broadcasted_iota(jnp.int32, (8, count), 0)
        as_head = (want == 1) & (f < 8)
        as_slot = (want == 2) & (f >= 8) & (f < 16)
        weight = jnp.where(want == 0, dest_weight(f).astype(F32), jnp.where(as_head | as_slot, 1.0, 0.0))
        rows_ref[:, rows] = dot_nt(weight.astype(BF16), mixed)

    cot_in.wait()
    for c in range(routes // 256):
        rows = pl.ds(c * 256, 256)
        x_grad[rows, :] = (x_cot[rows, :].astype(F32) * gate_ref[rows, :]).astype(BF16)

    proj_in.wait()

    def dispatch(a, c):
        first = pl.multiple_of((((me >> 2) + c) & 3) * (4 * CAP), 4 * CAP)
        rows = pl.ds(first, 4 * CAP)
        r = lax.broadcasted_iota(jnp.int32, (4 * CAP, 128), 0) + first
        source = div48(r)
        ids = (source * (OWN * CAP) + (r - source * CAP) + a * CAP).astype(F32)
        hot = one_hot(jnp.concatenate([ids] * tiles, axis=1) == rows_ref[0:1, :])
        fsend[a, rows, : 3 * HS] = dot(hot, x_proj[...]).astype(BF16)
        fsend[a, rows, 3 * HS :] = dot(hot, x_grad[...]).astype(BF16)

    def ship(a, c):
        @pl.when(c == 0)
        def _():
            frecv[a, block(me), :] = fsend[a, block(me), :]

        @pl.loop(0, 4)
        def _(x):
            @pl.when(c * 4 + x > 0)
            def _():
                fwd_copy(a, c * 4 + x).start()

    dispatch(0, 0)
    pl.semaphore_wait(barrier, PEERS + 1)
    ship(0, 0)

    @pl.loop(1, 4)
    def _(n):
        dispatch(0, n)
        ship(0, n)

    lane_route = lax.broadcasted_iota(jnp.int32, (8, routes), 1)
    position = (lane_route >> 3) + (here * PEERS + me) * tokens
    docs = jnp.ones((8, routes), F32)
    lengths_in.wait()
    end = lengths_ref[0]
    for n in range(lengths_ref.shape[0]):
        docs = docs + jnp.where(position >= end, 1.0, 0.0)
        if n + 1 < lengths_ref.shape[0]:
            end = end + lengths_ref[n + 1]
    row = lax.broadcasted_iota(jnp.int32, (256, 128), 0)
    row_head = (4 * (row >> 4) + (row & 3)).astype(F32)
    at_head = jnp.concatenate([row_head] * tiles, axis=1) == rows_ref[1:2, :]
    docs_wide = jnp.where(at_head, docs[0:1, :], 0.0).astype(BF16)
    lane_slot = lax.broadcasted_iota(jnp.int32, (128, 128), 0).astype(F32)
    at_slot = one_hot(jnp.concatenate([lane_slot] * tiles, axis=1) == rows_ref[2:3, :])
    doc_send[...] = dot_nt(docs_wide, at_slot).astype(BF16)
    doc_recv[doc_rows(me), :] = doc_send[doc_rows(me), :]

    @pl.loop(1, PEERS)
    def _(d):
        doc_copy(d).start()

    def take_head(a):
        @pl.loop(1, PEERS)
        def _(d):
            fwd_copy(a, d).wait_recv()

        kv_copy(a).start()

    @pl.loop(0, routes // 256)
    def _(c):
        rows = pl.ds(pl.multiple_of(c * 256, 256), 256)
        f = lax.broadcasted_iota(jnp.int32, (count, 128), 0)
        dest_ref[rows, :] = dot(mixed_ref[rows, :], dest_weight(f))

    @pl.loop(4, 4 * OWN)
    def _(n):
        dispatch(n >> 2, n & 3)
        ship(n >> 2, n & 3)

    @pl.loop(1, PEERS)
    def _(d):
        doc_copy(d).wait_recv()

    doc_shift.start()
    take_head(0)

    def head_docs(a, docs_ref):
        r = lax.broadcasted_iota(jnp.int32, (SPAN, 128), 0)
        lane = lax.broadcasted_iota(jnp.int32, (SPAN, 128), 1)
        source = div48(r)
        wanted = source * 16 + a
        pick = one_hot(jnp.concatenate([lane, lane + 128], axis=1) == jnp.concatenate([wanted] * 2, axis=1))
        spread = dot(pick, docs_ref[...])
        return jnp.where(lane == r - source * CAP, spread, 0.0).astype(BF16)

    def finish(a):
        d_copy(a).wait_recv()
        dk = dk_acc[a, SPAN:, :] * scaling + drecv[a, :, :HS].astype(F32)
        dv = dv_acc[a, SPAN:, :] + drecv[a, :, HS:].astype(F32)
        rsend[a, 1, :, :HS] = dk.astype(BF16)
        rsend[a, 1, :, HS:] = dv.astype(BF16)
        send_home(a, 1)

    def attention(a):
        k_all[:SPAN, :] = kv_prev[a, :, :HS]
        v_all[:SPAN, :] = kv_prev[a, :, HS:]
        k_all[SPAN:, :] = frecv[a, :, HS : 2 * HS]
        v_all[SPAN:, :] = frecv[a, :, 2 * HS : 3 * HS]
        k_t[...] = k_all[...].T
        v_t[...] = v_all[...].T
        ones = jnp.ones((HS, HS), BF16)
        mine = head_docs(a, doc_recv)
        key_docs[:SPAN, :] = dot(head_docs(a, doc_prev), ones)
        key_docs[SPAN:, :] = dot(mine, ones)
        query_docs[...] = dot_nt(ones[:8], mine)
        dk_acc[a] = jnp.zeros((2 * SPAN, HS), F32)
        dv_acc[a] = jnp.zeros((2 * SPAN, HS), F32)

        for i in range(SPAN // QT):
            if i == 1:

                @pl.when(a < OWN - 1)
                def _():
                    take_head(a + 1)

            if i == 2:

                @pl.when(a > 0)
                def _():
                    finish(a - 1)

            first = i * QT
            left = first // CAP * CAP
            right = SPAN + first + QT
            start = left // 128 * 128
            skip = left - start
            cuts = [min(left + c * KC, right) for c in range((right - left - 1) // KC + 2)]
            chunks = list(zip(cuts, cuts[1:]))
            if skip:
                p_buf[:skip, :] = jnp.zeros((skip, QT), BF16)
                ds_buf[:skip, :] = jnp.zeros((skip, QT), BF16)
            q = frecv[a, first : first + QT, :HS]
            out_grad = frecv[a, first : first + QT, 3 * HS :]
            q_docs = query_docs[0:1, first : first + QT]
            top = jnp.full((1, QT), MASKED, F32)
            for low, high in chunks:
                s = dot_nt(k_all[low:high, :], q) * (scaling * math.log2(math.e))
                docs = key_docs[low:high, :]
                seen = jnp.concatenate([docs, docs], axis=1) == q_docs
                if high > SPAN + first:
                    k_at = lax.broadcasted_iota(jnp.int32, s.shape, 0) + (low - SPAN)
                    q_at = lax.broadcasted_iota(jnp.int32, s.shape, 1) + first
                    seen = seen & (k_at <= q_at)
                s = jnp.where(seen, s, MASKED)
                s_buf[low - start : high - start, :] = s
                top = jnp.maximum(top, jnp.max(s, axis=0, keepdims=True))
            total = jnp.zeros((1, QT), F32)
            for low, high in chunks:
                part = slice(low - start, high - start)
                p = jnp.exp2(s_buf[part, :] - top)
                total = total + jnp.sum(p, axis=0, keepdims=True)
                s_buf[part, :] = p
                p_buf[part, :] = p.astype(BF16)
            inverse = 1.0 / total
            attended = (dot(v_t[:, start:right], p_buf[: right - start, :]) * inverse).astype(BF16)
            out_grad_t = (out_grad.astype(F32).T * inverse).astype(BF16)
            delta = jnp.sum(out_grad_t.astype(F32) * attended.astype(F32), axis=0, keepdims=True)
            for low, high in chunks:
                part = slice(low - start, high - start)
                dp = dot(v_all[low:high, :], out_grad_t)
                ds = (s_buf[part, :] * (dp - delta)).astype(BF16)
                ds_buf[part, :] = ds
                dv_acc[a, low:high, :] += dot_nt(p_buf[part, :], out_grad_t)
                dk_acc[a, low:high, :] += dot(ds, q)
            dq = dot(k_t[:, start:right], ds_buf[: right - start, :]) * scaling
            rsend[a, 0, first : first + QT, :HS] = attended.astype(F32).T.astype(BF16)
            rsend[a, 0, first : first + QT, HS:] = dq.T.astype(BF16)

        dsend[a, :, :HS] = (dk_acc[a, :SPAN, :] * scaling).astype(BF16)
        dsend[a, :, HS:] = dv_acc[a, :SPAN, :].astype(BF16)
        d_copy(a).start()
        send_home(a, 0)

    doc_shift.wait_recv()

    @pl.loop(0, OWN)
    def _(a):
        kv_copy(a).wait_recv()
        attention(a)

    def await_half(a, half):
        @pl.loop(1, PEERS)
        def _(d):
            ret_copy(a, half, d).wait_recv()

    def combine(a):
        await_half(a, 0)
        await_half(a, 1)

        @pl.loop(0, routes // 256)
        def _(c):
            rows = pl.ds(pl.multiple_of(c * 256, 256), 256)
            hot = chosen(dest_ref[rows, :], head_slots(a))
            more = jnp.concatenate([dot(hot, rrecv[a, 0]), dot(hot, rrecv[a, 1])], axis=1)

            @pl.when(a == 0)
            def _():
                out_acc[rows, :] = more.astype(BF16)

            @pl.when(a > 0)
            def _():
                out_acc[rows, :] = (out_acc[rows, :].astype(F32) + more).astype(BF16)

    @pl.loop(0, OWN - 1)
    def _(a):
        @pl.when(a == OWN - 2)
        def _():
            finish(OWN - 1)

        combine(a)

    await_half(OWN - 1, 0)

    @pl.loop(0, routes // 256)
    def _(c):
        rows = pl.ds(pl.multiple_of(c * 256, 256), 256)
        hot = chosen(dest_ref[rows, :], head_slots(OWN - 1))
        more = dot(hot, rrecv[OWN - 1, 0])
        out_acc[rows, : 2 * HS] = (out_acc[rows, : 2 * HS].astype(F32) + more).astype(BF16)

    @pl.loop(1, PEERS)
    def _(d):
        doc_copy(d).wait_send()

    doc_shift.wait_send()

    @pl.loop(0, OWN)
    def _(a):
        @pl.loop(1, PEERS)
        def _(d):
            fwd_copy(a, d).wait_send()

        kv_copy(a).wait_send()
        d_copy(a).wait_send()

    @pl.loop(0, OWN)
    def _(a):
        @pl.loop(1, PEERS)
        def _(d):
            ret_copy(a, 0, d).wait_send()
            ret_copy(a, 1, d).wait_send()

    await_half(OWN - 1, 1)


def home_kernel(
    routes_ref,
    last_ref,
    dest_ref,
    gate_ref,
    cot_ref,
    logits_ref,
    head_out_hbm,
    proj_out_hbm,
    grad_out,
    out_head,
    out_proj,
    out_sem,
):
    tokens = logits_ref.shape[1]
    late = head_slots(OWN - 1)
    lane = lax.broadcasted_iota(jnp.int32, (8, HS), 1)
    eye = one_hot(lax.broadcasted_iota(jnp.int32, (8, HS), 0) == lane)
    grads = jnp.zeros((8, tokens), F32)
    copies = []
    for c in range(routes_ref.shape[0] // 256):
        rows = pl.ds(c * 256, 256)
        hot = chosen(dest_ref[rows, :], late)
        rest = routes_ref[rows, 2 * HS :].astype(F32) + dot(hot, last_ref[OWN - 1, 1])
        out_proj[rows, :HS] = routes_ref[rows, HS : 2 * HS]
        out_proj[rows, HS:] = rest.astype(BF16)
        attended = routes_ref[rows, :HS].astype(F32)
        out_head[rows, :] = (attended * gate_ref[rows, :]).astype(BF16)
        for n, (source, target) in enumerate(((out_head, head_out_hbm), (out_proj, proj_out_hbm))):
            copies.append(pltpu.make_async_copy(source.at[rows], target.at[rows], out_sem.at[c, n]))
            copies[-1].start()
        inner = jnp.sum(cot_ref[rows, :].astype(F32) * attended, axis=1, keepdims=True)
        r = lax.broadcasted_iota(jnp.int32, (256, HS), 0)
        lane = lax.broadcasted_iota(jnp.int32, (256, HS), 1)
        dots = jnp.where((r & 7) == lane, inner, 0.0)
        by_route = sum(dot_nt(eye, part.astype(BF16)) for part in thirds(dots))
        hot = token_rows(c, tokens)
        grads = grads + sum(dot(part.astype(BF16), hot) for part in thirds(by_route))
    gate = 1.0 / (1.0 + jnp.exp(-logits_ref[...]))
    grad_out[...] = grads * gate * (1.0 - gate)
    for copy in copies:
        copy.wait()


def per_device(projections, routed_heads, slot_index, gate_logits, doc_lengths, cotangent):
    tokens, top, width = projections.shape
    routes = tokens * top
    dma = pltpu.SemaphoreType.DMA
    vmem = pltpu.VMEM
    whole = pl.BlockSpec(memory_space=pltpu.VMEM)
    hbm = pl.BlockSpec(memory_space=pltpu.HBM)
    cot_rows = cotangent.reshape(routes, HS)
    logits = gate_logits.T
    handed = pl.pallas_call(
        kernel,
        out_shape=(
            jax.ShapeDtypeStruct((routes, WIDE), BF16),
            jax.ShapeDtypeStruct((OWN, 2, SPAN, 2 * HS), BF16),
            jax.ShapeDtypeStruct((routes, HS), F32),
            jax.ShapeDtypeStruct((routes, HS), F32),
        ),
        in_specs=[hbm, hbm, whole, whole, whole, hbm],
        out_specs=(whole, whole, whole, whole),
        scratch_shapes=[
            pltpu.SMEM(doc_lengths.shape, jnp.int32),
            vmem((routes, 3 * HS), BF16),
            vmem((routes, HS), BF16),
            vmem((routes, HS), BF16),
            vmem((routes, 5 * top), BF16),
            vmem((8, routes), F32),
            vmem((OWN, SPAN, WIDE), BF16),
            vmem((OWN, SPAN, WIDE), BF16),
            vmem((PEERS * 16, 128), BF16),
            vmem((PEERS * 16, 128), BF16),
            vmem((PEERS * 16, 128), BF16),
            vmem((OWN, SPAN, 2 * HS), BF16),
            vmem((OWN, SPAN, 2 * HS), BF16),
            vmem((OWN, SPAN, 2 * HS), BF16),
            vmem((OWN, 2, SPAN, 2 * HS), BF16),
            vmem((2 * SPAN, HS), BF16),
            vmem((2 * SPAN, HS), BF16),
            vmem((HS, 2 * SPAN), BF16),
            vmem((HS, 2 * SPAN), BF16),
            vmem((2 * SPAN, HS), F32),
            vmem((8, SPAN), F32),
            vmem((WIN, QT), F32),
            vmem((WIN, QT), BF16),
            vmem((WIN, QT), BF16),
            vmem((OWN, 2 * SPAN, HS), F32),
            vmem((OWN, 2 * SPAN, HS), F32),
            dma((OWN, PEERS)),
            dma((OWN, PEERS)),
            dma((PEERS,)),
            dma((PEERS,)),
            dma((2,)),
            dma((OWN,)),
            dma((OWN,)),
            dma((OWN,)),
            dma((OWN,)),
            dma((OWN, 2, PEERS)),
            dma((OWN, 2, PEERS)),
            dma((3,)),
        ],
        compiler_params=pltpu.CompilerParams(
            collective_id=0, has_side_effects=True, vmem_limit_bytes=44000 * 1024
        ),
    )(
        *(
            pltpu.with_memory_space_constraint(v, pltpu.HBM)
            for v in (
                projections.reshape(routes, width),
                cot_rows,
                routed_heads.T,
                slot_index.T,
                logits,
                doc_lengths,
            )
        ),
    )
    head_outputs, projection_grads, gate_grads = pl.pallas_call(
        home_kernel,
        out_shape=(
            jax.ShapeDtypeStruct((routes, HS), BF16),
            jax.ShapeDtypeStruct((routes, 3 * HS), BF16),
            jax.ShapeDtypeStruct((top, tokens), F32),
        ),
        in_specs=[whole] * 6,
        out_specs=(hbm, hbm, whole),
        scratch_shapes=[
            vmem((routes, HS), BF16),
            vmem((routes, 3 * HS), BF16),
            dma((routes // 256, 2)),
        ],
        compiler_params=pltpu.CompilerParams(vmem_limit_bytes=16000 * 1024),
    )(*handed, cot_rows, logits)
    return (
        head_outputs.reshape(tokens, top, HS),
        projection_grads.reshape(tokens, top, width),
        gate_grads.T,
    )


def solution(mesh):
    tokens = P(("seq", "head"), None, None)
    routes = P(("seq", "head"), None)
    return jax.shard_map(
        per_device,
        mesh=mesh,
        in_specs=(tokens, routes, routes, routes, P(), tokens),
        out_specs=(tokens, tokens, routes),
        check_vma=False,
    )
```
